32 devices in a mesh: fsdp: 8 (over y, x, core), seq: 4 (over z).
Axes of the slice: x: 2, y: 2, z: 4, core: 2. Of those that a mesh axis runs over, the one named last changes fastest.
Arguments:
- hidden_in: bfloat16 [24, 448, 1024], P('fsdp', 'seq'), may hold values from -6 to 6
- encoded: bfloat16 [24, 1500, 1024], P('fsdp', 'seq'), may hold values from -6 to 6
- out_grad: bfloat16 [24, 448, 1024], P('fsdp', 'seq'), may hold values from -6 to 6
- norm_gain: bfloat16 [3, 1024], P(None, 'fsdp'), may hold values from 0.25 to 1.75
- norm_shift: bfloat16 [3, 1024], P(None, 'fsdp'), may hold values from -3 to 3
- biases: bfloat16 [7, 1024], P(None, 'fsdp'), may hold values from -3 to 3
- self_qkv: bfloat16 [1024, 3072], P('fsdp'), may hold values from -0.1875 to 0.1875
- self_out: bfloat16 [1024, 1024], P('fsdp'), may hold values from -0.5 to 0.5
- cross_q: bfloat16 [1024, 1024], P('fsdp'), may hold values from -0.1875 to 0.1875
- cross_kv: bfloat16 [1024, 2048], P('fsdp'), may hold values from -0.1875 to 0.1875
- cross_out: bfloat16 [1024, 1024], P('fsdp'), may hold values from -0.75 to 0.75
- mlp_in: bfloat16 [1024, 4096], P('fsdp'), may hold values from -0.1875 to 0.1875
- mlp_in_bias: bfloat16 [4096], P('fsdp'), may hold values from -3 to 3
- mlp_out: bfloat16 [4096, 1024], P('fsdp'), may hold values from -0.09375 to 0.09375
Outputs:
- hidden_out: bfloat16 [24, 448, 1024], P('fsdp', 'seq')
- grad_hidden_in: bfloat16 [24, 448, 1024], P('fsdp', 'seq')
- grad_encoded: bfloat16 [24, 1500, 1024], P('fsdp', 'seq')
- grad_norm_gain: float32 [3, 1024], P(None, 'fsdp')
- grad_norm_shift: float32 [3, 1024], P(None, 'fsdp')
- grad_biases: float32 [7, 1024], P(None, 'fsdp')
- grad_self_qkv: float32 [1024, 3072], P('fsdp')
- grad_self_out: float32 [1024, 1024], P('fsdp')
- grad_cross_q: float32 [1024, 1024], P('fsdp')
- grad_cross_kv: float32 [1024, 2048], P('fsdp')
- grad_cross_out: float32 [1024, 1024], P('fsdp')
- grad_mlp_in: float32 [1024, 4096], P('fsdp')
- grad_mlp_in_bias: float32 [4096], P('fsdp')
- grad_mlp_out: float32 [4096, 1024], P('fsdp')
The draws below stay inside these ranges and needn't reach their ends.
All inputs are finite; a program needn't handle non-finite values.
Results may differ from the reference program's by a relative error of at most 0.018.
Values may be sent and summed in bfloat16 or wider, within the bound.
No kernel may reach another device: no remote copies, remote signals or barrier semaphores. Data moves between devices by JAX's collectives and lax.ppermute only.
A program may use at most 256 MiB of HBM per device.

```python
import jax
import jax.numpy as jnp
from jax import lax

D = 1024
HD = 64
FF = 4096
LEN = 448
FRAMES = 1500
CLIPS = 24


def shard_levels(own_key, dims, cuts, smallest, high):
    def one(position, parts):
        heights = jax.random.uniform(jax.random.fold_in(jax.random.fold_in(own_key, 6), position), (parts,), jnp.float32, smallest / len(cuts), high / len(cuts))
        return jnp.repeat(jnp.exp(heights), dims[position] // parts).reshape((-1,) + (1,) * (len(dims) - position - 1))

    gain = one(*cuts[0])
    for cut in cuts[1:]:
        gain = gain * one(*cut)
    return gain


def normal_values(rng, extent, deviation, bound, split=(), kind=jnp.bfloat16):
    array = jax.random.normal(rng, extent, jnp.float32) * deviation
    if len(split) > 0:
        array = shard_levels(rng, extent, split, -0.22, 0.18) * array
    return jnp.clip(array, min=-bound, max=bound).astype(kind)


def setup_inputs(seed: int = 0) -> dict:
    key_of = jax.random.split(jax.random.key(seed), 15)
    return {
        "hidden_in": normal_values(key_of[0], (CLIPS, LEN, D), 1.0, 6.0, ((0, 8), (1, 4))),
        "encoded": normal_values(key_of[1], (CLIPS, FRAMES, D), 1.0, 6.0, ((0, 8), (1, 4))),
        "out_grad": normal_values(key_of[2], (CLIPS, LEN, D), 1.0, 6.0, ((0, 8), (1, 4))),
        "norm_gain": jnp.clip(1.0 + 0.15 * jax.random.normal(key_of[3], (3, D), jnp.float32), 0.25, 1.75).astype(jnp.bfloat16),
        "norm_shift": normal_values(key_of[4], (3, D), 0.5, 3.0, ((1, 8),)),
        "biases": normal_values(key_of[5], (7, D), 0.5, 3.0, ((1, 8),)),
        "self_qkv": normal_values(key_of[6], (D, 3 * D), D ** -0.5, 0.1875, ((0, 8),)),
        "self_out": normal_values(key_of[7], (D, D), (D // 8) ** -0.5, 0.5, ((0, 8),)),
        "cross_q": normal_values(key_of[8], (D, D), D ** -0.5, 0.1875, ((0, 8),)),
        "cross_kv": normal_values(key_of[9], (D, 2 * D), D ** -0.5, 0.1875, ((0, 8),)),
        "cross_out": normal_values(key_of[10], (D, D), (D // 16) ** -0.5, 0.75, ((0, 8),)),
        "mlp_in": normal_values(key_of[11], (D, FF), D ** -0.5, 0.1875, ((0, 8),)),
        "mlp_in_bias": normal_values(key_of[12], (FF,), 0.5, 3.0, ((0, 8),)),
        "mlp_out": normal_values(key_of[13], (FF, D), FF ** -0.5, 0.09375, ((0, 8),)),
    }


NORM_EPSILON = 1e-05

@jax.custom_vjp
def low(v):
    return lax.optimization_barrier(v.astype(jnp.bfloat16)).astype(jnp.float32)

@jax.custom_vjp
def low_back(v):
    return v

def low_keep(v):
    return (low(v), None)

def low_pass(kept, grad):
    return (grad,)

def back_keep(v):
    return (v, None)

def back_low(kept, grad):
    return (low(grad),)
low.defvjp(low_keep, low_pass)
low_back.defvjp(back_keep, back_low)

def matmul(first, second):
    return jnp.dot(first, second, precision=lax.Precision.HIGHEST)

def norm_apply(values, gain_row, shift_row):
    average = lax.optimization_barrier(jnp.mean(values, axis=-1, keepdims=True))
    centred = values - average
    variance = lax.optimization_barrier(jnp.mean(centred * centred, axis=-1, keepdims=True))
    return centred * lax.rsqrt(variance + NORM_EPSILON) * gain_row + shift_row

def attend(query_rows, key_rows, value_rows, causal):
    query_count = query_rows.shape[0]
    key_count = key_rows.shape[0]
    query_heads = query_rows.reshape(query_count, -1, HD)
    key_heads = key_rows.reshape(key_count, -1, HD)
    value_heads = value_rows.reshape(key_count, -1, HD)
    scores = low_back(jnp.einsum('qhd,khd->hqk', query_heads, key_heads, precision=lax.Precision.HIGHEST))
    if causal:
        allowed = jnp.arange(query_count)[:, None] >= jnp.arange(key_count)[None, :]
        scores = jnp.where(allowed[None, :, :], scores, -jnp.inf)
    soft_weights = jax.nn.softmax(scores, axis=-1)
    mixed = jnp.einsum('hqk,khd->qhd', low(soft_weights), value_heads, precision=lax.Precision.HIGHEST)
    return mixed.reshape(query_count, -1)

def layer(residual_in, encoded_rows, gains, shifts, bias_rows, w_qkv, w_self_out, w_cross_q, w_cross_kv, w_cross_out, w_inner, inner_bias, w_outer):
    width = residual_in.shape[1]
    scaling = HD ** (-0.5)
    normed_one = low(norm_apply(residual_in, gains[0], shifts[0]))
    pre_qkv = matmul(normed_one, w_qkv)
    queries = low_back(low((pre_qkv[:, :width] + bias_rows[0]) * scaling))
    key_rows = low_back(low(pre_qkv[:, width:2 * width]))
    value_rows = low_back(low(pre_qkv[:, 2 * width:] + bias_rows[1]))
    self_mix = low_back(low(attend(queries, key_rows, value_rows, True)))
    after_self = residual_in + low_back(matmul(self_mix, w_self_out)) + bias_rows[2]
    normed_two = low(norm_apply(after_self, gains[1], shifts[1]))
    cross_queries = low_back(low((matmul(normed_two, w_cross_q) + bias_rows[3]) * scaling))
    encoded_pre = matmul(encoded_rows, w_cross_kv)
    cross_keys = low_back(low(encoded_pre[:, :width]))
    cross_values = low_back(low(encoded_pre[:, width:] + bias_rows[4]))
    cross_mix = low_back(low(attend(cross_queries, cross_keys, cross_values, False)))
    after_cross = after_self + low_back(matmul(cross_mix, w_cross_out)) + bias_rows[5]
    normed_three = low(norm_apply(after_cross, gains[2], shifts[2]))
    inner = low_back(matmul(normed_three, w_inner)) + inner_bias
    activated = low(jax.nn.gelu(inner, approximate=False))
    return after_cross + low_back(matmul(activated, w_outer)) + bias_rows[6]

def reference(hidden_in, encoded, out_grad, norm_gain, norm_shift, biases, self_qkv, self_out, cross_q, cross_kv, cross_out, mlp_in, mlp_in_bias, mlp_out):
    weights = tuple((member.astype(jnp.float32) for member in (norm_gain, norm_shift, biases, self_qkv, self_out, cross_q, cross_kv, cross_out, mlp_in, mlp_in_bias, mlp_out)))

    def clip_step(totals, clip_rows):
        clip_input, clip_encoded, clip_grad = clip_rows
        result, pull_back = jax.vjp(layer, clip_input.astype(jnp.float32), clip_encoded.astype(jnp.float32), *weights)
        gradients = pull_back(clip_grad.astype(jnp.float32))
        totals = jax.tree.map(jnp.add, totals, tuple(gradients[2:]))
        return (totals, (result.astype(jnp.bfloat16), gradients[0].astype(jnp.bfloat16), gradients[1].astype(jnp.bfloat16)))
    initial = tuple((jnp.zeros(member.shape, jnp.float32) for member in weights))
    totals, per_clip = lax.scan(clip_step, initial, (hidden_in, encoded, out_grad))
    return (per_clip[0], per_clip[1], per_clip[2], totals[0], totals[1], totals[2], totals[3], totals[4], totals[5], totals[6], totals[7], totals[8], totals[9], totals[10])
```

```python
import functools

import jax
import jax.numpy as jnp
from jax import lax
from jax.experimental import pallas as pl
from jax.experimental.pallas import tpu as pltpu
from jax.sharding import PartitionSpec as P

HD = 64
LANES = 128
NORM_EPSILON = 1e-05
LOW = -1e30
F32 = jnp.float32
BF = jnp.bfloat16
AXES = ("fsdp", "seq")


def two_heads(rows):
    lane = lax.broadcasted_iota(jnp.int32, rows.shape, 1)
    zero = jnp.zeros_like(rows)
    return jnp.concatenate(
        [jnp.where(lane < HD, rows, zero), jnp.where(lane >= HD, rows, zero)], axis=0
    )


def one_row(stacked):
    count = stacked.shape[0] // 2
    lane = lax.broadcasted_iota(jnp.int32, (count, stacked.shape[1]), 1)
    return jnp.where(lane < HD, stacked[:count], stacked[count:])


def over_rows(first, second):
    return lax.dot_general(first, second, (((0,), (0,)), ((), ())), preferred_element_type=F32)


def over_lanes(first, second):
    return lax.dot_general(first, second, (((1,), (1,)), ((), ())), preferred_element_type=F32)


def fill_scores(scores_ref, keys, queries, valid, places):
    size = keys.shape[0]
    scores = over_lanes(keys, queries)
    if places is not None:
        key_place, query_place = places
        scores = jnp.where(key_place <= query_place, scores, LOW)
    scores_ref[...] = scores
    if valid < size:
        first = valid // 8 * 8
        row = lax.broadcasted_iota(jnp.int32, (size - first, queries.shape[0]), 0)
        scores_ref[first:size] = jnp.where(row < valid - first, scores_ref[first:size], LOW)


def forward_kernel(chunk, valid, causal, *refs):
    if causal:
        q_ref, k_ref, v_ref, kp_ref, qp_ref, o_ref, log_ref, s_ref = refs
    else:
        q_ref, k_ref, v_ref, o_ref, log_ref, s_ref = refs
    queries = two_heads(q_ref[...])
    count = k_ref.shape[0] // chunk
    width = queries.shape[0]

    def first(step, top):
        rows = pl.ds(pl.multiple_of(step * chunk, chunk), chunk)
        places = (kp_ref[rows], qp_ref[...]) if causal else None
        part = s_ref.at[rows]
        fill_scores(part, k_ref[rows], queries, valid, places)
        return jnp.maximum(top, jnp.max(part[...], axis=0, keepdims=True))

    top = lax.fori_loop(0, count, first, jnp.full((1, width), LOW, F32))

    def second(step, carry):
        total, mixed = carry
        rows = pl.ds(pl.multiple_of(step * chunk, chunk), chunk)
        raised = jnp.exp(s_ref[rows] - top)
        total = total + jnp.sum(raised, axis=0, keepdims=True)
        mixed = mixed + over_rows(v_ref[rows], raised.astype(BF))
        return total, mixed

    total, mixed = lax.fori_loop(
        0, count, second, (jnp.zeros((1, width), F32), jnp.zeros((LANES, width), F32))
    )
    o_ref[...] = one_row(jnp.transpose(mixed / total)).astype(BF)
    log_ref[...] = (top + jnp.log(total))[None]


def backward_kernel(chunk, valid, causal, *refs):
    if causal:
        q_ref, k_ref, v_ref, o_ref, g_ref, log_ref, kp_ref, qp_ref = refs[:8]
    else:
        q_ref, k_ref, v_ref, o_ref, g_ref, log_ref = refs[:6]
    gq_ref, gk_ref, gv_ref, s_ref = refs[-4:]
    queries = two_heads(q_ref[...])
    grads = two_heads(g_ref[...])
    mixed = o_ref[...].astype(F32)
    product = grads.astype(F32) * jnp.concatenate([mixed, mixed], axis=0)
    row_dot = jnp.sum(jnp.transpose(product), axis=0, keepdims=True)
    log_total = log_ref[0]
    count = k_ref.shape[0] // chunk
    width = queries.shape[0]

    def body(step, grad_queries):
        rows = pl.ds(pl.multiple_of(step * chunk, chunk), chunk)
        places = (kp_ref[rows], qp_ref[...]) if causal else None
        keys = k_ref[rows]
        fill_scores(s_ref, keys, queries, valid, places)
        weights = jnp.exp(s_ref[...] - log_total)
        grad_weights = over_lanes(v_ref[rows], grads)
        grad_scores = (weights * (grad_weights - row_dot)).astype(BF)
        gv_ref[rows] = jnp.dot(weights.astype(BF), grads, preferred_element_type=F32).astype(BF)
        gk_ref[rows] = jnp.dot(grad_scores, queries, preferred_element_type=F32).astype(BF)
        return grad_queries + over_rows(keys, grad_scores)

    grad_queries = lax.fori_loop(0, count, body, jnp.zeros((LANES, width), F32))
    gq_ref[...] = one_row(jnp.transpose(grad_queries)).astype(BF)


def columns(rows):
    return pl.BlockSpec((rows, LANES), lambda pair: (0, pair))


def place_specs(keys, tokens):
    return [
        pl.BlockSpec((keys, 1), lambda pair: (0, 0)),
        pl.BlockSpec((1, 2 * tokens), lambda pair: (0, 0)),
    ]


def attend(queries, keys, values, places, chunk, valid):
    tokens, width = queries.shape
    count = keys.shape[0]
    causal = places is not None
    pairs = width // LANES
    specs = [columns(tokens), columns(count), columns(count)]
    operands = [queries, keys, values]
    if causal:
        specs += place_specs(count, tokens)
        operands += list(places)
    return pl.pallas_call(
        functools.partial(forward_kernel, chunk, valid, causal),
        grid=(pairs,),
        in_specs=specs,
        out_specs=[columns(tokens), pl.BlockSpec((1, 1, 2 * tokens), lambda pair: (pair, 0, 0))],
        out_shape=[
            jax.ShapeDtypeStruct((tokens, width), BF),
            jax.ShapeDtypeStruct((pairs, 1, 2 * tokens), F32),
        ],
        scratch_shapes=[pltpu.VMEM((count, 2 * tokens), F32)],
        compiler_params=pltpu.CompilerParams(vmem_limit_bytes=32 << 20),
        cost_estimate=pl.CostEstimate(
            flops=16 * tokens * count * width,
            transcendentals=tokens * count * width // HD,
            bytes_accessed=4 * (tokens + count) * width,
        ),
        name="attend_causal" if causal else "attend_cross",
    )(*operands)


def attend_back(queries, keys, values, mixed, grads, logs, places, chunk, valid):
    tokens, width = queries.shape
    count = keys.shape[0]
    causal = places is not None
    pairs = width // LANES
    specs = [
        columns(tokens),
        columns(count),
        columns(count),
        columns(tokens),
        columns(tokens),
        pl.BlockSpec((1, 1, 2 * tokens), lambda pair: (pair, 0, 0)),
    ]
    operands = [queries, keys, values, mixed, grads, logs]
    if causal:
        specs += place_specs(count, tokens)
        operands += list(places)
    return pl.pallas_call(
        functools.partial(backward_kernel, chunk, valid, causal),
        grid=(pairs,),
        in_specs=specs,
        out_specs=[columns(tokens), columns(count), columns(count)],
        out_shape=[
            jax.ShapeDtypeStruct((tokens, width), BF),
            jax.ShapeDtypeStruct((count, width), BF),
            jax.ShapeDtypeStruct((count, width), BF),
        ],
        scratch_shapes=[pltpu.VMEM((chunk, 2 * tokens), F32)],
        compiler_params=pltpu.CompilerParams(vmem_limit_bytes=32 << 20),
        cost_estimate=pl.CostEstimate(
            flops=40 * tokens * count * width,
            transcendentals=tokens * count * width // HD,
            bytes_accessed=8 * (tokens + count) * width,
        ),
        name="attend_causal_back" if causal else "attend_cross_back",
    )(*operands)


def product(first, second):
    return jnp.dot(first, second, preferred_element_type=F32)


def product_back(incoming, weight):
    return lax.dot_general(
        incoming, weight, (((1,), (1,)), ((), ())), preferred_element_type=F32
    )


def weight_grad(operand, incoming):
    return lax.dot_general(
        operand, incoming, (((0,), (0,)), ((), ())), preferred_element_type=F32
    ).astype(BF)


def normalized(values):
    average = jnp.mean(values, axis=-1, keepdims=True)
    centred = values - average
    variance = jnp.mean(centred * centred, axis=-1, keepdims=True)
    inverse = lax.rsqrt(variance + NORM_EPSILON)
    return centred * inverse, inverse


def norm_back(incoming, values, gain_row):
    rows, inverse = normalized(values)
    scaled = incoming * gain_row
    average = jnp.mean(scaled, axis=-1, keepdims=True)
    aligned = jnp.mean(scaled * rows, axis=-1, keepdims=True)
    gain_grad = jnp.sum(incoming * rows, axis=0)
    shift_grad = jnp.sum(incoming, axis=0)
    return (scaled - average - rows * aligned) * inverse, gain_grad, shift_grad


def gelu(values):
    return values * (1.0 + lax.erf(values * (0.5**0.5))) * 0.5


def gelu_slope(values):
    return (1.0 + lax.erf(values * (0.5**0.5))) * 0.5 + values * jnp.exp(
        -0.5 * values * values
    ) * (0.5 / jnp.pi) ** 0.5


class Grid:
    def __init__(self, fsdp, seq, clips):
        self.fsdp, self.seq, self.clips = fsdp, seq, clips
        self.here = lax.axis_index("seq")
        self.first = self.first_of(lax.axis_index("fsdp"))

    def first_of(self, group):
        return (group % 2) * (self.seq - self.clips)

    def works(self, group, place):
        return 0 <= place - self.first_of(group) < self.clips

    def turn(self, values, step, to_workers):
        pairs = []
        for group in range(self.fsdp):
            for place in range(self.seq):
                target = (place + step) % self.seq
                worker = target if to_workers else place
                if self.works(group, worker):
                    pairs.append((group * self.seq + place, group * self.seq + target))
        return lax.ppermute(values, AXES, pairs)

    def clip_at(self, place):
        return jnp.clip(place - self.first, 0, self.clips - 1)

    def collect(self, values):
        own = lax.dynamic_index_in_dim(values, self.clip_at(self.here), 0, keepdims=False)
        active = (self.here >= self.first) & (self.here < self.first + self.clips)
        pieces = [jnp.where(active, own, jnp.zeros_like(own))]
        for step in range(1, self.seq):
            target = (self.here + step) % self.seq
            sent = lax.dynamic_index_in_dim(values, self.clip_at(target), 0, keepdims=False)
            pieces.append(self.turn(sent, step, True))
        return pieces

    def hand_back(self, pieces):
        arrived = [pieces[0]]
        for step in range(1, self.seq):
            arrived.append(self.turn(pieces[step], self.seq - step, False))
        stacked = jnp.stack(arrived)
        rows = []
        for clip in range(self.clips):
            step = (clip + self.first - self.here) % self.seq
            rows.append(lax.dynamic_index_in_dim(stacked, step, 0, keepdims=False))
        return jnp.stack(rows)

    def places(self, rows):
        source = (self.here - jnp.arange(self.seq)) % self.seq
        return (source[:, None] * rows + jnp.arange(rows)[None, :]).reshape(-1)

    def seq_sum(self, values):
        if self.seq != 4:
            return lax.psum(values, "seq")

        def chain(moved, links):
            pairs = [
                (group * self.seq + a, group * self.seq + b)
                for group in range(self.fsdp)
                for a, b in links
            ]
            return lax.ppermute(moved, AXES, pairs)

        half = (values.astype(F32) + chain(values, ((0, 1), (3, 2))).astype(F32)).astype(BF)
        whole = (half.astype(F32) + chain(half, ((1, 2), (2, 1))).astype(F32)).astype(BF)
        back = chain(whole, ((1, 0), (2, 3)))
        return jnp.where((self.here == 0) | (self.here == 3), back, whole)


def local(
    mesh_shape,
    hidden_in,
    encoded,
    out_grad,
    norm_gain,
    norm_shift,
    biases,
    self_qkv,
    self_out,
    cross_q,
    cross_kv,
    cross_out,
    mlp_in,
    mlp_in_bias,
    mlp_out,
):
    clips, rows, width = hidden_in.shape
    frames = encoded.shape[1]
    padded = (frames + 15) // 16 * 16
    grid = Grid(mesh_shape["fsdp"], mesh_shape["seq"], clips)
    shard = norm_gain.shape[1]
    norms = norm_gain.shape[0]
    bias_count = biases.shape[0]
    scaling = HD ** (-0.5)

    def gathered(member):
        return lax.all_gather(member, "fsdp", axis=0, tiled=True)

    def reduced(member):
        part = lax.psum_scatter(member, "fsdp", scatter_dimension=0, tiled=True)
        return grid.seq_sum(part).astype(F32)

    residual_in = jnp.concatenate(grid.collect(hidden_in), axis=0).astype(F32)
    small = jnp.concatenate([norm_gain, norm_shift, biases, mlp_in_bias.reshape(-1, shard)], axis=0)
    small = lax.all_gather(small, "fsdp", axis=0)
    vectors = small[:, : 2 * norms + bias_count].swapaxes(0, 1).reshape(-1, width).astype(F32)
    gain, shift, bias = vectors[:norms], vectors[norms : 2 * norms], vectors[2 * norms :]
    inner_bias = small[:, 2 * norms + bias_count :].reshape(1, -1).astype(F32)

    full_qkv = gathered(self_qkv)
    frame_pieces = [
        jnp.pad(piece, ((0, padded - frames), (0, 0)))
        for piece in grid.collect(encoded)
    ]
    frame_rows = jnp.concatenate(frame_pieces, axis=0)
    top = jnp.concatenate(grid.collect(out_grad), axis=0)
    full_self_out = gathered(self_out)
    full_cross_kv = gathered(cross_kv)
    full_cross_q = gathered(cross_q)
    full_cross_out = gathered(cross_out)
    full_inner = gathered(mlp_in)
    full_outer = gathered(mlp_out)

    place = grid.places(rows)
    places = (place[:, None], jnp.concatenate([place, place])[None, :])
    tokens = place.shape[0]

    normed_one = (normalized(residual_in)[0] * gain[0] + shift[0]).astype(BF)
    pre_qkv = product(normed_one, full_qkv)
    queries = ((pre_qkv[:, :width] + bias[0]) * scaling).astype(BF)
    keys = pre_qkv[:, width : 2 * width].astype(BF)
    values = (pre_qkv[:, 2 * width :] + bias[1]).astype(BF)
    self_mix, self_log = attend(queries, keys, values, places, tokens, tokens)
    after_self = residual_in + product(self_mix, full_self_out) + bias[2]
    normed_two = (normalized(after_self)[0] * gain[1] + shift[1]).astype(BF)
    cross_queries = ((product(normed_two, full_cross_q) + bias[3]) * scaling).astype(BF)
    cross_pre = product(frame_rows, full_cross_kv)
    cross_keys = cross_pre[:, :width].astype(BF)
    cross_values = (cross_pre[:, width:] + bias[4]).astype(BF)
    cross_mix, cross_log = attend(cross_queries, cross_keys, cross_values, None, padded, frames)
    after_cross = after_self + product(cross_mix, full_cross_out) + bias[5]
    normed_three = (normalized(after_cross)[0] * gain[2] + shift[2]).astype(BF)
    inner = product(normed_three, full_inner) + inner_bias
    activated = gelu(inner).astype(BF)
    hidden_rows = (after_cross + product(activated, full_outer) + bias[6]).astype(BF)

    top_wide = top.astype(F32)
    grad_w_outer = weight_grad(activated, top)
    grad_bias_six = jnp.sum(top_wide, axis=0)
    grad_inner = product_back(top, full_outer) * gelu_slope(inner)
    grad_inner_low = grad_inner.astype(BF)
    grad_w_inner = weight_grad(normed_three, grad_inner_low)
    grad_inner_bias = jnp.sum(grad_inner, axis=0)
    grad_normed_three = product_back(grad_inner_low, full_inner)
    from_three, gain_three, shift_three = norm_back(grad_normed_three, after_cross, gain[2])
    grad_after_cross = top_wide + from_three
    grad_cross_low = grad_after_cross.astype(BF)
    grad_w_cross_out = weight_grad(cross_mix, grad_cross_low)
    grad_bias_five = jnp.sum(grad_after_cross, axis=0)
    grad_cross_mix = product_back(grad_cross_low, full_cross_out).astype(BF)
    grad_cross_queries, grad_cross_keys, grad_cross_values = attend_back(
        cross_queries,
        cross_keys,
        cross_values,
        cross_mix,
        grad_cross_mix,
        cross_log,
        None,
        padded,
        frames,
    )
    scaled_cross = grad_cross_queries * scaling
    grad_w_cross_q = weight_grad(normed_two, scaled_cross)
    grad_bias_three = jnp.sum(scaled_cross.astype(F32), axis=0)
    grad_normed_two = product_back(scaled_cross, full_cross_q)
    grad_pair = jnp.concatenate([grad_cross_keys, grad_cross_values], axis=1)
    grad_w_cross_kv = weight_grad(frame_rows, grad_pair)
    grad_bias_four = jnp.sum(grad_cross_values.astype(F32), axis=0)
    grad_frames = product_back(grad_pair, full_cross_kv).astype(BF)
    from_two, gain_two, shift_two = norm_back(grad_normed_two, after_self, gain[1])
    grad_after_self = grad_after_cross + from_two
    grad_self_low = grad_after_self.astype(BF)
    grad_w_self_out = weight_grad(self_mix, grad_self_low)
    grad_bias_two = jnp.sum(grad_after_self, axis=0)
    grad_self_mix = product_back(grad_self_low, full_self_out).astype(BF)
    grad_queries, grad_keys, grad_values = attend_back(
        queries, keys, values, self_mix, grad_self_mix, self_log, places, tokens, tokens
    )
    scaled_query = grad_queries * scaling
    grad_pre = jnp.concatenate([scaled_query, grad_keys, grad_values], axis=1)
    grad_w_qkv = weight_grad(normed_one, grad_pre)
    grad_bias_zero = jnp.sum(scaled_query.astype(F32), axis=0)
    grad_bias_one = jnp.sum(grad_values.astype(F32), axis=0)
    grad_normed_one = product_back(grad_pre, full_qkv)
    from_one, gain_one, shift_one = norm_back(grad_normed_one, residual_in, gain[0])
    grad_rows = (grad_after_self + from_one).astype(BF)

    total_outer = reduced(grad_w_outer)
    total_inner = reduced(grad_w_inner)
    total_cross_out = reduced(grad_w_cross_out)
    total_cross_q = reduced(grad_w_cross_q)
    total_cross_kv = reduced(grad_w_cross_kv)
    total_self_out = reduced(grad_w_self_out)
    total_qkv = reduced(grad_w_qkv)

    def token_pieces(member):
        return [member[rows * step : rows * (step + 1)] for step in range(grid.seq)]

    hidden_out = grid.hand_back(token_pieces(hidden_rows))
    grad_encoded = grid.hand_back(
        [grad_frames[padded * step : padded * step + frames] for step in range(grid.seq)]
    )
    grad_hidden_in = grid.hand_back(token_pieces(grad_rows))

    sums = jnp.stack(
        [
            gain_one,
            gain_two,
            gain_three,
            shift_one,
            shift_two,
            shift_three,
            grad_bias_zero,
            grad_bias_one,
            grad_bias_two,
            grad_bias_three,
            grad_bias_four,
            grad_bias_five,
            grad_bias_six,
        ]
    )
    inner_sums = grad_inner_bias.reshape(grid.fsdp, -1, shard)
    packed = jnp.concatenate(
        [sums.reshape(-1, grid.fsdp, shard).swapaxes(0, 1), inner_sums], axis=1
    )
    packed = lax.psum(packed, AXES)
    mine = lax.dynamic_index_in_dim(packed, lax.axis_index("fsdp"), 0, keepdims=False)
    return (
        hidden_out,
        grad_hidden_in,
        grad_encoded,
        mine[:norms],
        mine[norms : 2 * norms],
        mine[2 * norms : 2 * norms + bias_count],
        total_qkv,
        total_self_out,
        total_cross_q,
        total_cross_kv,
        total_cross_out,
        total_inner,
        mine[2 * norms + bias_count :].reshape(-1),
        total_outer,
    )


def solution(mesh):
    rows = P("fsdp", "seq", None)
    wide = P(None, "fsdp")
    tall = P("fsdp", None)
    in_specs = (rows,) * 3 + (wide,) * 3 + (tall,) * 6 + (P("fsdp"), tall)
    out_specs = (rows,) * 3 + (wide,) * 3 + (tall,) * 6 + (P("fsdp"), tall)
    return jax.shard_map(
        functools.partial(local, dict(mesh.shape)),
        mesh=mesh,
        in_specs=in_specs,
        out_specs=out_specs,
        check_vma=False,
    )
```

```python
import functools

import jax
import jax.numpy as jnp
import numpy as np
from jax import lax
from jax.experimental import pallas as pl
from jax.experimental.pallas import tpu as pltpu
from jax.sharding import PartitionSpec as P

HD = 64
LANES = 128
NORM_EPSILON = 1e-05
LOW = -1e30
F32 = jnp.float32
BF = jnp.bfloat16
AXES = ("fsdp", "seq")


def two_heads(rows):
    lane = lax.broadcasted_iota(jnp.int32, rows.shape, 1)
    zero = jnp.zeros_like(rows)
    return jnp.concatenate(
        [jnp.where(lane < HD, rows, zero), jnp.where(lane >= HD, rows, zero)], axis=0
    )


def one_row(stacked):
    count = stacked.shape[0] // 2
    lane = lax.broadcasted_iota(jnp.int32, (count, stacked.shape[1]), 1)
    return jnp.where(lane < HD, stacked[:count], stacked[count:])


def over_rows(first, second):
    return lax.dot_general(first, second, (((0,), (0,)), ((), ())), preferred_element_type=F32)


def over_lanes(first, second):
    return lax.dot_general(first, second, (((1,), (1,)), ((), ())), preferred_element_type=F32)


def fill_scores(scores_ref, keys, queries, valid, places):
    size = keys.shape[0]
    scores = over_lanes(keys, queries)
    if places is not None:
        key_place, query_place = places
        scores = jnp.where(key_place <= query_place, scores, LOW)
    scores_ref[...] = scores
    if valid < size:
        first = valid // 8 * 8
        row = lax.broadcasted_iota(jnp.int32, (size - first, queries.shape[0]), 0)
        scores_ref[first:size] = jnp.where(row < valid - first, scores_ref[first:size], LOW)


def forward_kernel(chunk, valid, causal, *refs):
    if causal:
        q_ref, k_ref, v_ref, kp_ref, qp_ref, o_ref, log_ref, s_ref = refs
    else:
        q_ref, k_ref, v_ref, o_ref, log_ref, s_ref = refs
    queries = two_heads(q_ref[...])
    count = k_ref.shape[0] // chunk
    width = queries.shape[0]

    def first(step, top):
        rows = pl.ds(pl.multiple_of(step * chunk, chunk), chunk)
        places = (kp_ref[rows], qp_ref[...]) if causal else None
        part = s_ref.at[rows]
        fill_scores(part, k_ref[rows], queries, valid, places)
        return jnp.maximum(top, jnp.max(part[...], axis=0, keepdims=True))

    top = lax.fori_loop(0, count, first, jnp.full((1, width), LOW, F32))

    def second(step, carry):
        total, mixed = carry
        rows = pl.ds(pl.multiple_of(step * chunk, chunk), chunk)
        raised = jnp.exp(s_ref[rows] - top)
        total = total + jnp.sum(raised, axis=0, keepdims=True)
        mixed = mixed + over_rows(v_ref[rows], raised.astype(BF))
        return total, mixed

    total, mixed = lax.fori_loop(
        0, count, second, (jnp.zeros((1, width), F32), jnp.zeros((LANES, width), F32))
    )
    o_ref[...] = one_row(jnp.transpose(mixed / total)).astype(BF)
    log_ref[...] = (top + jnp.log(total))[None]


def backward_kernel(chunk, valid, causal, *refs):
    if causal:
        q_ref, k_ref, v_ref, o_ref, g_ref, log_ref, kp_ref, qp_ref = refs[:8]
    else:
        q_ref, k_ref, v_ref, o_ref, g_ref, log_ref = refs[:6]
    gq_ref, gk_ref, gv_ref, s_ref = refs[-4:]
    queries = two_heads(q_ref[...])
    grads = two_heads(g_ref[...])
    mixed = o_ref[...].astype(F32)
    product = grads.astype(F32) * jnp.concatenate([mixed, mixed], axis=0)
    row_dot = jnp.sum(jnp.transpose(product), axis=0, keepdims=True)
    log_total = log_ref[0]
    count = k_ref.shape[0] // chunk
    width = queries.shape[0]

    def body(step, grad_queries):
        rows = pl.ds(pl.multiple_of(step * chunk, chunk), chunk)
        places = (kp_ref[rows], qp_ref[...]) if causal else None
        keys = k_ref[rows]
        fill_scores(s_ref, keys, queries, valid, places)
        weights = jnp.exp(s_ref[...] - log_total)
        grad_weights = over_lanes(v_ref[rows], grads)
        grad_scores = (weights * (grad_weights - row_dot)).astype(BF)
        gv_ref[rows] = jnp.dot(weights.astype(BF), grads, preferred_element_type=F32).astype(BF)
        gk_ref[rows] = jnp.dot(grad_scores, queries, preferred_element_type=F32).astype(BF)
        return grad_queries + over_rows(keys, grad_scores)

    grad_queries = lax.fori_loop(0, count, body, jnp.zeros((LANES, width), F32))
    gq_ref[...] = one_row(jnp.transpose(grad_queries)).astype(BF)


def columns(rows):
    return pl.BlockSpec((rows, LANES), lambda pair: (0, pair))


def place_specs(keys, tokens):
    return [
        pl.BlockSpec((keys, 1), lambda pair: (0, 0)),
        pl.BlockSpec((1, 2 * tokens), lambda pair: (0, 0)),
    ]


def attend(queries, keys, values, places, chunk, valid):
    tokens, width = queries.shape
    count = keys.shape[0]
    causal = places is not None
    pairs = width // LANES
    specs = [columns(tokens), columns(count), columns(count)]
    operands = [queries, keys, values]
    if causal:
        specs += place_specs(count, tokens)
        operands += list(places)
    return pl.pallas_call(
        functools.partial(forward_kernel, chunk, valid, causal),
        grid=(pairs,),
        in_specs=specs,
        out_specs=[columns(tokens), pl.BlockSpec((1, 1, 2 * tokens), lambda pair: (pair, 0, 0))],
        out_shape=[
            jax.ShapeDtypeStruct((tokens, width), BF),
            jax.ShapeDtypeStruct((pairs, 1, 2 * tokens), F32),
        ],
        scratch_shapes=[pltpu.VMEM((count, 2 * tokens), F32)],
        compiler_params=pltpu.CompilerParams(vmem_limit_bytes=32 << 20),
        cost_estimate=pl.CostEstimate(
            flops=16 * tokens * count * width,
            transcendentals=tokens * count * width // HD,
            bytes_accessed=4 * (tokens + count) * width,
        ),
        name="attend_causal" if causal else "attend_cross",
    )(*operands)


def attend_back(
    queries, keys, values, mixed, grads, logs, places, chunk, valid, part=0, parts=1
):
    tokens, width = queries.shape
    count = keys.shape[0]
    causal = places is not None
    pairs = width // LANES // parts
    first = part * pairs

    def shifted(rows):
        return pl.BlockSpec((rows, LANES), lambda pair: (0, pair + first))

    specs = [
        shifted(tokens),
        shifted(count),
        shifted(count),
        shifted(tokens),
        shifted(tokens),
        pl.BlockSpec((1, 1, 2 * tokens), lambda pair: (pair + first, 0, 0)),
    ]
    operands = [queries, keys, values, mixed, grads, logs]
    if causal:
        specs += place_specs(count, tokens)
        operands += list(places)
    return pl.pallas_call(
        functools.partial(backward_kernel, chunk, valid, causal),
        grid=(pairs,),
        in_specs=specs,
        out_specs=[columns(tokens), columns(count), columns(count)],
        out_shape=[
            jax.ShapeDtypeStruct((tokens, width // parts), BF),
            jax.ShapeDtypeStruct((count, width // parts), BF),
            jax.ShapeDtypeStruct((count, width // parts), BF),
        ],
        scratch_shapes=[pltpu.VMEM((chunk, 2 * tokens), F32)],
        compiler_params=pltpu.CompilerParams(vmem_limit_bytes=32 << 20),
        cost_estimate=pl.CostEstimate(
            flops=40 * tokens * count * width // parts,
            transcendentals=tokens * count * width // HD // parts,
            bytes_accessed=8 * (tokens + count) * width // parts,
        ),
        name="attend_causal_back" if causal else "attend_cross_back",
    )(*operands)


def product(first, second):
    return jnp.dot(first, second, preferred_element_type=F32)


def product_back(incoming, weight):
    return lax.dot_general(
        incoming, weight, (((1,), (1,)), ((), ())), preferred_element_type=F32
    )


def weight_grad(operand, incoming):
    return lax.dot_general(
        operand, incoming, (((0,), (0,)), ((), ())), preferred_element_type=F32
    ).astype(BF)


def normalized(values):
    average = jnp.mean(values, axis=-1, keepdims=True)
    centred = values - average
    variance = jnp.mean(centred * centred, axis=-1, keepdims=True)
    inverse = lax.rsqrt(variance + NORM_EPSILON)
    return centred * inverse, inverse


def norm_back(incoming, values, gain_row):
    rows, inverse = normalized(values)
    scaled = incoming * gain_row
    average = jnp.mean(scaled, axis=-1, keepdims=True)
    aligned = jnp.mean(scaled * rows, axis=-1, keepdims=True)
    gain_grad = jnp.sum(incoming * rows, axis=0)
    shift_grad = jnp.sum(incoming, axis=0)
    return (scaled - average - rows * aligned) * inverse, gain_grad, shift_grad


def gelu(values):
    return values * (1.0 + lax.erf(values * (0.5**0.5))) * 0.5


def gelu_slope(values):
    return (1.0 + lax.erf(values * (0.5**0.5))) * 0.5 + values * jnp.exp(
        -0.5 * values * values
    ) * (0.5 / jnp.pi) ** 0.5


class Grid:
    def __init__(self, fsdp, seq, clips):
        self.fsdp, self.seq, self.clips = fsdp, seq, clips
        self.here = lax.axis_index("seq")
        self.group = lax.axis_index("fsdp")
        self.first = self.first_of(self.group)

    def first_of(self, group):
        return (group % 2) * (self.seq - self.clips)

    def works(self, group, place):
        return 0 <= place - self.first_of(group) < self.clips

    def turn(self, values, step, to_workers):
        pairs = []
        for group in range(self.fsdp):
            for place in range(self.seq):
                target = (place + step) % self.seq
                worker = target if to_workers else place
                if self.works(group, worker):
                    pairs.append((group * self.seq + place, group * self.seq + target))
        return lax.ppermute(values, AXES, pairs)

    def clip_at(self, place):
        return jnp.clip(place - self.first, 0, self.clips - 1)

    def collect(self, values):
        own = lax.dynamic_index_in_dim(values, self.clip_at(self.here), 0, keepdims=False)
        active = (self.here >= self.first) & (self.here < self.first + self.clips)
        pieces = [jnp.where(active, own, jnp.zeros_like(own))]
        for step in range(1, self.seq):
            target = (self.here + step) % self.seq
            sent = lax.dynamic_index_in_dim(values, self.clip_at(target), 0, keepdims=False)
            pieces.append(self.turn(sent, step, True))
        return pieces

    def hand_back(self, pieces):
        arrived = [pieces[0]]
        for step in range(1, self.seq):
            arrived.append(self.turn(pieces[step], self.seq - step, False))
        stacked = jnp.stack(arrived)
        rows = []
        for clip in range(self.clips):
            step = (clip + self.first - self.here) % self.seq
            rows.append(lax.dynamic_index_in_dim(stacked, step, 0, keepdims=False))
        return jnp.stack(rows)

    def places(self, rows):
        source = (self.here - jnp.arange(self.seq)) % self.seq
        return (source[:, None] * rows + jnp.arange(rows)[None, :]).reshape(-1)

    def chain(self, values, links):
        pairs = [
            (group * self.seq + a, group * self.seq + b)
            for group in range(self.fsdp)
            for a, b in links
        ]
        return lax.ppermute(values, AXES, pairs)

    def seq_sum(self, values):
        if self.seq != 4:
            return lax.psum(values, "seq")
        half = plus(values, self.chain(values, ((0, 1), (3, 2))))
        whole = plus(half, self.chain(half, ((1, 2), (2, 1))))
        back = self.chain(whole, ((1, 0), (2, 3)))
        return jnp.where((self.here == 0) | (self.here == 3), back, whole)

    def flip(self, values, bits):
        return lax.ppermute(values, "fsdp", [(f, f ^ bits) for f in range(self.fsdp)])

    def spread_far(self, shard, by_x, by_y):
        half = shard.shape[0] // 2
        return self.flip(by_y[:half], 2), self.flip(by_x[half:], 4)

    def spread_core(self, shard, by_x, by_y, far_x, far_y):
        mine = jnp.stack([shard, by_x, by_y, jnp.concatenate([far_x, far_y], axis=0)])
        return mine, self.flip(mine, 1)

    def fold_parts(self, members):
        parts = [m.reshape(4, 2, m.shape[0] // 8, m.shape[1]) for m in members]
        core = self.group % 2
        sent = jnp.concatenate([pick(p, 1 - core, 1) for p in parts], axis=2)
        kept = jnp.concatenate([pick(p, core, 1) for p in parts], axis=2)
        return kept, self.flip(sent, 1)

    def fold_far(self, kept, arrived):
        sums = plus(kept, arrived)
        half = sums.shape[1] // 2
        far = pick(sums, (self.group // 2) ^ 3, 0)
        return sums, self.flip(far[:half], 2), self.flip(far[half:], 4)

    def fold_near(self, sums, from_x, from_y):
        chip, half = self.group // 2, sums.shape[1] // 2
        to_x, to_y = pick(sums, chip ^ 1, 0), pick(sums, chip ^ 2, 0)
        to_x = jnp.concatenate([to_x[:half], plus(to_x[half:], from_y)], axis=0)
        to_y = jnp.concatenate([plus(to_y[:half], from_x), to_y[half:]], axis=0)
        return pick(sums, chip, 0), self.flip(to_x, 2), self.flip(to_y, 4)

    def hop_one(self, values):
        return values, self.chain(values, ((0, 1), (3, 2)))

    def hop_two(self, values, arrived):
        half = plus(values, arrived)
        return half, self.chain(half, ((1, 2), (2, 1)))

    def hop_three(self, half, arrived):
        whole = plus(half, arrived)
        return whole, self.chain(whole, ((1, 0), (2, 3)))

    def hop_end(self, whole, back):
        return jnp.where((self.here == 0) | (self.here == 3), back, whole).astype(F32)


def plus3(first, second, third):
    return (first.astype(F32) + second.astype(F32) + third.astype(F32)).astype(BF)


def pick(values, index, axis):
    return lax.dynamic_index_in_dim(values, index, axis, keepdims=False)


def plus(first, second):
    return (first.astype(F32) + second.astype(F32)).astype(BF)


def tied(*members):
    return lax.optimization_barrier(members)


def assemble_kernel(widths, group_ref, mine_ref, other_ref, *outs):
    slot = pl.program_id(0) * 2 + pl.program_id(1)

    def store(source_ref):
        start = 0
        for out, width in zip(outs, widths):
            out[...] = source_ref[0, :, start : start + width]
            start += width

    pl.when(slot % 2 == 0)(lambda: store(mine_ref))
    pl.when(slot % 2 == 1)(lambda: store(other_ref))


def assemble(group, mine, other, widths):
    rows, total = mine.shape[1], mine.shape[2]
    cut = 2
    step_rows = rows // cut
    source = pl.BlockSpec((1, step_rows, total), lambda chip, core, part, group: (chip, part, 0))
    return pl.pallas_call(
        functools.partial(assemble_kernel, widths),
        grid_spec=pltpu.PrefetchScalarGridSpec(
            num_scalar_prefetch=1,
            grid=(4, 2, cut),
            in_specs=[source, source],
            out_specs=[
                pl.BlockSpec(
                    (step_rows, width),
                    lambda chip, core, part, group: (
                        (group[0] ^ (2 * chip + core)) * cut + part,
                        0,
                    ),
                )
                for width in widths
            ],
        ),
        out_shape=[jax.ShapeDtypeStruct((8 * rows, width), BF) for width in widths],
        cost_estimate=pl.CostEstimate(
            flops=0, transcendentals=0, bytes_accessed=32 * rows * total
        ),
        name="assemble",
    )(group.reshape(1), mine, other)


def local(
    mesh_shape,
    hidden_in,
    encoded,
    out_grad,
    norm_gain,
    norm_shift,
    biases,
    self_qkv,
    self_out,
    cross_q,
    cross_kv,
    cross_out,
    mlp_in,
    mlp_in_bias,
    mlp_out,
):
    clips, rows, width = hidden_in.shape
    frames = encoded.shape[1]
    padded = (frames + 15) // 16 * 16
    grid = Grid(mesh_shape["fsdp"], mesh_shape["seq"], clips)
    shard = norm_gain.shape[1]
    norms = norm_gain.shape[0]
    bias_count = biases.shape[0]
    scaling = HD ** (-0.5)
    swift = grid.fsdp == 8 and grid.seq == 4

    def gathered(*members):
        widths = [member.shape[1] for member in members]
        joined = jnp.concatenate(members, axis=1)
        joined = lax.all_gather(joined, "fsdp", axis=0, tiled=True)
        return jnp.split(joined, np.cumsum(widths)[:-1].tolist(), axis=1)

    def scattered(member):
        return lax.psum_scatter(member, "fsdp", scatter_dimension=0, tiled=True)

    token_pieces = grid.collect(hidden_in)
    small = jnp.concatenate([norm_gain, norm_shift, biases, mlp_in_bias.reshape(-1, shard)], axis=0)
    small = lax.all_gather(small, "fsdp", axis=0)
    vectors = small[:, : 2 * norms + bias_count].swapaxes(0, 1).reshape(-1, width).astype(F32)
    gain, shift, bias = vectors[:norms], vectors[norms : 2 * norms], vectors[2 * norms :]
    inner_bias = small[:, 2 * norms + bias_count :].reshape(1, -1).astype(F32)

    full_qkv, full_self_out = gathered(self_qkv, self_out)
    cross_widths = (cross_kv.shape[1], cross_q.shape[1], cross_out.shape[1])
    cross_shard = jnp.concatenate([cross_kv, cross_q, cross_out], axis=1)
    if swift:
        cross_x, cross_y = grid.flip(cross_shard, 2), grid.flip(cross_shard, 4)
    residual_in = jnp.concatenate(token_pieces, axis=0).astype(F32)
    normed_one = (normalized(residual_in)[0] * gain[0] + shift[0]).astype(BF)
    late_in = jnp.concatenate([encoded, out_grad], axis=1)
    late_in, normed_one = tied(late_in, normed_one)
    late = grid.collect(late_in)
    full_inner = gathered(mlp_in)[0]

    if swift:
        normed_one, cross_x, cross_y = tied(normed_one, cross_x, cross_y)
        cross_far = grid.spread_far(cross_shard, cross_x, cross_y)
    else:
        full_cross_kv, full_cross_q, full_cross_out = gathered(cross_kv, cross_q, cross_out)
        full_outer = gathered(mlp_out)[0]

    place = grid.places(rows)
    places = (place[:, None], jnp.concatenate([place, place])[None, :])
    tokens = place.shape[0]

    pre_qkv = product(normed_one, full_qkv)
    queries = ((pre_qkv[:, :width] + bias[0]) * scaling).astype(BF)
    keys = pre_qkv[:, width : 2 * width].astype(BF)
    values = (pre_qkv[:, 2 * width :] + bias[1]).astype(BF)
    self_mix, self_log = attend(queries, keys, values, places, tokens, tokens)
    if swift:
        self_mix, far_x, far_y = tied(self_mix, *cross_far)
        cross_mine, cross_other = grid.spread_core(cross_shard, cross_x, cross_y, far_x, far_y)
    after_self = residual_in + product(self_mix, full_self_out) + bias[2]
    normed_two = (normalized(after_self)[0] * gain[1] + shift[1]).astype(BF)
    if swift:
        cross_other, mlp_out = tied(cross_other, mlp_out)
        outer_x, outer_y = grid.flip(mlp_out, 2), grid.flip(mlp_out, 4)
        full_cross_kv, full_cross_q, full_cross_out = assemble(
            grid.group, cross_mine, cross_other, cross_widths
        )
    cross_queries = ((product(normed_two, full_cross_q) + bias[3]) * scaling).astype(BF)
    frame_rows = jnp.concatenate(
        [jnp.pad(piece[:frames], ((0, padded - frames), (0, 0))) for piece in late], axis=0
    )
    top = jnp.concatenate([piece[frames:] for piece in late], axis=0)
    cross_pre = product(frame_rows, full_cross_kv)
    cross_keys = cross_pre[:, :width].astype(BF)
    cross_values = (cross_pre[:, width:] + bias[4]).astype(BF)
    if swift:
        cross_queries, outer_x, outer_y = tied(cross_queries, outer_x, outer_y)
        outer_far = grid.spread_far(mlp_out, outer_x, outer_y)
    cross_mix, cross_log = attend(cross_queries, cross_keys, cross_values, None, padded, frames)
    if swift:
        cross_mix, far_x, far_y = tied(cross_mix, *outer_far)
        outer_mine, outer_other = grid.spread_core(mlp_out, outer_x, outer_y, far_x, far_y)
    after_cross = after_self + product(cross_mix, full_cross_out) + bias[5]
    normed_three = (normalized(after_cross)[0] * gain[2] + shift[2]).astype(BF)
    inner = product(normed_three, full_inner) + inner_bias
    activated = gelu(inner).astype(BF)

    top_wide = top.astype(F32)
    grad_w_outer = weight_grad(activated, top)
    grad_w_outer, top = tied(grad_w_outer, top)
    part_outer = scattered(grad_w_outer)
    grad_bias_six = jnp.sum(top_wide, axis=0)
    if swift:
        (full_outer,) = assemble(grid.group, outer_mine, outer_other, (mlp_out.shape[1],))
    grad_inner = product_back(top, full_outer) * gelu_slope(inner)
    grad_inner_low = grad_inner.astype(BF)
    grad_w_inner = weight_grad(normed_three, grad_inner_low)
    grad_w_inner, grad_inner_low = tied(grad_w_inner, grad_inner_low)
    grad_inner_bias = jnp.sum(grad_inner, axis=0)
    if swift:
        inner_kept, inner_core = grid.fold_parts([grad_w_inner])
    else:
        part_inner = scattered(grad_w_inner)
    grad_normed_three = product_back(grad_inner_low, full_inner)
    from_three, gain_three, shift_three = norm_back(grad_normed_three, after_cross, gain[2])
    grad_after_cross = top_wide + from_three
    grad_cross_low = grad_after_cross.astype(BF)
    grad_bias_five = jnp.sum(grad_after_cross, axis=0)
    if swift:
        grad_cross_low, inner_core = tied(grad_cross_low, inner_core)
        inner_sums, inner_x, inner_y = grid.fold_far(inner_kept, inner_core)
    grad_w_cross_out = weight_grad(cross_mix, grad_cross_low)
    grad_cross_mix = product_back(grad_cross_low, full_cross_out).astype(BF)

    def cross_back(half, count, grads):
        return attend_back(
            cross_queries,
            cross_keys,
            cross_values,
            cross_mix,
            grads,
            cross_log,
            None,
            padded,
            frames,
            half,
            count,
        )

    first_half = cross_back(0, 2, grad_cross_mix)
    if swift:
        grad_cross_mix, inner_x, inner_y, *first_half = tied(
            grad_cross_mix, inner_x, inner_y, *first_half
        )
        inner_own, inner_near_x, inner_near_y = grid.fold_near(inner_sums, inner_x, inner_y)
    second_half = cross_back(1, 2, grad_cross_mix)
    if swift:
        part_outer, *second_half = tied(part_outer, *second_half)
        outer_sum, outer_in = grid.hop_one(part_outer)
    grad_cross_queries = jnp.concatenate([first_half[0], second_half[0]], axis=1)
    grad_pair = jnp.concatenate(
        [first_half[1], second_half[1], first_half[2], second_half[2]], axis=1
    )
    grad_cross_values = grad_pair[:, width:]
    grad_w_cross_kv = weight_grad(frame_rows, grad_pair)
    scaled_cross = grad_cross_queries * scaling
    scaled_cross, grad_w_cross_kv = tied(scaled_cross, grad_w_cross_kv)
    part_kv = scattered(grad_w_cross_kv)
    grad_bias_four = jnp.sum(grad_cross_values.astype(F32), axis=0)
    grad_w_cross_q = weight_grad(normed_two, scaled_cross)
    grad_bias_three = jnp.sum(scaled_cross.astype(F32), axis=0)
    grad_normed_two = product_back(scaled_cross, full_cross_q)
    from_two, gain_two, shift_two = norm_back(grad_normed_two, after_self, gain[1])
    grad_after_self = grad_after_cross + from_two
    grad_self_low = grad_after_self.astype(BF)
    grad_w_self_out = weight_grad(self_mix, grad_self_low)
    grad_bias_two = jnp.sum(grad_after_self, axis=0)
    grad_self_mix = product_back(grad_self_low, full_self_out).astype(BF)
    middle = [grad_w_cross_out, grad_w_cross_q, grad_w_self_out]
    if swift:
        grad_self_mix, inner_near_x, inner_near_y, outer_in, *middle = tied(
            grad_self_mix, inner_near_x, inner_near_y, outer_in, *middle
        )
        part_inner = plus3(inner_own, inner_near_x, inner_near_y)
        inner_sum, inner_in = grid.hop_one(part_inner)
        outer_sum, outer_in = grid.hop_two(outer_sum, outer_in)
        middle_kept, middle_core = grid.fold_parts(middle)
    grad_queries, grad_keys, grad_values = attend_back(
        queries, keys, values, self_mix, grad_self_mix, self_log, places, tokens, tokens
    )
    if swift:
        grad_queries, middle_core = tied(grad_queries, middle_core)
        middle_sums, middle_x, middle_y = grid.fold_far(middle_kept, middle_core)
    scaled_query = grad_queries * scaling
    grad_pre = jnp.concatenate([scaled_query, grad_keys, grad_values], axis=1)
    grad_normed_one = product_back(grad_pre, full_qkv)
    grad_w_qkv = weight_grad(normed_one, grad_pre)
    grad_bias_zero = jnp.sum(scaled_query.astype(F32), axis=0)
    grad_bias_one = jnp.sum(grad_values.astype(F32), axis=0)
    from_one, gain_one, shift_one = norm_back(grad_normed_one, residual_in, gain[0])
    grad_rows = (grad_after_self + from_one).astype(BF)

    sums = jnp.stack(
        [
            gain_one,
            gain_two,
            gain_three,
            shift_one,
            shift_two,
            shift_three,
            grad_bias_zero,
            grad_bias_one,
            grad_bias_two,
            grad_bias_three,
            grad_bias_four,
            grad_bias_five,
            grad_bias_six,
        ]
    )
    inner_sums_row = grad_inner_bias.reshape(grid.fsdp, -1, shard)
    packed = jnp.concatenate(
        [sums.reshape(-1, grid.fsdp, shard).swapaxes(0, 1), inner_sums_row], axis=1
    )
    kinds = packed.shape[1]
    packed = packed.reshape(grid.fsdp, -1).astype(BF)
    span = grad_w_qkv.shape[1]
    lines = -(-packed.shape[1] // span)
    filled = -(-lines // 16) * 16
    packed = jnp.pad(packed, ((0, 0), (0, filled * span - packed.shape[1])))
    packed = packed.reshape(grid.fsdp, filled, span)
    shard_rows = grad_w_qkv.shape[0] // grid.fsdp
    joined = jnp.concatenate([grad_w_qkv.reshape(grid.fsdp, shard_rows, span), packed], axis=1)
    joined = joined.reshape(-1, span)
    if swift:
        joined, inner_in, outer_in, middle_x, middle_y = tied(
            joined, inner_in, outer_in, middle_x, middle_y
        )
        inner_sum, inner_in = grid.hop_two(inner_sum, inner_in)
        outer_sum, outer_in = grid.hop_three(outer_sum, outer_in)
        middle_own, middle_x, middle_y = grid.fold_near(middle_sums, middle_x, middle_y)
        last_kept, last_core = grid.fold_parts([joined])
    grad_frames = product_back(grad_pair, full_cross_kv).astype(BF)
    hidden_rows = (after_cross + product(activated, full_outer) + bias[6]).astype(BF)
    if swift:
        grad_frames, hidden_rows, inner_in, outer_in, middle_x, middle_y, last_core = tied(
            grad_frames, hidden_rows, inner_in, outer_in, middle_x, middle_y, last_core
        )
        last_sums, last_x, last_y = grid.fold_far(last_kept, last_core)
        inner_sum, inner_in = grid.hop_three(inner_sum, inner_in)
        total_outer = grid.hop_end(outer_sum, outer_in)
        part_middle = plus3(middle_own, middle_x, middle_y)
        part_middle = jnp.concatenate([part_middle, part_kv], axis=1)
        last_own, last_x, last_y = grid.fold_near(last_sums, last_x, last_y)
        part_last = plus3(last_own, last_x, last_y)
        total_inner = grid.hop_end(inner_sum, inner_in)
    else:
        part_middle = scattered(jnp.concatenate(middle, axis=1))
        part_middle = jnp.concatenate([part_middle, part_kv], axis=1)
        part_last = scattered(joined)
        total_outer = grid.seq_sum(part_outer).astype(F32)
        total_inner = grid.seq_sum(part_inner).astype(F32)
    total_middle = grid.seq_sum(part_middle).astype(F32)
    total_cross_out, total_cross_q, total_self_out, total_cross_kv = jnp.split(
        total_middle, (width, 2 * width, 3 * width), axis=1
    )
    total = grid.seq_sum(part_last).astype(F32)
    total_qkv = total[:shard_rows]
    mine = total[shard_rows:].reshape(-1)[: kinds * shard].reshape(kinds, shard)

    late_rows = [
        jnp.concatenate(
            [
                grad_frames[padded * step : padded * step + frames],
                hidden_rows[rows * step : rows * (step + 1)],
            ],
            axis=0,
        )
        for step in range(grid.seq)
    ]
    late_rows = grid.hand_back(late_rows)
    grad_encoded, hidden_out = late_rows[:, :frames], late_rows[:, frames:]
    grad_hidden_in = grid.hand_back(
        [grad_rows[rows * step : rows * (step + 1)] for step in range(grid.seq)]
    )
    return (
        hidden_out,
        grad_hidden_in,
        grad_encoded,
        mine[:norms],
        mine[norms : 2 * norms],
        mine[2 * norms : 2 * norms + bias_count],
        total_qkv,
        total_self_out,
        total_cross_q,
        total_cross_kv,
        total_cross_out,
        total_inner,
        mine[2 * norms + bias_count :].reshape(-1),
        total_outer,
    )


def solution(mesh):
    rows = P("fsdp", "seq", None)
    wide = P(None, "fsdp")
    tall = P("fsdp", None)
    in_specs = (rows,) * 3 + (wide,) * 3 + (tall,) * 6 + (P("fsdp"), tall)
    out_specs = (rows,) * 3 + (wide,) * 3 + (tall,) * 6 + (P("fsdp"), tall)
    return jax.shard_map(
        functools.partial(local, dict(mesh.shape)),
        mesh=mesh,
        in_specs=in_specs,
        out_specs=out_specs,
        check_vma=False,
    )
```

```python
import functools

import jax
import jax.numpy as jnp
import numpy as np
from jax import lax
from jax.experimental import pallas as pl
from jax.experimental.pallas import tpu as pltpu
from jax.sharding import PartitionSpec as P

HD = 64
LANES = 128
NORM_EPSILON = 1e-05
LOW = -1e30
F32 = jnp.float32
BF = jnp.bfloat16
AXES = ("fsdp", "seq")


def two_heads(rows):
    lane = lax.broadcasted_iota(jnp.int32, rows.shape, 1)
    zero = jnp.zeros_like(rows)
    return jnp.concatenate(
        [jnp.where(lane < HD, rows, zero), jnp.where(lane >= HD, rows, zero)], axis=0
    )


def one_row(stacked):
    count = stacked.shape[0] // 2
    lane = lax.broadcasted_iota(jnp.int32, (count, stacked.shape[1]), 1)
    return jnp.where(lane < HD, stacked[:count], stacked[count:])


def over_rows(first, second):
    return lax.dot_general(first, second, (((0,), (0,)), ((), ())), preferred_element_type=F32)


def over_lanes(first, second):
    return lax.dot_general(first, second, (((1,), (1,)), ((), ())), preferred_element_type=F32)


def fill_scores(scores_ref, keys, queries, valid, places):
    size = keys.shape[0]
    scores = over_lanes(keys, queries)
    if places is not None:
        key_place, query_place = places
        scores = jnp.where(key_place <= query_place, scores, LOW)
    scores_ref[...] = scores
    if valid < size:
        first = valid // 8 * 8
        row = lax.broadcasted_iota(jnp.int32, (size - first, queries.shape[0]), 0)
        scores_ref[first:size] = jnp.where(row < valid - first, scores_ref[first:size], LOW)


def forward_kernel(chunk, valid, causal, *refs):
    if causal:
        q_ref, k_ref, v_ref, kp_ref, qp_ref, o_ref, log_ref, s_ref = refs
    else:
        q_ref, k_ref, v_ref, o_ref, log_ref, s_ref = refs
    queries = two_heads(q_ref[...])
    count = k_ref.shape[0] // chunk
    width = queries.shape[0]

    def first(step, top):
        rows = pl.ds(pl.multiple_of(step * chunk, chunk), chunk)
        places = (kp_ref[rows], qp_ref[...]) if causal else None
        part = s_ref.at[rows]
        fill_scores(part, k_ref[rows], queries, valid, places)
        return jnp.maximum(top, jnp.max(part[...], axis=0, keepdims=True))

    top = lax.fori_loop(0, count, first, jnp.full((1, width), LOW, F32))

    def second(step, carry):
        total, mixed = carry
        rows = pl.ds(pl.multiple_of(step * chunk, chunk), chunk)
        raised = jnp.exp(s_ref[rows] - top)
        total = total + jnp.sum(raised, axis=0, keepdims=True)
        mixed = mixed + over_rows(v_ref[rows], raised.astype(BF))
        return total, mixed

    total, mixed = lax.fori_loop(
        0, count, second, (jnp.zeros((1, width), F32), jnp.zeros((LANES, width), F32))
    )
    o_ref[...] = one_row(jnp.transpose(mixed / total)).astype(BF)
    log_ref[...] = (top + jnp.log(total))[None]


def backward_kernel(chunk, valid, causal, *refs):
    q_ref, k_ref, v_ref, o_ref, g_ref, log_ref = refs[:6]
    if causal:
        kp_ref, qp_ref = refs[6:8]
        joint_ref, s_ref, gk_ref, gv_ref = refs[-4:]
    else:
        gq_ref, joint_ref, s_ref, gv_ref = refs[-4:]
        gk_ref = joint_ref
    phase = pl.program_id(1)

    @pl.when(phase == 0)
    def _():
        queries = two_heads(q_ref[...])
        grads = two_heads(g_ref[...])
        mixed = o_ref[...].astype(F32)
        product = grads.astype(F32) * jnp.concatenate([mixed, mixed], axis=0)
        row_dot = jnp.sum(jnp.transpose(product), axis=0, keepdims=True)
        log_total = log_ref[0]
        width = queries.shape[0]

        def body(step, grad_queries):
            rows = pl.ds(pl.multiple_of(step * chunk, chunk), chunk)
            places = (kp_ref[rows], qp_ref[...]) if causal else None
            keys = k_ref[rows]
            fill_scores(s_ref, keys, queries, valid, places)
            weights = jnp.exp(s_ref[...] - log_total)
            grad_weights = over_lanes(v_ref[rows], grads)
            grad_scores = (weights * (grad_weights - row_dot)).astype(BF)
            gv_ref[rows] = jnp.dot(
                weights.astype(BF), grads, preferred_element_type=F32
            ).astype(BF)
            gk_ref[rows] = jnp.dot(grad_scores, queries, preferred_element_type=F32).astype(BF)
            return grad_queries + over_rows(keys, grad_scores)

        steps = k_ref.shape[0] // chunk
        grad_queries = lax.fori_loop(0, steps, body, jnp.zeros((LANES, width), F32))
        grad_queries = one_row(jnp.transpose(grad_queries)).astype(BF) * BF(HD**-0.5)
        (joint_ref if causal else gq_ref)[...] = grad_queries

    if causal:

        @pl.when(phase == 1)
        def _():
            joint_ref[...] = gk_ref[...]

    @pl.when(phase == (2 if causal else 1))
    def _():
        joint_ref[...] = gv_ref[...]


def columns(rows, first=0):
    return pl.BlockSpec((rows, LANES), lambda pair, *phase: (0, pair + first))


def place_specs(keys, tokens):
    return [
        pl.BlockSpec((keys, 1), lambda pair, *phase: (0, 0)),
        pl.BlockSpec((1, 2 * tokens), lambda pair, *phase: (0, 0)),
    ]


def log_spec(tokens, first=0):
    return pl.BlockSpec((1, 1, 2 * tokens), lambda pair, *phase: (pair + first, 0, 0))


def attend(sources, places, chunk, valid, width):
    tokens, count = sources[0][0].shape[0], sources[1][0].shape[0]
    causal = places is not None
    pairs = width // LANES
    specs = [columns(member.shape[0], first) for member, first in sources]
    operands = [member for member, _ in sources]
    if causal:
        specs += place_specs(count, tokens)
        operands += list(places)
    return pl.pallas_call(
        functools.partial(forward_kernel, chunk, valid, causal),
        grid=(pairs,),
        in_specs=specs,
        out_specs=[columns(tokens), log_spec(tokens)],
        out_shape=[
            jax.ShapeDtypeStruct((tokens, width), BF),
            jax.ShapeDtypeStruct((pairs, 1, 2 * tokens), F32),
        ],
        scratch_shapes=[pltpu.VMEM((count, 2 * tokens), F32)],
        compiler_params=pltpu.CompilerParams(vmem_limit_bytes=32 << 20),
        cost_estimate=pl.CostEstimate(
            flops=16 * tokens * count * width,
            transcendentals=tokens * count * width // HD,
            bytes_accessed=4 * (tokens + count) * width,
        ),
        name="attend_causal" if causal else "attend_cross",
    )(*operands)


def attend_back(
    sources, mixed, grads, logs, places, chunk, valid, width, part=0, parts=1, before=()
):
    tokens, count = sources[0][0].shape[0], sources[1][0].shape[0]
    causal = places is not None
    pairs = width // LANES
    count_here = pairs // parts
    low = part * count_here
    specs = [columns(member.shape[0], first + low) for member, first in sources]
    specs += [columns(tokens, low), columns(tokens, low), log_spec(tokens, low)]
    operands = [member for member, _ in sources] + [mixed, grads, logs]
    joint_spec = pl.BlockSpec(
        (count, LANES), lambda pair, phase: (0, pair + low + pairs * phase)
    )
    if causal:
        specs += place_specs(count, tokens)
        operands += list(places)
        out_specs = [joint_spec]
        out_shape = [jax.ShapeDtypeStruct((count, 3 * width), BF)]
    else:
        out_specs = [columns(tokens, low), joint_spec]
        out_shape = [
            jax.ShapeDtypeStruct((tokens, width), BF),
            jax.ShapeDtypeStruct((count, 2 * width), BF),
        ]
    aliases = {len(operands) + i: i for i in range(len(before))}
    specs += [pl.BlockSpec(memory_space=pl.ANY)] * len(before)
    operands += list(before)
    kept = [pltpu.VMEM((count, LANES), BF)] * (2 if causal else 1)
    return pl.pallas_call(
        functools.partial(backward_kernel, chunk, valid, causal),
        grid=(count_here, 3 if causal else 2),
        in_specs=specs,
        out_specs=out_specs,
        out_shape=out_shape,
        scratch_shapes=[pltpu.VMEM((chunk, 2 * tokens), F32)] + kept,
        input_output_aliases=aliases,
        compiler_params=pltpu.CompilerParams(vmem_limit_bytes=32 << 20),
        cost_estimate=pl.CostEstimate(
            flops=40 * tokens * count * width // parts,
            transcendentals=tokens * count * width // HD // parts,
            bytes_accessed=8 * (tokens + count) * width // parts,
        ),
        name="attend_causal_back" if causal else "attend_cross_back",
    )(*operands)


def product(first, second):
    return jnp.dot(first, second, preferred_element_type=F32)


def product_back(incoming, weight):
    return lax.dot_general(
        incoming, weight, (((1,), (1,)), ((), ())), preferred_element_type=F32
    )


def weight_grad(operand, incoming):
    return lax.dot_general(
        operand, incoming, (((0,), (0,)), ((), ())), preferred_element_type=F32
    ).astype(BF)


def normalized(values):
    average = jnp.mean(values, axis=-1, keepdims=True)
    centred = values - average
    variance = jnp.mean(centred * centred, axis=-1, keepdims=True)
    inverse = lax.rsqrt(variance + NORM_EPSILON)
    return centred * inverse, inverse


def norm_back(incoming, values, gain_row):
    rows, inverse = normalized(values)
    scaled = incoming * gain_row
    average = jnp.mean(scaled, axis=-1, keepdims=True)
    aligned = jnp.mean(scaled * rows, axis=-1, keepdims=True)
    gain_grad = jnp.sum(incoming * rows, axis=0)
    shift_grad = jnp.sum(incoming, axis=0)
    return (scaled - average - rows * aligned) * inverse, gain_grad, shift_grad


def gelu(values):
    return values * (1.0 + lax.erf(values * (0.5**0.5))) * 0.5


def gelu_slope(values):
    return (1.0 + lax.erf(values * (0.5**0.5))) * 0.5 + values * jnp.exp(
        -0.5 * values * values
    ) * (0.5 / jnp.pi) ** 0.5


class Grid:
    def __init__(self, fsdp, seq, clips):
        self.fsdp, self.seq, self.clips = fsdp, seq, clips
        self.here = lax.axis_index("seq")
        self.group = lax.axis_index("fsdp")
        self.first = self.first_of(self.group)

    def first_of(self, group):
        return (group % 2) * (self.seq - self.clips)

    def works(self, group, place):
        return 0 <= place - self.first_of(group) < self.clips

    def turn(self, values, step, to_workers):
        pairs = []
        for group in range(self.fsdp):
            for place in range(self.seq):
                target = (place + step) % self.seq
                worker = target if to_workers else place
                if self.works(group, worker):
                    pairs.append((group * self.seq + place, group * self.seq + target))
        return lax.ppermute(values, AXES, pairs)

    def clip_at(self, place):
        return jnp.clip(place - self.first, 0, self.clips - 1)

    def collect(self, values, steps):
        pieces = {}
        for step in steps:
            target = (self.here + step) % self.seq
            sent = lax.dynamic_index_in_dim(values, self.clip_at(target), 0, keepdims=False)
            if step == 0:
                active = (self.here >= self.first) & (self.here < self.first + self.clips)
                pieces[step] = jnp.where(active, sent, jnp.zeros_like(sent))
            else:
                pieces[step] = self.turn(sent, step, True)
        return pieces

    def hand_back(self, rows):
        parts = rows.reshape(self.seq, -1, rows.shape[1])
        moved = lax.all_to_all(parts, "seq", split_axis=0, concat_axis=0, tiled=True)
        return lax.dynamic_slice_in_dim(moved, self.first, self.clips, 0)

    def chain(self, values, links):
        pairs = [
            (group * self.seq + a, group * self.seq + b)
            for group in range(self.fsdp)
            for a, b in links
        ]
        return lax.ppermute(values, AXES, pairs)

    def flip(self, values, bits):
        return lax.ppermute(values, "fsdp", [(f, f ^ bits) for f in range(self.fsdp)])

    def spread_far(self, shard, by_x, by_y):
        half = shard.shape[0] // 2
        return self.flip(by_y[:half], 2), self.flip(by_x[half:], 4)

    def spread_core(self, shard, by_x, by_y, far_x, far_y):
        mine = jnp.stack([shard, by_x, by_y, jnp.concatenate([far_x, far_y], axis=0)])
        return mine, self.flip(mine, 1)

    def fold_core(self, *members):
        core = self.group % 2
        parts = [m.reshape(4, 2, m.shape[0] // 8, m.shape[1]) for m in members]
        sent = jnp.concatenate([pick(p, 1 - core, 1) for p in parts], axis=2)
        kept = jnp.concatenate([pick(p, core, 1) for p in parts], axis=2)
        return kept, self.flip(sent, 1)

    def fold_chips(self, kept, arrived):
        sums = plus(kept, arrived)
        chip = self.group // 2
        moved = [self.flip(pick(sums, chip ^ bits, 0), 2 * bits) for bits in (1, 2, 3)]
        return pick(sums, chip, 0), moved

    def hop_one(self, values):
        return values, self.chain(values, ((0, 1), (3, 2)))

    def hop_two(self, values, arrived):
        half = plus(values, arrived)
        return half, self.chain(half, ((1, 2), (2, 1)))

    def hop_three(self, half, arrived):
        whole = plus(half, arrived)
        return whole, self.chain(whole, ((1, 0), (2, 3)))

    def hop_end(self, whole, back):
        return jnp.where((self.here == 0) | (self.here == 3), back, whole).astype(F32)

    def seq_sum(self, values):
        if self.seq != 4:
            return lax.psum(values, "seq").astype(F32)
        return self.hop_end(*self.hop_three(*self.hop_two(*self.hop_one(values))))


def pick(values, index, axis):
    return lax.dynamic_index_in_dim(values, index, axis, keepdims=False)


def plus(first, second):
    return (first.astype(F32) + second.astype(F32)).astype(first.dtype)


def plus_all(first, others):
    total = first.astype(F32)
    for other in others:
        total = total + other.astype(F32)
    return total.astype(first.dtype)


def tied(*members):
    return lax.optimization_barrier(members)


def place_kernel(parts, here_ref, *refs):
    count = len(refs) - len(parts)
    pieces, outs = refs[:count], refs[count:]

    def store(piece):
        for out, (low, high, padded) in zip(outs, parts):
            out[: high - low] = piece[low:high]
            if padded > high - low:
                out[high - low :] = jnp.zeros((padded - high + low, out.shape[1]), out.dtype)

    for step, piece in enumerate(pieces):
        pl.when(pl.program_id(0) == step)(functools.partial(store, piece))


def place(here, pieces, parts):
    count = len(pieces)
    rows, width = pieces[0].shape
    return pl.pallas_call(
        functools.partial(place_kernel, parts),
        grid_spec=pltpu.PrefetchScalarGridSpec(
            num_scalar_prefetch=1,
            grid=(count,),
            in_specs=[pl.BlockSpec((rows, width), lambda step, here: (0, 0))] * count,
            out_specs=[
                pl.BlockSpec((padded, width), lambda step, here: ((here[0] - step) % count, 0))
                for _, _, padded in parts
            ],
        ),
        out_shape=[
            jax.ShapeDtypeStruct((count * padded, width), BF) for _, _, padded in parts
        ],
        compiler_params=pltpu.CompilerParams(vmem_limit_bytes=24 << 20),
        cost_estimate=pl.CostEstimate(
            flops=0, transcendentals=0, bytes_accessed=4 * count * rows * width
        ),
        name="place",
    )(here.reshape(1), *pieces)


def assemble_kernel(widths, rows, group_ref, mine_ref, other_ref, *outs):
    flipped = group_ref[0] % 2

    def store(first_ref, second_ref):
        start = 0
        for out, width in zip(outs, widths):
            out[:rows] = first_ref[0, :, start : start + width]
            out[rows:] = second_ref[0, :, start : start + width]
            start += width

    pl.when(flipped == 0)(lambda: store(mine_ref, other_ref))
    pl.when(flipped == 1)(lambda: store(other_ref, mine_ref))


def assemble(group, mine, other, widths):
    rows, total = mine.shape[1], mine.shape[2]
    source = pl.BlockSpec((1, rows, total), lambda chip, group: (chip, 0, 0))
    return pl.pallas_call(
        functools.partial(assemble_kernel, widths, rows),
        grid_spec=pltpu.PrefetchScalarGridSpec(
            num_scalar_prefetch=1,
            grid=(4,),
            in_specs=[source, source],
            out_specs=[
                pl.BlockSpec((2 * rows, width), lambda chip, group: ((group[0] // 2) ^ chip, 0))
                for width in widths
            ],
        ),
        out_shape=[jax.ShapeDtypeStruct((8 * rows, width), BF) for width in widths],
        compiler_params=pltpu.CompilerParams(vmem_limit_bytes=16 << 20),
        cost_estimate=pl.CostEstimate(
            flops=0, transcendentals=0, bytes_accessed=32 * rows * total
        ),
        name="assemble",
    )(group.reshape(1), mine, other)


def local(
    mesh_shape,
    hidden_in,
    encoded,
    out_grad,
    norm_gain,
    norm_shift,
    biases,
    self_qkv,
    self_out,
    cross_q,
    cross_kv,
    cross_out,
    mlp_in,
    mlp_in_bias,
    mlp_out,
):
    clips, rows, width = hidden_in.shape
    frames = encoded.shape[1]
    padded = (frames + 15) // 16 * 16
    grid = Grid(mesh_shape["fsdp"], mesh_shape["seq"], clips)
    shard = norm_gain.shape[1]
    norms = norm_gain.shape[0]
    bias_count = biases.shape[0]
    scaling = HD ** (-0.5)
    swift = grid.fsdp == 8 and grid.seq == 4 and self_qkv.shape[0] >= 32

    def gathered(*members):
        widths = [member.shape[1] for member in members]
        joined = jnp.concatenate(members, axis=1)
        joined = lax.all_gather(joined, "fsdp", axis=0, tiled=True)
        return jnp.split(joined, np.cumsum(widths)[:-1].tolist(), axis=1)

    def scattered(member):
        return lax.psum_scatter(member, "fsdp", scatter_dimension=0, tiled=True)

    tokens_in = jnp.concatenate([hidden_in, encoded], axis=1)
    pieces = grid.collect(tokens_in, (0, 1, 3) if swift else range(grid.seq))
    small = jnp.concatenate([norm_gain, norm_shift, biases, mlp_in_bias.reshape(-1, shard)], axis=0)
    kinds = small.shape[0]
    shard_rows = self_qkv.shape[0]
    if swift:
        small = jnp.pad(small, ((0, shard_rows - kinds), (0, 0)))
        first_shard = jnp.concatenate([self_qkv, small], axis=1)
        first_widths = (self_qkv.shape[1], shard)
        first_x, first_y = grid.flip(first_shard, 2), grid.flip(first_shard, 4)
    full_self_out, full_cross_q, full_cross_kv = gathered(self_out, cross_q, cross_kv)
    full_cross_out, full_inner = gathered(cross_out, mlp_in)
    if swift:
        first_x, first_y, pieces[1], pieces[3], tokens_in = tied(
            first_x, first_y, pieces[1], pieces[3], tokens_in
        )
        pieces.update(grid.collect(tokens_in, (2,)))
        far_x, far_y = grid.spread_far(first_shard, first_x, first_y)
        far_x, far_y, pieces[2] = tied(far_x, far_y, pieces[2])
        mine, other = grid.spread_core(first_shard, first_x, first_y, far_x, far_y)
        other, mlp_out = tied(other, mlp_out)
        outer_x, outer_y = grid.flip(mlp_out, 2), grid.flip(mlp_out, 4)
        full_qkv, small = assemble(grid.group, mine, other, first_widths)
        small = small.reshape(grid.fsdp, shard_rows, shard)[:, :kinds]
    else:
        (full_qkv,) = gathered(self_qkv)
        small = lax.all_gather(small, "fsdp", axis=0)
        (full_outer,) = gathered(mlp_out)
    vectors = small[:, : 2 * norms + bias_count].swapaxes(0, 1).reshape(-1, width).astype(F32)
    gain, shift, bias = vectors[:norms], vectors[norms : 2 * norms], vectors[2 * norms :]
    inner_bias = small[:, 2 * norms + bias_count :].reshape(1, -1).astype(F32)
    none = jnp.zeros((width,), F32)

    token_rows, frame_rows = place(
        grid.here,
        [pieces[step] for step in range(grid.seq)],
        ((0, rows, rows), (rows, rows + frames, padded)),
    )
    residual_in = token_rows.astype(F32)
    normed_one = (normalized(residual_in)[0] * gain[0] + shift[0]).astype(BF)
    tokens = grid.seq * rows
    line = jnp.arange(tokens)
    places = (line[:, None], jnp.concatenate([line, line])[None, :])
    blocks = width // LANES

    qkv_bias = jnp.concatenate([bias[0], none, bias[1]])
    qkv_scale = jnp.concatenate([none + scaling, none + 1.0, none + 1.0])
    qkv = ((product(normed_one, full_qkv) + qkv_bias) * qkv_scale).astype(BF)
    self_sources = ((qkv, 0), (qkv, blocks), (qkv, 2 * blocks))
    self_mix, self_log = attend(self_sources, places, tokens, tokens, width)
    after_self = residual_in + product(self_mix, full_self_out) + bias[2]
    normed_two = (normalized(after_self)[0] * gain[1] + shift[1]).astype(BF)
    cross_queries = ((product(normed_two, full_cross_q) + bias[3]) * scaling).astype(BF)
    out_grad, cross_queries = tied(out_grad, cross_queries)
    top_pieces = list(grid.collect(out_grad, range(grid.seq)).values())
    kv_bias = jnp.concatenate([none, bias[4]])
    cross_pair = (product(frame_rows, full_cross_kv) + kv_bias).astype(BF)
    cross_sources = ((cross_queries, 0), (cross_pair, 0), (cross_pair, blocks))
    cross_mix, cross_log = attend(cross_sources, None, padded, frames, width)
    if swift:
        cross_mix, outer_x, outer_y, *top_pieces = tied(cross_mix, outer_x, outer_y, *top_pieces)
        far_x, far_y = grid.spread_far(mlp_out, outer_x, outer_y)
    (top,) = place(grid.here, top_pieces, ((0, rows, rows),))
    after_cross = after_self + product(cross_mix, full_cross_out) + bias[5]
    normed_three = (normalized(after_cross)[0] * gain[2] + shift[2]).astype(BF)
    inner = product(normed_three, full_inner) + inner_bias
    activated = gelu(inner).astype(BF)
    if swift:
        activated, far_x, far_y = tied(activated, far_x, far_y)
        mine, other = grid.spread_core(mlp_out, outer_x, outer_y, far_x, far_y)

    top_wide = top.astype(F32)
    grad_w_outer = weight_grad(activated, top)
    if swift:
        grad_w_outer, top, other = tied(grad_w_outer, top, other)
        (full_outer,) = assemble(grid.group, mine, other, (mlp_out.shape[1],))
    part_outer = scattered(grad_w_outer)
    grad_bias_six = jnp.sum(top_wide, axis=0)
    grad_inner = product_back(top, full_outer) * gelu_slope(inner)
    grad_inner_low = grad_inner.astype(BF)
    grad_w_inner = weight_grad(normed_three, grad_inner_low)
    grad_w_inner, grad_inner_low = tied(grad_w_inner, grad_inner_low)
    part_inner = scattered(grad_w_inner)
    grad_inner_bias = jnp.sum(grad_inner, axis=0)
    grad_normed_three = product_back(grad_inner_low, full_inner)
    from_three, gain_three, shift_three = norm_back(grad_normed_three, after_cross, gain[2])
    grad_after_cross = top_wide + from_three
    grad_cross_low = grad_after_cross.astype(BF)
    grad_bias_five = jnp.sum(grad_after_cross, axis=0)
    grad_w_cross_out = weight_grad(cross_mix, grad_cross_low)
    grad_cross_mix = product_back(grad_cross_low, full_cross_out).astype(BF)

    cross_back = functools.partial(
        attend_back,
        cross_sources,
        cross_mix,
        logs=cross_log,
        places=None,
        chunk=padded,
        valid=frames,
        width=width,
        parts=2,
    )
    first_part = cross_back(grads=grad_cross_mix)
    if swift:
        grad_cross_mix, part_outer, *first_part = tied(grad_cross_mix, part_outer, *first_part)
        outer_sum, outer_in = grid.hop_one(part_outer)
    grad_cross_queries, grad_pair = cross_back(
        grads=grad_cross_mix, part=1, before=tuple(first_part)
    )
    if swift:
        grad_cross_queries, grad_pair, outer_in = tied(grad_cross_queries, grad_pair, outer_in)
        outer_sum, outer_in = grid.hop_two(outer_sum, outer_in)
    grad_frames = product_back(grad_pair, full_cross_kv).astype(BF)
    grad_frames, grad_pair = tied(grad_frames, grad_pair)
    grad_encoded = grid.hand_back(grad_frames)
    grad_w_cross_kv = weight_grad(frame_rows, grad_pair)
    if swift:
        grad_w_cross_kv, grad_cross_queries, outer_in = tied(
            grad_w_cross_kv, grad_cross_queries, outer_in
        )
        outer_sum, outer_in = grid.hop_three(outer_sum, outer_in)
    part_kv = scattered(grad_w_cross_kv)
    grad_bias_four = jnp.sum(grad_pair[:, width:].astype(F32), axis=0)
    grad_w_cross_q = weight_grad(normed_two, grad_cross_queries)
    grad_bias_three = jnp.sum(grad_cross_queries.astype(F32), axis=0)
    grad_normed_two = product_back(grad_cross_queries, full_cross_q)
    from_two, gain_two, shift_two = norm_back(grad_normed_two, after_self, gain[1])
    grad_after_self = grad_after_cross + from_two
    grad_self_low = grad_after_self.astype(BF)
    grad_w_self_out = weight_grad(self_mix, grad_self_low)
    grad_bias_two = jnp.sum(grad_after_self, axis=0)
    grad_self_mix = product_back(grad_self_low, full_self_out).astype(BF)
    middle = [grad_w_cross_out, grad_w_cross_q, grad_w_self_out]
    if swift:
        grad_self_mix, *middle = tied(grad_self_mix, *middle)
        middle_kept, middle_core = grid.fold_core(*middle)
    (grad_pre,) = attend_back(
        self_sources, self_mix, grad_self_mix, self_log, places, tokens, tokens, width
    )
    if swift:
        grad_pre, middle_core, part_inner = tied(grad_pre, middle_core, part_inner)
        middle_own, middle_near = grid.fold_chips(middle_kept, middle_core)
        inner_sum, inner_in = grid.hop_one(part_inner)
    grad_normed_one = product_back(grad_pre, full_qkv)
    grad_w_qkv = weight_grad(normed_one, grad_pre)
    pre_sums = jnp.sum(grad_pre.astype(F32), axis=0)
    from_one, gain_one, shift_one = norm_back(grad_normed_one, residual_in, gain[0])
    grad_rows = (grad_after_self + from_one).astype(BF)

    sums = jnp.stack(
        [
            gain_one,
            gain_two,
            gain_three,
            shift_one,
            shift_two,
            shift_three,
            pre_sums[:width],
            pre_sums[2 * width :],
            grad_bias_two,
            grad_bias_three,
            grad_bias_four,
            grad_bias_five,
            grad_bias_six,
        ]
    )
    inner_sums = grad_inner_bias.reshape(grid.fsdp, -1, shard)
    packed = jnp.concatenate(
        [sums.reshape(-1, grid.fsdp, shard).swapaxes(0, 1), inner_sums], axis=1
    )
    if swift:
        packed = jnp.pad(packed.astype(BF), ((0, 0), (0, shard_rows - kinds), (0, 0)))
        packed = packed.reshape(-1, shard)
        last_kept, last_core = grid.fold_core(grad_w_qkv, packed)
        last_kept, activated, grad_rows = tied(last_kept, activated, grad_rows)
    hidden_rows = (after_cross + product(activated, full_outer) + bias[6]).astype(BF)
    leaving = jnp.concatenate(
        [
            grad_rows.reshape(grid.seq, rows, width),
            hidden_rows.reshape(grid.seq, rows, width),
        ],
        axis=1,
    ).reshape(-1, width)
    if swift:
        last_core, leaving, inner_in, outer_in = tied(last_core, leaving, inner_in, outer_in)
        last_own, last_near = grid.fold_chips(last_kept, last_core)
        inner_sum, inner_in = grid.hop_two(inner_sum, inner_in)
    leaving = grid.hand_back(leaving)
    if swift:
        part_middle = jnp.concatenate([plus_all(middle_own, middle_near), part_kv], axis=1)
        middle_sum, middle_in = grid.hop_one(part_middle)
        middle_in, inner_in, grad_encoded, *last_near = tied(
            middle_in, inner_in, grad_encoded, *last_near
        )
        part_last = plus_all(last_own, last_near)
        half = 12 * LANES
        last_one, one_in = grid.hop_one(part_last[:, :half])
        last_two, two_in = grid.hop_one(part_last[:, half:])
        inner_sum, inner_in = grid.hop_three(inner_sum, inner_in)
        middle_sum, middle_in = grid.hop_two(middle_sum, middle_in)
        total_outer = grid.hop_end(outer_sum, outer_in)
        last_one, one_in = grid.hop_two(last_one, one_in)
        last_two, two_in = grid.hop_two(last_two, two_in)
        middle_sum, middle_in = grid.hop_three(middle_sum, middle_in)
        total_inner = grid.hop_end(inner_sum, inner_in)
        last_one, one_in = grid.hop_three(last_one, one_in)
        last_two, two_in = grid.hop_three(last_two, two_in)
        total_middle = grid.hop_end(middle_sum, middle_in)
        total_last = jnp.concatenate(
            [grid.hop_end(last_one, one_in), grid.hop_end(last_two, two_in)], axis=1
        )
        total_qkv = total_last[:, : grad_w_qkv.shape[1]]
        mine = total_last[:kinds, grad_w_qkv.shape[1] :]
    else:
        part_middle = jnp.concatenate(
            [scattered(jnp.concatenate(middle, axis=1)), part_kv], axis=1
        )
        total_outer = grid.seq_sum(part_outer)
        total_inner = grid.seq_sum(part_inner)
        total_middle = grid.seq_sum(part_middle)
        total_qkv = grid.seq_sum(scattered(grad_w_qkv))
        mine = pick(lax.psum(packed, AXES), grid.group, 0)
    total_cross_out, total_cross_q, total_self_out, total_cross_kv = jnp.split(
        total_middle, (width, 2 * width, 3 * width), axis=1
    )

    grad_encoded = grad_encoded[:, :frames]
    grad_hidden_in, hidden_out = leaving[:, :rows], leaving[:, rows:]
    return (
        hidden_out,
        grad_hidden_in,
        grad_encoded,
        mine[:norms],
        mine[norms : 2 * norms],
        mine[2 * norms : 2 * norms + bias_count],
        total_qkv,
        total_self_out,
        total_cross_q,
        total_cross_kv,
        total_cross_out,
        total_inner,
        mine[2 * norms + bias_count :].reshape(-1),
        total_outer,
    )


def solution(mesh):
    rows = P("fsdp", "seq", None)
    wide = P(None, "fsdp")
    tall = P("fsdp", None)
    in_specs = (rows,) * 3 + (wide,) * 3 + (tall,) * 6 + (P("fsdp"), tall)
    out_specs = (rows,) * 3 + (wide,) * 3 + (tall,) * 6 + (P("fsdp"), tall)
    return jax.shard_map(
        functools.partial(local, dict(mesh.shape)),
        mesh=mesh,
        in_specs=in_specs,
        out_specs=out_specs,
        check_vma=False,
    )
```

```python
import functools

import jax
import jax.numpy as jnp
import numpy as np
from jax import lax
from jax.experimental import pallas as pl
from jax.experimental.pallas import tpu as pltpu
from jax.sharding import PartitionSpec as P

HD = 64
LANES = 128
NORM_EPSILON = 1e-05
LOW = -1e30
F32 = jnp.float32
BF = jnp.bfloat16
AXES = ("fsdp", "seq")


def two_heads(rows):
    lane = lax.broadcasted_iota(jnp.int32, rows.shape, 1)
    zero = jnp.zeros_like(rows)
    return jnp.concatenate(
        [jnp.where(lane < HD, rows, zero), jnp.where(lane >= HD, rows, zero)], axis=0
    )


def one_row(stacked):
    count = stacked.shape[0] // 2
    lane = lax.broadcasted_iota(jnp.int32, (count, stacked.shape[1]), 1)
    return jnp.where(lane < HD, stacked[:count], stacked[count:])


def over_rows(first, second):
    return lax.dot_general(first, second, (((0,), (0,)), ((), ())), preferred_element_type=F32)


def over_lanes(first, second):
    return lax.dot_general(first, second, (((1,), (1,)), ((), ())), preferred_element_type=F32)


def chunk_scores(keys, queries, places, step):
    scores = over_lanes(keys, queries)
    if places is not None:
        key_ref, query_ref = places
        rows = slice(step * keys.shape[0], (step + 1) * keys.shape[0])
        scores = jnp.where(key_ref[rows] <= query_ref[...], scores, LOW)
    return scores


def tail_kept(values, valid, other):
    size = values.shape[0]
    if valid == size:
        return values
    first = valid // 8 * 8
    row = lax.broadcasted_iota(jnp.int32, (size - first, values.shape[1]), 0)
    tail = jnp.where(row < valid - first, values[first:], other)
    return jnp.concatenate([values[:first], tail], axis=0)


def forward_kernel(chunk, valid, causal, *refs):
    q_ref, k_ref, v_ref = refs[:3]
    places = refs[3:5] if causal else None
    o_ref, log_ref, s_ref = refs[-3:]
    queries = two_heads(q_ref[...])
    width = queries.shape[0]
    strips = [slice(low, low + chunk) for low in range(0, k_ref.shape[0], chunk)]
    top = jnp.full((1, width), LOW, F32)
    for step, rows in enumerate(strips):
        scores = tail_kept(chunk_scores(k_ref[rows], queries, places, step), valid, LOW)
        s_ref[rows] = scores
        top = jnp.maximum(top, jnp.max(scores, axis=0, keepdims=True))
    total, mixed = jnp.zeros((1, width), F32), jnp.zeros((LANES, width), F32)
    for rows in strips:
        raised = jnp.exp(s_ref[rows] - top)
        total = total + jnp.sum(raised, axis=0, keepdims=True)
        mixed = mixed + over_rows(v_ref[rows], raised.astype(BF))
    o_ref[...] = one_row(jnp.transpose(mixed / total)).astype(BF)
    log_ref[...] = (top + jnp.log(total))[None]


def pair_back(chunk, valid, places, refs, store_key, store_value):
    q_ref, k_ref, v_ref, o_ref, g_ref, log_ref = refs
    queries = two_heads(q_ref[...])
    grads = two_heads(g_ref[...])
    mixed = o_ref[...].astype(F32)
    product = grads.astype(F32) * jnp.concatenate([mixed, mixed], axis=0)
    row_dot = jnp.sum(jnp.transpose(product), axis=0, keepdims=True)
    log_total = log_ref[0]
    grad_queries = jnp.zeros((LANES, queries.shape[0]), F32)
    for step, low in enumerate(range(0, k_ref.shape[0], chunk)):
        rows = slice(low, low + chunk)
        keys = k_ref[rows]
        scores = chunk_scores(keys, queries, places, step)
        weights = jnp.exp(tail_kept(scores, valid, LOW) - log_total)
        grad_weights = over_lanes(v_ref[rows], grads)
        grad_scores = (weights * (grad_weights - row_dot)).astype(BF)
        store_value(rows, jnp.dot(weights.astype(BF), grads, preferred_element_type=F32))
        store_key(rows, jnp.dot(grad_scores, queries, preferred_element_type=F32))
        grad_queries = grad_queries + over_rows(keys, grad_scores)
    return one_row(jnp.transpose(grad_queries)).astype(BF) * BF(HD**-0.5)


def cross_back_kernel(chunk, valid, *refs):
    gq_ref, joint_ref, gv_ref = refs[-3:]
    phase = pl.program_id(1)

    @pl.when(phase == 0)
    def _():
        def store_key(rows, part):
            joint_ref[rows] = part.astype(BF)

        def store_value(rows, part):
            gv_ref[rows] = part.astype(BF)

        gq_ref[...] = pair_back(chunk, valid, None, refs[:6], store_key, store_value)

    @pl.when(phase == 1)
    def _():
        joint_ref[...] = gv_ref[...]


def causal_back_kernel(chunk, width, *refs):
    joint_ref = refs[-1]

    def lanes(part):
        start = part * width + pl.program_id(0) * LANES
        return pl.ds(pl.multiple_of(start, LANES), LANES)

    def store_key(rows, part):
        joint_ref[rows, lanes(1)] = part.astype(BF)

    def store_value(rows, part):
        joint_ref[rows, lanes(2)] = part.astype(BF)

    joint_ref[:, lanes(0)] = pair_back(
        chunk, chunk, refs[6:8], refs[:6], store_key, store_value
    )


def columns(rows, first=0):
    return pl.BlockSpec((rows, LANES), lambda pair, *phase: (0, pair + first))


def place_specs(keys, tokens):
    return [
        pl.BlockSpec((keys, 1), lambda pair, *phase: (0, 0)),
        pl.BlockSpec((1, 2 * tokens), lambda pair, *phase: (0, 0)),
    ]


def log_spec(tokens, first=0):
    return pl.BlockSpec((1, 1, 2 * tokens), lambda pair, *phase: (pair + first, 0, 0))


def attend(sources, places, chunk, valid, width):
    tokens, count = sources[0][0].shape[0], sources[1][0].shape[0]
    causal = places is not None
    pairs = width // LANES
    specs = [columns(member.shape[0], first) for member, first in sources]
    operands = [member for member, _ in sources]
    if causal:
        specs += place_specs(count, tokens)
        operands += list(places)
    return pl.pallas_call(
        functools.partial(forward_kernel, chunk, valid, causal),
        grid=(pairs,),
        in_specs=specs,
        out_specs=[columns(tokens), log_spec(tokens)],
        out_shape=[
            jax.ShapeDtypeStruct((tokens, width), BF),
            jax.ShapeDtypeStruct((pairs, 1, 2 * tokens), F32),
        ],
        scratch_shapes=[pltpu.VMEM((count, 2 * tokens), F32)],
        compiler_params=pltpu.CompilerParams(vmem_limit_bytes=32 << 20),
        cost_estimate=pl.CostEstimate(
            flops=16 * tokens * count * width,
            transcendentals=tokens * count * width // HD,
            bytes_accessed=4 * (tokens + count) * width,
        ),
        name="attend_causal" if causal else "attend_cross",
    )(*operands)


def attend_back(
    sources, mixed, grads, logs, places, chunk, valid, width, part=0, parts=1, before=()
):
    tokens, count = sources[0][0].shape[0], sources[1][0].shape[0]
    causal = places is not None
    pairs = width // LANES
    count_here = pairs // parts
    low = part * count_here
    specs = [columns(member.shape[0], first + low) for member, first in sources]
    specs += [columns(tokens, low), columns(tokens, low), log_spec(tokens, low)]
    operands = [member for member, _ in sources] + [mixed, grads, logs]
    if causal:
        specs += place_specs(count, tokens)
        operands += list(places)
        kernel = functools.partial(causal_back_kernel, chunk, width)
        grid = (count_here,)
        out_specs = [pl.BlockSpec((count, 3 * width), lambda pair: (0, 0))]
        out_shape = [jax.ShapeDtypeStruct((count, 3 * width), BF)]
        kept = []
    else:
        kernel = functools.partial(cross_back_kernel, chunk, valid)
        grid = (count_here, 2)
        out_specs = [
            columns(tokens, low),
            pl.BlockSpec((count, LANES), lambda pair, phase: (0, pair + low + pairs * phase)),
        ]
        out_shape = [
            jax.ShapeDtypeStruct((tokens, width), BF),
            jax.ShapeDtypeStruct((count, 2 * width), BF),
        ]
        kept = [pltpu.VMEM((count, LANES), BF)]
    aliases = {len(operands) + i: i for i in range(len(before))}
    specs += [pl.BlockSpec(memory_space=pl.ANY)] * len(before)
    operands += list(before)
    return pl.pallas_call(
        kernel,
        grid=grid,
        in_specs=specs,
        out_specs=out_specs,
        out_shape=out_shape,
        scratch_shapes=kept,
        input_output_aliases=aliases,
        compiler_params=pltpu.CompilerParams(vmem_limit_bytes=32 << 20),
        cost_estimate=pl.CostEstimate(
            flops=40 * tokens * count * width // parts,
            transcendentals=tokens * count * width // HD // parts,
            bytes_accessed=8 * (tokens + count) * width // parts,
        ),
        name="attend_causal_back" if causal else "attend_cross_back",
    )(*operands)


def product(first, second):
    return jnp.dot(first, second, preferred_element_type=F32)


def product_back(incoming, weight):
    return lax.dot_general(
        incoming, weight, (((1,), (1,)), ((), ())), preferred_element_type=F32
    )


def weight_grad(operand, incoming):
    return lax.dot_general(
        operand, incoming, (((0,), (0,)), ((), ())), preferred_element_type=F32
    ).astype(BF)


def normalized(values):
    average = jnp.mean(values, axis=-1, keepdims=True)
    centred = values - average
    variance = jnp.mean(centred * centred, axis=-1, keepdims=True)
    inverse = lax.rsqrt(variance + NORM_EPSILON)
    return centred * inverse, inverse


def norm_back(incoming, values, gain_row):
    rows, inverse = normalized(values)
    scaled = incoming * gain_row
    average = jnp.mean(scaled, axis=-1, keepdims=True)
    aligned = jnp.mean(scaled * rows, axis=-1, keepdims=True)
    gain_grad = jnp.sum(incoming * rows, axis=0)
    shift_grad = jnp.sum(incoming, axis=0)
    return (scaled - average - rows * aligned) * inverse, gain_grad, shift_grad


def gelu(values):
    return values * (1.0 + lax.erf(values * (0.5**0.5))) * 0.5


def gelu_slope(values):
    return (1.0 + lax.erf(values * (0.5**0.5))) * 0.5 + values * jnp.exp(
        -0.5 * values * values
    ) * (0.5 / jnp.pi) ** 0.5


class Grid:
    def __init__(self, fsdp, seq, clips):
        self.fsdp, self.seq, self.clips = fsdp, seq, clips
        self.here = lax.axis_index("seq")
        self.group = lax.axis_index("fsdp")
        self.first = self.first_of(self.group)

    def first_of(self, group):
        return (group % 2) * (self.seq - self.clips)

    def works(self, group, place):
        return 0 <= place - self.first_of(group) < self.clips

    def turn(self, values, step, to_workers):
        pairs = []
        for group in range(self.fsdp):
            for place in range(self.seq):
                target = (place + step) % self.seq
                worker = target if to_workers else place
                if self.works(group, worker):
                    pairs.append((group * self.seq + place, group * self.seq + target))
        return lax.ppermute(values, AXES, pairs)

    def clip_at(self, place):
        return jnp.clip(place - self.first, 0, self.clips - 1)

    def collect(self, values, steps):
        pieces = {}
        for step in steps:
            target = (self.here + step) % self.seq
            sent = lax.dynamic_index_in_dim(values, self.clip_at(target), 0, keepdims=False)
            if step == 0:
                active = (self.here >= self.first) & (self.here < self.first + self.clips)
                pieces[step] = jnp.where(active, sent, jnp.zeros_like(sent))
            else:
                pieces[step] = self.turn(sent, step, True)
        return pieces

    def hand_back(self, rows):
        parts = rows.reshape(self.seq, -1, rows.shape[1])
        moved = lax.all_to_all(parts, "seq", split_axis=0, concat_axis=0, tiled=True)
        return lax.dynamic_slice_in_dim(moved, self.first, self.clips, 0)

    def chain(self, values, links):
        pairs = [
            (group * self.seq + a, group * self.seq + b)
            for group in range(self.fsdp)
            for a, b in links
        ]
        return lax.ppermute(values, AXES, pairs)

    def flip(self, values, bits):
        return lax.ppermute(values, "fsdp", [(f, f ^ bits) for f in range(self.fsdp)])

    def spread_far(self, shard, by_x, by_y):
        half = shard.shape[0] // 2
        return self.flip(by_y[:half], 2), self.flip(by_x[half:], 4)

    def spread_core(self, shard, by_x, by_y, far_x, far_y):
        mine = jnp.stack([shard, by_x, by_y, jnp.concatenate([far_x, far_y], axis=0)])
        return mine, self.flip(mine, 1)

    def fold_core(self, *members):
        core = self.group % 2
        parts = [m.reshape(4, 2, m.shape[0] // 8, m.shape[1]) for m in members]
        sent = jnp.concatenate([pick(p, 1 - core, 1) for p in parts], axis=2)
        kept = jnp.concatenate([pick(p, core, 1) for p in parts], axis=2)
        return kept, self.flip(sent, 1)

    def fold_chips(self, kept, arrived):
        sums = plus(kept, arrived)
        chip = self.group // 2
        moved = [self.flip(pick(sums, chip ^ bits, 0), 2 * bits) for bits in (1, 2, 3)]
        return pick(sums, chip, 0), moved

    def hop_one(self, values):
        return values, self.chain(values, ((0, 1), (3, 2)))

    def hop_two(self, values, arrived):
        half = plus(values, arrived)
        return half, self.chain(half, ((1, 2), (2, 1)))

    def hop_three(self, half, arrived):
        whole = plus(half, arrived)
        return whole, self.chain(whole, ((1, 0), (2, 3)))

    def hop_end(self, whole, back):
        return jnp.where((self.here == 0) | (self.here == 3), back, whole).astype(F32)

    def seq_sum(self, values):
        if self.seq != 4:
            return lax.psum(values, "seq").astype(F32)
        return self.hop_end(*self.hop_three(*self.hop_two(*self.hop_one(values))))


def pick(values, index, axis):
    return lax.dynamic_index_in_dim(values, index, axis, keepdims=False)


def plus(first, second):
    return (first.astype(F32) + second.astype(F32)).astype(first.dtype)


def plus_all(first, others):
    total = first.astype(F32)
    for other in others:
        total = total + other.astype(F32)
    return total.astype(first.dtype)


def tied(*members):
    return lax.optimization_barrier(members)


def place_kernel(parts, here_ref, *refs):
    count = len(refs) - len(parts)
    pieces, outs = refs[:count], refs[count:]

    def store(piece):
        for out, (low, high, padded) in zip(outs, parts):
            out[: high - low] = piece[low:high]
            if padded > high - low:
                out[high - low :] = jnp.zeros((padded - high + low, out.shape[1]), out.dtype)

    for step, piece in enumerate(pieces):
        pl.when(pl.program_id(0) == step)(functools.partial(store, piece))


def place(here, pieces, parts):
    count = len(pieces)
    rows, width = pieces[0].shape
    return pl.pallas_call(
        functools.partial(place_kernel, parts),
        grid_spec=pltpu.PrefetchScalarGridSpec(
            num_scalar_prefetch=1,
            grid=(count,),
            in_specs=[pl.BlockSpec((rows, width), lambda step, here: (0, 0))] * count,
            out_specs=[
                pl.BlockSpec((padded, width), lambda step, here: ((here[0] - step) % count, 0))
                for _, _, padded in parts
            ],
        ),
        out_shape=[
            jax.ShapeDtypeStruct((count * padded, width), BF) for _, _, padded in parts
        ],
        compiler_params=pltpu.CompilerParams(vmem_limit_bytes=24 << 20),
        cost_estimate=pl.CostEstimate(
            flops=0, transcendentals=0, bytes_accessed=4 * count * rows * width
        ),
        name="place",
    )(here.reshape(1), *pieces)


def assemble_kernel(widths, rows, group_ref, mine_ref, other_ref, *outs):
    flipped = group_ref[0] % 2

    def store(first_ref, second_ref):
        start = 0
        for out, width in zip(outs, widths):
            out[:rows] = first_ref[0, :, start : start + width]
            out[rows:] = second_ref[0, :, start : start + width]
            start += width

    pl.when(flipped == 0)(lambda: store(mine_ref, other_ref))
    pl.when(flipped == 1)(lambda: store(other_ref, mine_ref))


def assemble(group, mine, other, widths):
    rows, total = mine.shape[1], mine.shape[2]
    source = pl.BlockSpec((1, rows, total), lambda chip, group: (chip, 0, 0))
    return pl.pallas_call(
        functools.partial(assemble_kernel, widths, rows),
        grid_spec=pltpu.PrefetchScalarGridSpec(
            num_scalar_prefetch=1,
            grid=(4,),
            in_specs=[source, source],
            out_specs=[
                pl.BlockSpec((2 * rows, width), lambda chip, group: ((group[0] // 2) ^ chip, 0))
                for width in widths
            ],
        ),
        out_shape=[jax.ShapeDtypeStruct((8 * rows, width), BF) for width in widths],
        compiler_params=pltpu.CompilerParams(vmem_limit_bytes=16 << 20),
        cost_estimate=pl.CostEstimate(
            flops=0, transcendentals=0, bytes_accessed=32 * rows * total
        ),
        name="assemble",
    )(group.reshape(1), mine, other)


def local(
    mesh_shape,
    hidden_in,
    encoded,
    out_grad,
    norm_gain,
    norm_shift,
    biases,
    self_qkv,
    self_out,
    cross_q,
    cross_kv,
    cross_out,
    mlp_in,
    mlp_in_bias,
    mlp_out,
):
    clips, rows, width = hidden_in.shape
    frames = encoded.shape[1]
    padded = (frames + 15) // 16 * 16
    grid = Grid(mesh_shape["fsdp"], mesh_shape["seq"], clips)
    shard = norm_gain.shape[1]
    norms = norm_gain.shape[0]
    bias_count = biases.shape[0]
    scaling = HD ** (-0.5)
    swift = grid.fsdp == 8 and grid.seq == 4 and self_qkv.shape[0] >= 32

    def gathered(*members):
        widths = [member.shape[1] for member in members]
        joined = jnp.concatenate(members, axis=1)
        joined = lax.all_gather(joined, "fsdp", axis=0, tiled=True)
        return jnp.split(joined, np.cumsum(widths)[:-1].tolist(), axis=1)

    def scattered(member):
        return lax.psum_scatter(member, "fsdp", scatter_dimension=0, tiled=True)

    tokens_in = jnp.concatenate([hidden_in, encoded], axis=1)
    pieces = grid.collect(tokens_in, (0, 1, 3) if swift else range(grid.seq))
    small = jnp.concatenate([norm_gain, norm_shift, biases, mlp_in_bias.reshape(-1, shard)], axis=0)
    kinds = small.shape[0]
    shard_rows = self_qkv.shape[0]
    if swift:
        small = jnp.pad(small, ((0, shard_rows - kinds), (0, 0)))
        first_shard = jnp.concatenate([self_qkv, small], axis=1)
        first_widths = (self_qkv.shape[1], shard)
        first_x, first_y = grid.flip(first_shard, 2), grid.flip(first_shard, 4)
    full_self_out, full_cross_q, full_cross_kv = gathered(self_out, cross_q, cross_kv)
    full_cross_out, full_inner = gathered(cross_out, mlp_in)
    if swift:
        first_x, first_y, pieces[1], pieces[3], tokens_in = tied(
            first_x, first_y, pieces[1], pieces[3], tokens_in
        )
        pieces.update(grid.collect(tokens_in, (2,)))
        far_x, far_y = grid.spread_far(first_shard, first_x, first_y)
        far_x, far_y, pieces[2] = tied(far_x, far_y, pieces[2])
        mine, other = grid.spread_core(first_shard, first_x, first_y, far_x, far_y)
        other, mlp_out = tied(other, mlp_out)
        outer_x, outer_y = grid.flip(mlp_out, 2), grid.flip(mlp_out, 4)
        full_qkv, small = assemble(grid.group, mine, other, first_widths)
        small = small.reshape(grid.fsdp, shard_rows, shard)[:, :kinds]
    else:
        (full_qkv,) = gathered(self_qkv)
        small = lax.all_gather(small, "fsdp", axis=0)
        (full_outer,) = gathered(mlp_out)
    vectors = small[:, : 2 * norms + bias_count].swapaxes(0, 1).reshape(-1, width).astype(F32)
    gain, shift, bias = vectors[:norms], vectors[norms : 2 * norms], vectors[2 * norms :]
    inner_bias = small[:, 2 * norms + bias_count :].reshape(1, -1).astype(F32)
    none = jnp.zeros((width,), F32)

    token_rows, frame_rows = place(
        grid.here,
        [pieces[step] for step in range(grid.seq)],
        ((0, rows, rows), (rows, rows + frames, padded)),
    )
    residual_in = token_rows.astype(F32)
    normed_one = (normalized(residual_in)[0] * gain[0] + shift[0]).astype(BF)
    tokens = grid.seq * rows
    line = jnp.arange(tokens)
    places = (line[:, None], jnp.concatenate([line, line])[None, :])
    blocks = width // LANES

    qkv_bias = jnp.concatenate([bias[0], none, bias[1]])
    qkv_scale = jnp.concatenate([none + scaling, none + 1.0, none + 1.0])
    qkv = ((product(normed_one, full_qkv) + qkv_bias) * qkv_scale).astype(BF)
    self_sources = ((qkv, 0), (qkv, blocks), (qkv, 2 * blocks))
    self_mix, self_log = attend(self_sources, places, tokens, tokens, width)
    after_self = residual_in + product(self_mix, full_self_out) + bias[2]
    normed_two = (normalized(after_self)[0] * gain[1] + shift[1]).astype(BF)
    cross_queries = ((product(normed_two, full_cross_q) + bias[3]) * scaling).astype(BF)
    out_grad, cross_queries = tied(out_grad, cross_queries)
    top_pieces = list(grid.collect(out_grad, range(grid.seq)).values())
    kv_bias = jnp.concatenate([none, bias[4]])
    cross_pair = (product(frame_rows, full_cross_kv) + kv_bias).astype(BF)
    cross_sources = ((cross_queries, 0), (cross_pair, 0), (cross_pair, blocks))
    cross_mix, cross_log = attend(cross_sources, None, padded, frames, width)
    if swift:
        cross_mix, outer_x, outer_y, *top_pieces = tied(cross_mix, outer_x, outer_y, *top_pieces)
        far_x, far_y = grid.spread_far(mlp_out, outer_x, outer_y)
    (top,) = place(grid.here, top_pieces, ((0, rows, rows),))
    after_cross = after_self + product(cross_mix, full_cross_out) + bias[5]
    normed_three = (normalized(after_cross)[0] * gain[2] + shift[2]).astype(BF)
    inner = product(normed_three, full_inner) + inner_bias
    activated = gelu(inner).astype(BF)
    if swift:
        activated, far_x, far_y = tied(activated, far_x, far_y)
        mine, other = grid.spread_core(mlp_out, outer_x, outer_y, far_x, far_y)

    top_wide = top.astype(F32)
    grad_w_outer = weight_grad(activated, top)
    if swift:
        grad_w_outer, top, other = tied(grad_w_outer, top, other)
        (full_outer,) = assemble(grid.group, mine, other, (mlp_out.shape[1],))
    part_outer = scattered(grad_w_outer)
    grad_bias_six = jnp.sum(top_wide, axis=0)
    grad_inner = product_back(top, full_outer) * gelu_slope(inner)
    grad_inner_low = grad_inner.astype(BF)
    grad_w_inner = weight_grad(normed_three, grad_inner_low)
    grad_w_inner, grad_inner_low = tied(grad_w_inner, grad_inner_low)
    part_inner = scattered(grad_w_inner)
    grad_inner_bias = jnp.sum(grad_inner, axis=0)
    grad_normed_three = product_back(grad_inner_low, full_inner)
    from_three, gain_three, shift_three = norm_back(grad_normed_three, after_cross, gain[2])
    grad_after_cross = top_wide + from_three
    grad_cross_low = grad_after_cross.astype(BF)
    grad_bias_five = jnp.sum(grad_after_cross, axis=0)
    grad_w_cross_out = weight_grad(cross_mix, grad_cross_low)
    grad_cross_mix = product_back(grad_cross_low, full_cross_out).astype(BF)

    cross_back = functools.partial(
        attend_back,
        cross_sources,
        cross_mix,
        logs=cross_log,
        places=None,
        chunk=padded,
        valid=frames,
        width=width,
        parts=2,
    )
    first_part = cross_back(grads=grad_cross_mix)
    if swift:
        grad_cross_mix, part_outer, *first_part = tied(grad_cross_mix, part_outer, *first_part)
        outer_sum, outer_in = grid.hop_one(part_outer)
    grad_cross_queries, grad_pair = cross_back(
        grads=grad_cross_mix, part=1, before=tuple(first_part)
    )
    if swift:
        grad_cross_queries, grad_pair, outer_in = tied(grad_cross_queries, grad_pair, outer_in)
        outer_sum, outer_in = grid.hop_two(outer_sum, outer_in)
    grad_frames = product_back(grad_pair, full_cross_kv).astype(BF)
    grad_frames, grad_pair = tied(grad_frames, grad_pair)
    grad_encoded = grid.hand_back(grad_frames)
    grad_w_cross_kv = weight_grad(frame_rows, grad_pair)
    if swift:
        grad_w_cross_kv, grad_cross_queries, outer_in = tied(
            grad_w_cross_kv, grad_cross_queries, outer_in
        )
        outer_sum, outer_in = grid.hop_three(outer_sum, outer_in)
    part_kv = scattered(grad_w_cross_kv)
    grad_bias_four = jnp.sum(grad_pair[:, width:].astype(F32), axis=0)
    grad_w_cross_q = weight_grad(normed_two, grad_cross_queries)
    grad_bias_three = jnp.sum(grad_cross_queries.astype(F32), axis=0)
    grad_normed_two = product_back(grad_cross_queries, full_cross_q)
    from_two, gain_two, shift_two = norm_back(grad_normed_two, after_self, gain[1])
    grad_after_self = grad_after_cross + from_two
    grad_self_low = grad_after_self.astype(BF)
    grad_w_self_out = weight_grad(self_mix, grad_self_low)
    grad_bias_two = jnp.sum(grad_after_self, axis=0)
    grad_self_mix = product_back(grad_self_low, full_self_out).astype(BF)
    middle = [grad_w_cross_out, grad_w_cross_q, grad_w_self_out]
    if swift:
        grad_self_mix, *middle = tied(grad_self_mix, *middle)
        middle_kept, middle_core = grid.fold_core(*middle)
    (grad_pre,) = attend_back(
        self_sources, self_mix, grad_self_mix, self_log, places, tokens, tokens, width
    )
    if swift:
        grad_pre, middle_core, part_inner = tied(grad_pre, middle_core, part_inner)
        middle_own, middle_near = grid.fold_chips(middle_kept, middle_core)
        inner_sum, inner_in = grid.hop_one(part_inner)
    grad_normed_one = product_back(grad_pre, full_qkv)
    grad_w_qkv = weight_grad(normed_one, grad_pre)
    pre_sums = jnp.sum(grad_pre.astype(F32), axis=0)
    from_one, gain_one, shift_one = norm_back(grad_normed_one, residual_in, gain[0])
    grad_rows = (grad_after_self + from_one).astype(BF)

    sums = jnp.stack(
        [
            gain_one,
            gain_two,
            gain_three,
            shift_one,
            shift_two,
            shift_three,
            pre_sums[:width],
            pre_sums[2 * width :],
            grad_bias_two,
            grad_bias_three,
            grad_bias_four,
            grad_bias_five,
            grad_bias_six,
        ]
    )
    inner_sums = grad_inner_bias.reshape(grid.fsdp, -1, shard)
    packed = jnp.concatenate(
        [sums.reshape(-1, grid.fsdp, shard).swapaxes(0, 1), inner_sums], axis=1
    )
    if swift:
        packed = jnp.pad(packed.astype(BF), ((0, 0), (0, shard_rows - kinds), (0, 0)))
        packed = packed.reshape(-1, shard)
        last_kept, last_core = grid.fold_core(grad_w_qkv, packed)
        last_kept, activated, grad_rows = tied(last_kept, activated, grad_rows)
    hidden_rows = (after_cross + product(activated, full_outer) + bias[6]).astype(BF)
    leaving = jnp.concatenate(
        [
            grad_rows.reshape(grid.seq, rows, width),
            hidden_rows.reshape(grid.seq, rows, width),
        ],
        axis=1,
    ).reshape(-1, width)
    if swift:
        last_core, leaving = tied(last_core, leaving)
        last_own, last_near = grid.fold_chips(last_kept, last_core)
        inner_sum, inner_in = grid.hop_two(inner_sum, inner_in)
    leaving = grid.hand_back(leaving)
    if swift:
        part_middle = jnp.concatenate([plus_all(middle_own, middle_near), part_kv], axis=1)
        middle_sum, middle_in = grid.hop_one(part_middle)
        middle_in, inner_in, outer_in, grad_encoded, *last_near = tied(
            middle_in, inner_in, outer_in, grad_encoded, *last_near
        )
        part_last = plus_all(last_own, last_near)
        half = 12 * LANES
        last_one, one_in = grid.hop_one(part_last[:, :half])
        last_two, two_in = grid.hop_one(part_last[:, half:])
        inner_sum, inner_in = grid.hop_three(inner_sum, inner_in)
        middle_sum, middle_in = grid.hop_two(middle_sum, middle_in)
        total_outer = grid.hop_end(outer_sum, outer_in)
        last_one, one_in = grid.hop_two(last_one, one_in)
        last_two, two_in = grid.hop_two(last_two, two_in)
        middle_sum, middle_in = grid.hop_three(middle_sum, middle_in)
        total_inner = grid.hop_end(inner_sum, inner_in)
        last_one, one_in = grid.hop_three(last_one, one_in)
        last_two, two_in = grid.hop_three(last_two, two_in)
        total_middle = grid.hop_end(middle_sum, middle_in)
        total_last = jnp.concatenate(
            [grid.hop_end(last_one, one_in), grid.hop_end(last_two, two_in)], axis=1
        )
        total_qkv = total_last[:, : grad_w_qkv.shape[1]]
        mine = total_last[:kinds, grad_w_qkv.shape[1] :]
    else:
        part_middle = jnp.concatenate(
            [scattered(jnp.concatenate(middle, axis=1)), part_kv], axis=1
        )
        total_outer = grid.seq_sum(part_outer)
        total_inner = grid.seq_sum(part_inner)
        total_middle = grid.seq_sum(part_middle)
        total_qkv = grid.seq_sum(scattered(grad_w_qkv))
        mine = pick(lax.psum(packed, AXES), grid.group, 0)
    total_cross_out, total_cross_q, total_self_out, total_cross_kv = jnp.split(
        total_middle, (width, 2 * width, 3 * width), axis=1
    )

    grad_encoded = grad_encoded[:, :frames]
    grad_hidden_in, hidden_out = leaving[:, :rows], leaving[:, rows:]
    return (
        hidden_out,
        grad_hidden_in,
        grad_encoded,
        mine[:norms],
        mine[norms : 2 * norms],
        mine[2 * norms : 2 * norms + bias_count],
        total_qkv,
        total_self_out,
        total_cross_q,
        total_cross_kv,
        total_cross_out,
        total_inner,
        mine[2 * norms + bias_count :].reshape(-1),
        total_outer,
    )


def solution(mesh):
    rows = P("fsdp", "seq", None)
    wide = P(None, "fsdp")
    tall = P("fsdp", None)
    in_specs = (rows,) * 3 + (wide,) * 3 + (tall,) * 6 + (P("fsdp"), tall)
    out_specs = (rows,) * 3 + (wide,) * 3 + (tall,) * 6 + (P("fsdp"), tall)
    return jax.shard_map(
        functools.partial(local, dict(mesh.shape)),
        mesh=mesh,
        in_specs=in_specs,
        out_specs=out_specs,
        check_vma=False,
    )
```

```python
import functools

import jax
import jax.numpy as jnp
import numpy as np
from jax import lax
from jax.experimental import pallas as pl
from jax.experimental.pallas import tpu as pltpu
from jax.sharding import PartitionSpec as P

HD = 64
LANES = 128
NORM_EPSILON = 1e-05
LOW = -1e30
F32 = jnp.float32
BF = jnp.bfloat16
AXES = ("fsdp", "seq")


def two_heads(rows):
    lane = lax.broadcasted_iota(jnp.int32, rows.shape, 1)
    zero = jnp.zeros_like(rows)
    return jnp.concatenate(
        [jnp.where(lane < HD, rows, zero), jnp.where(lane >= HD, rows, zero)], axis=0
    )


def one_row(stacked):
    count = stacked.shape[0] // 2
    lane = lax.broadcasted_iota(jnp.int32, (count, stacked.shape[1]), 1)
    return jnp.where(lane < HD, stacked[:count], stacked[count:])


def over_rows(first, second):
    return lax.dot_general(first, second, (((0,), (0,)), ((), ())), preferred_element_type=F32)


def over_lanes(first, second):
    return lax.dot_general(first, second, (((1,), (1,)), ((), ())), preferred_element_type=F32)


def chunk_scores(keys, queries, places, step):
    scores = over_lanes(keys, queries)
    if places is not None:
        key_ref, query_ref = places
        rows = slice(step * keys.shape[0], (step + 1) * keys.shape[0])
        scores = jnp.where(key_ref[rows] <= query_ref[...], scores, LOW)
    return scores


def tail_kept(values, valid, other):
    size = values.shape[0]
    if valid == size:
        return values
    first = valid // 8 * 8
    row = lax.broadcasted_iota(jnp.int32, (size - first, values.shape[1]), 0)
    tail = jnp.where(row < valid - first, values[first:], other)
    return jnp.concatenate([values[:first], tail], axis=0)


def forward_kernel(chunk, valid, causal, *refs):
    q_ref, k_ref, v_ref = refs[:3]
    places = refs[3:5] if causal else None
    o_ref, log_ref, s_ref = refs[-3:]
    queries = two_heads(q_ref[...])
    width = queries.shape[0]
    strips = [slice(low, low + chunk) for low in range(0, k_ref.shape[0], chunk)]
    top = jnp.full((1, width), LOW, F32)
    for step, rows in enumerate(strips):
        scores = tail_kept(chunk_scores(k_ref[rows], queries, places, step), valid, LOW)
        s_ref[rows] = scores
        top = jnp.maximum(top, jnp.max(scores, axis=0, keepdims=True))
    total, mixed = jnp.zeros((1, width), F32), jnp.zeros((LANES, width), F32)
    for rows in strips:
        raised = jnp.exp(s_ref[rows] - top)
        total = total + jnp.sum(raised, axis=0, keepdims=True)
        mixed = mixed + over_rows(v_ref[rows], raised.astype(BF))
    o_ref[...] = one_row(jnp.transpose(mixed / total)).astype(BF)
    log_ref[...] = (top + jnp.log(total))[None]


def pair_back(chunk, valid, places, refs, store_key, store_value):
    q_ref, k_ref, v_ref, o_ref, g_ref, log_ref = refs
    queries = two_heads(q_ref[...])
    grads = two_heads(g_ref[...])
    mixed = o_ref[...].astype(F32)
    product = grads.astype(F32) * jnp.concatenate([mixed, mixed], axis=0)
    row_dot = jnp.sum(jnp.transpose(product), axis=0, keepdims=True)
    log_total = log_ref[0]
    grad_queries = jnp.zeros((LANES, queries.shape[0]), F32)
    for step, low in enumerate(range(0, k_ref.shape[0], chunk)):
        rows = slice(low, low + chunk)
        keys = k_ref[rows]
        scores = chunk_scores(keys, queries, places, step)
        weights = jnp.exp(tail_kept(scores, valid, LOW) - log_total)
        grad_weights = over_lanes(v_ref[rows], grads)
        grad_scores = (weights * (grad_weights - row_dot)).astype(BF)
        store_value(rows, jnp.dot(weights.astype(BF), grads, preferred_element_type=F32))
        store_key(rows, jnp.dot(grad_scores, queries, preferred_element_type=F32))
        grad_queries = grad_queries + over_rows(keys, grad_scores)
    return one_row(jnp.transpose(grad_queries)).astype(BF) * BF(HD**-0.5)


def joint_stores(joint_ref, width, first):
    def lanes(part):
        start = (part + first) * width + pl.program_id(0) * LANES
        return pl.ds(pl.multiple_of(start, LANES), LANES)

    def store_key(rows, part):
        joint_ref[rows, lanes(0)] = part.astype(BF)

    def store_value(rows, part):
        joint_ref[rows, lanes(1)] = part.astype(BF)

    return lanes, store_key, store_value


def cross_back_kernel(chunk, valid, width, *refs):
    gq_ref, joint_ref = refs[-2:]
    _, store_key, store_value = joint_stores(joint_ref, width, 0)
    gq_ref[...] = pair_back(chunk, valid, None, refs[:6], store_key, store_value)


def causal_back_kernel(chunk, width, *refs):
    joint_ref = refs[-1]
    lanes, store_key, store_value = joint_stores(joint_ref, width, 1)
    joint_ref[:, lanes(-1)] = pair_back(
        chunk, chunk, refs[6:8], refs[:6], store_key, store_value
    )


def columns(rows, first=0):
    return pl.BlockSpec((rows, LANES), lambda pair, *phase: (0, pair + first))


def place_specs(keys, tokens):
    return [
        pl.BlockSpec((keys, 1), lambda pair, *phase: (0, 0)),
        pl.BlockSpec((1, 2 * tokens), lambda pair, *phase: (0, 0)),
    ]


def log_spec(tokens, first=0):
    return pl.BlockSpec((1, 1, 2 * tokens), lambda pair, *phase: (pair + first, 0, 0))


def attend(sources, places, chunk, valid, width):
    tokens, count = sources[0][0].shape[0], sources[1][0].shape[0]
    causal = places is not None
    pairs = width // LANES
    specs = [columns(member.shape[0], first) for member, first in sources]
    operands = [member for member, _ in sources]
    if causal:
        specs += place_specs(count, tokens)
        operands += list(places)
    return pl.pallas_call(
        functools.partial(forward_kernel, chunk, valid, causal),
        grid=(pairs,),
        in_specs=specs,
        out_specs=[columns(tokens), log_spec(tokens)],
        out_shape=[
            jax.ShapeDtypeStruct((tokens, width), BF),
            jax.ShapeDtypeStruct((pairs, 1, 2 * tokens), F32),
        ],
        scratch_shapes=[pltpu.VMEM((count, 2 * tokens), F32)],
        compiler_params=pltpu.CompilerParams(vmem_limit_bytes=32 << 20),
        cost_estimate=pl.CostEstimate(
            flops=16 * tokens * count * width,
            transcendentals=tokens * count * width // HD,
            bytes_accessed=4 * (tokens + count) * width,
        ),
        name="attend_causal" if causal else "attend_cross",
    )(*operands)


def attend_back(sources, mixed, grads, logs, places, chunk, valid, width):
    tokens, count = sources[0][0].shape[0], sources[1][0].shape[0]
    causal = places is not None
    pairs = width // LANES
    specs = [columns(member.shape[0], first) for member, first in sources]
    specs += [columns(tokens), columns(tokens), log_spec(tokens)]
    operands = [member for member, _ in sources] + [mixed, grads, logs]
    parts = 3 if causal else 2
    out_specs = [pl.BlockSpec((count, parts * width), lambda pair: (0, 0))]
    out_shape = [jax.ShapeDtypeStruct((count, parts * width), BF)]
    if causal:
        specs += place_specs(count, tokens)
        operands += list(places)
        kernel = functools.partial(causal_back_kernel, chunk, width)
    else:
        kernel = functools.partial(cross_back_kernel, chunk, valid, width)
        out_specs = [columns(tokens)] + out_specs
        out_shape = [jax.ShapeDtypeStruct((tokens, width), BF)] + out_shape
    return pl.pallas_call(
        kernel,
        grid=(pairs,),
        in_specs=specs,
        out_specs=out_specs,
        out_shape=out_shape,
        compiler_params=pltpu.CompilerParams(vmem_limit_bytes=40 << 20),
        cost_estimate=pl.CostEstimate(
            flops=40 * tokens * count * width,
            transcendentals=tokens * count * width // HD,
            bytes_accessed=8 * (tokens + count) * width,
        ),
        name="attend_causal_back" if causal else "attend_cross_back",
    )(*operands)


def product(first, second):
    return jnp.dot(first, second, preferred_element_type=F32)


def product_back(incoming, weight):
    return lax.dot_general(
        incoming, weight, (((1,), (1,)), ((), ())), preferred_element_type=F32
    )


def weight_grad(operand, incoming):
    return lax.dot_general(
        operand, incoming, (((0,), (0,)), ((), ())), preferred_element_type=F32
    ).astype(BF)


def normalized(values):
    average = jnp.mean(values, axis=-1, keepdims=True)
    centred = values - average
    variance = jnp.mean(centred * centred, axis=-1, keepdims=True)
    inverse = lax.rsqrt(variance + NORM_EPSILON)
    return centred * inverse, inverse


def norm_back(incoming, values, gain_row):
    rows, inverse = normalized(values)
    scaled = incoming * gain_row
    average = jnp.mean(scaled, axis=-1, keepdims=True)
    aligned = jnp.mean(scaled * rows, axis=-1, keepdims=True)
    gain_grad = jnp.sum(incoming * rows, axis=0)
    shift_grad = jnp.sum(incoming, axis=0)
    return (scaled - average - rows * aligned) * inverse, gain_grad, shift_grad


def gelu(values):
    return values * (1.0 + lax.erf(values * (0.5**0.5))) * 0.5


def gelu_slope(values):
    return (1.0 + lax.erf(values * (0.5**0.5))) * 0.5 + values * jnp.exp(
        -0.5 * values * values
    ) * (0.5 / jnp.pi) ** 0.5


class Grid:
    def __init__(self, fsdp, seq, clips):
        self.fsdp, self.seq, self.clips = fsdp, seq, clips
        self.here = lax.axis_index("seq")
        self.group = lax.axis_index("fsdp")
        self.first = self.first_of(self.group)

    def first_of(self, group):
        return (group % 2) * (self.seq - self.clips)

    def works(self, group, place):
        return 0 <= place - self.first_of(group) < self.clips

    def turn(self, values, step, to_workers):
        pairs = []
        for group in range(self.fsdp):
            for place in range(self.seq):
                target = (place + step) % self.seq
                worker = target if to_workers else place
                if self.works(group, worker):
                    pairs.append((group * self.seq + place, group * self.seq + target))
        return lax.ppermute(values, AXES, pairs)

    def clip_at(self, place):
        return jnp.clip(place - self.first, 0, self.clips - 1)

    def collect(self, values, steps):
        pieces = {}
        for step in steps:
            target = (self.here + step) % self.seq
            sent = lax.dynamic_index_in_dim(values, self.clip_at(target), 0, keepdims=False)
            if step == 0:
                active = (self.here >= self.first) & (self.here < self.first + self.clips)
                pieces[step] = jnp.where(active, sent, jnp.zeros_like(sent))
            else:
                pieces[step] = self.turn(sent, step, True)
        return pieces

    def hand_back(self, rows):
        parts = rows.reshape(self.seq, -1, rows.shape[1])
        moved = lax.all_to_all(parts, "seq", split_axis=0, concat_axis=0, tiled=True)
        return lax.dynamic_slice_in_dim(moved, self.first, self.clips, 0)

    def chain(self, values, links):
        pairs = [
            (group * self.seq + a, group * self.seq + b)
            for group in range(self.fsdp)
            for a, b in links
        ]
        return lax.ppermute(values, AXES, pairs)

    def flip(self, values, bits):
        return lax.ppermute(values, "fsdp", [(f, f ^ bits) for f in range(self.fsdp)])

    def spread_far(self, shard, by_x, by_y):
        half = shard.shape[0] // 2
        return self.flip(by_y[:half], 2), self.flip(by_x[half:], 4)

    def spread_core(self, shard, by_x, by_y, far_x, far_y):
        mine = jnp.stack([shard, by_x, by_y, jnp.concatenate([far_x, far_y], axis=0)])
        return mine, self.flip(mine, 1)

    def fold_core(self, *members):
        core = self.group % 2
        parts = [m.reshape(4, 2, m.shape[0] // 8, m.shape[1]) for m in members]
        sent = jnp.concatenate([pick(p, 1 - core, 1) for p in parts], axis=2)
        kept = jnp.concatenate([pick(p, core, 1) for p in parts], axis=2)
        return kept, self.flip(sent, 1)

    def fold_chips(self, kept, arrived):
        sums = plus(kept, arrived)
        chip = self.group // 2
        moved = [self.flip(pick(sums, chip ^ bits, 0), 2 * bits) for bits in (1, 2, 3)]
        return pick(sums, chip, 0), moved

    def hop_one(self, values):
        return values, self.chain(values, ((0, 1), (3, 2)))

    def hop_two(self, values, arrived):
        half = plus(values, arrived)
        return half, self.chain(half, ((1, 2), (2, 1)))

    def hop_three(self, half, arrived):
        whole = plus(half, arrived)
        return whole, self.chain(whole, ((1, 0), (2, 3)))

    def hop_end(self, whole, back):
        return jnp.where((self.here == 0) | (self.here == 3), back, whole).astype(F32)

    def seq_sum(self, values):
        if self.seq != 4:
            return lax.psum(values, "seq").astype(F32)
        return self.hop_end(*self.hop_three(*self.hop_two(*self.hop_one(values))))


def pick(values, index, axis):
    return lax.dynamic_index_in_dim(values, index, axis, keepdims=False)


def plus(first, second):
    return (first.astype(F32) + second.astype(F32)).astype(first.dtype)


def plus_all(first, others):
    total = first.astype(F32)
    for other in others:
        total = total + other.astype(F32)
    return total.astype(first.dtype)


def tied(*members):
    return lax.optimization_barrier(members)


def join_kernel(*refs):
    start = 0
    for member in refs[:-1]:
        refs[-1][:, start : start + member.shape[1]] = member[...]
        start += member.shape[1]


def join(*members):
    rows, step = members[0].shape[0], 128
    widths = [member.shape[1] for member in members]

    def strip(width):
        return pl.BlockSpec((step, width), lambda i: (i, 0))

    return pl.pallas_call(
        join_kernel,
        grid=(rows // step,),
        in_specs=[strip(width) for width in widths],
        out_specs=strip(sum(widths)),
        out_shape=jax.ShapeDtypeStruct((rows, sum(widths)), BF),
        compiler_params=pltpu.CompilerParams(vmem_limit_bytes=16 << 20),
        cost_estimate=pl.CostEstimate(
            flops=0, transcendentals=0, bytes_accessed=4 * rows * sum(widths)
        ),
        name="join",
    )(*members)


def place_kernel(parts, here_ref, *refs):
    count = len(refs) - len(parts)
    pieces, outs = refs[:count], refs[count:]

    def store(piece):
        for out, (low, high, padded) in zip(outs, parts):
            out[: high - low] = piece[low:high]
            if padded > high - low:
                out[high - low :] = jnp.zeros((padded - high + low, out.shape[1]), out.dtype)

    for step, piece in enumerate(pieces):
        pl.when(pl.program_id(0) == step)(functools.partial(store, piece))


def place(here, pieces, parts):
    count = len(pieces)
    rows, width = pieces[0].shape
    return pl.pallas_call(
        functools.partial(place_kernel, parts),
        grid_spec=pltpu.PrefetchScalarGridSpec(
            num_scalar_prefetch=1,
            grid=(count,),
            in_specs=[pl.BlockSpec((rows, width), lambda step, here: (0, 0))] * count,
            out_specs=[
                pl.BlockSpec((padded, width), lambda step, here: ((here[0] - step) % count, 0))
                for _, _, padded in parts
            ],
        ),
        out_shape=[
            jax.ShapeDtypeStruct((count * padded, width), BF) for _, _, padded in parts
        ],
        compiler_params=pltpu.CompilerParams(vmem_limit_bytes=24 << 20),
        cost_estimate=pl.CostEstimate(
            flops=0, transcendentals=0, bytes_accessed=4 * count * rows * width
        ),
        name="place",
    )(here.reshape(1), *pieces)


def assemble_kernel(widths, rows, group_ref, mine_ref, other_ref, *outs):
    flipped = group_ref[0] % 2

    def store(first_ref, second_ref):
        start = 0
        for out, width in zip(outs, widths):
            out[:rows] = first_ref[0, :, start : start + width]
            out[rows:] = second_ref[0, :, start : start + width]
            start += width

    pl.when(flipped == 0)(lambda: store(mine_ref, other_ref))
    pl.when(flipped == 1)(lambda: store(other_ref, mine_ref))


def assemble(group, mine, other, widths):
    rows, total = mine.shape[1], mine.shape[2]
    source = pl.BlockSpec((1, rows, total), lambda chip, group: (chip, 0, 0))
    return pl.pallas_call(
        functools.partial(assemble_kernel, widths, rows),
        grid_spec=pltpu.PrefetchScalarGridSpec(
            num_scalar_prefetch=1,
            grid=(4,),
            in_specs=[source, source],
            out_specs=[
                pl.BlockSpec((2 * rows, width), lambda chip, group: ((group[0] // 2) ^ chip, 0))
                for width in widths
            ],
        ),
        out_shape=[jax.ShapeDtypeStruct((8 * rows, width), BF) for width in widths],
        compiler_params=pltpu.CompilerParams(vmem_limit_bytes=16 << 20),
        cost_estimate=pl.CostEstimate(
            flops=0, transcendentals=0, bytes_accessed=32 * rows * total
        ),
        name="assemble",
    )(group.reshape(1), mine, other)


def local(
    mesh_shape,
    hidden_in,
    encoded,
    out_grad,
    norm_gain,
    norm_shift,
    biases,
    self_qkv,
    self_out,
    cross_q,
    cross_kv,
    cross_out,
    mlp_in,
    mlp_in_bias,
    mlp_out,
):
    clips, rows, width = hidden_in.shape
    frames = encoded.shape[1]
    padded = (frames + 15) // 16 * 16
    grid = Grid(mesh_shape["fsdp"], mesh_shape["seq"], clips)
    shard = norm_gain.shape[1]
    norms = norm_gain.shape[0]
    bias_count = biases.shape[0]
    scaling = HD ** (-0.5)
    swift = grid.fsdp == 8 and grid.seq == 4 and self_qkv.shape[0] >= 32

    def gathered(*members):
        widths = [member.shape[1] for member in members]
        joined = jnp.concatenate(members, axis=1)
        joined = lax.all_gather(joined, "fsdp", axis=0, tiled=True)
        return jnp.split(joined, np.cumsum(widths)[:-1].tolist(), axis=1)

    def scattered(member):
        return lax.psum_scatter(member, "fsdp", scatter_dimension=0, tiled=True)

    tokens_in = jnp.concatenate([hidden_in, encoded], axis=1)
    pieces = grid.collect(tokens_in, (0, 1, 3) if swift else range(grid.seq))
    small = jnp.concatenate([norm_gain, norm_shift, biases, mlp_in_bias.reshape(-1, shard)], axis=0)
    kinds = small.shape[0]
    shard_rows = self_qkv.shape[0]
    if swift:
        small = jnp.pad(small, ((0, shard_rows - kinds), (0, 0)))
        first_shard = jnp.concatenate([self_qkv, small], axis=1)
        first_widths = (self_qkv.shape[1], shard)
        first_x, first_y = grid.flip(first_shard, 2), grid.flip(first_shard, 4)
    full_self_out, full_cross_q, full_cross_kv = gathered(self_out, cross_q, cross_kv)
    full_cross_out, full_inner = gathered(cross_out, mlp_in)
    if swift:
        first_x, first_y, pieces[1], pieces[3], tokens_in = tied(
            first_x, first_y, pieces[1], pieces[3], tokens_in
        )
        pieces.update(grid.collect(tokens_in, (2,)))
        far_x, far_y = grid.spread_far(first_shard, first_x, first_y)
        far_x, far_y, pieces[2] = tied(far_x, far_y, pieces[2])
        mine, other = grid.spread_core(first_shard, first_x, first_y, far_x, far_y)
        other, mlp_out = tied(other, mlp_out)
        outer_x, outer_y = grid.flip(mlp_out, 2), grid.flip(mlp_out, 4)
        full_qkv, small = assemble(grid.group, mine, other, first_widths)
        small = small.reshape(grid.fsdp, shard_rows, shard)[:, :kinds]
    else:
        (full_qkv,) = gathered(self_qkv)
        small = lax.all_gather(small, "fsdp", axis=0)
        (full_outer,) = gathered(mlp_out)
    vectors = small[:, : 2 * norms + bias_count].swapaxes(0, 1).reshape(-1, width).astype(F32)
    gain, shift, bias = vectors[:norms], vectors[norms : 2 * norms], vectors[2 * norms :]
    inner_bias = small[:, 2 * norms + bias_count :].reshape(1, -1).astype(F32)
    none = jnp.zeros((width,), F32)

    token_rows, frame_rows = place(
        grid.here,
        [pieces[step] for step in range(grid.seq)],
        ((0, rows, rows), (rows, rows + frames, padded)),
    )
    residual_in = token_rows.astype(F32)
    normed_one = (normalized(residual_in)[0] * gain[0] + shift[0]).astype(BF)
    tokens = grid.seq * rows
    line = jnp.arange(tokens)
    places = (line[:, None], jnp.concatenate([line, line])[None, :])
    blocks = width // LANES

    qkv_bias = jnp.concatenate([bias[0], none, bias[1]])
    qkv_scale = jnp.concatenate([none + scaling, none + 1.0, none + 1.0])
    qkv = ((product(normed_one, full_qkv) + qkv_bias) * qkv_scale).astype(BF)
    self_sources = ((qkv, 0), (qkv, blocks), (qkv, 2 * blocks))
    self_mix, self_log = attend(self_sources, places, tokens, tokens, width)
    after_self = residual_in + product(self_mix, full_self_out) + bias[2]
    normed_two = (normalized(after_self)[0] * gain[1] + shift[1]).astype(BF)
    cross_queries = ((product(normed_two, full_cross_q) + bias[3]) * scaling).astype(BF)
    out_grad, cross_queries = tied(out_grad, cross_queries)
    top_pieces = list(grid.collect(out_grad, range(grid.seq)).values())
    kv_bias = jnp.concatenate([none, bias[4]])
    cross_pair = (product(frame_rows, full_cross_kv) + kv_bias).astype(BF)
    cross_sources = ((cross_queries, 0), (cross_pair, 0), (cross_pair, blocks))
    cross_mix, cross_log = attend(cross_sources, None, padded, frames, width)
    if swift:
        cross_mix, outer_x, outer_y, *top_pieces = tied(cross_mix, outer_x, outer_y, *top_pieces)
        far_x, far_y = grid.spread_far(mlp_out, outer_x, outer_y)
    (top,) = place(grid.here, top_pieces, ((0, rows, rows),))
    after_cross = after_self + product(cross_mix, full_cross_out) + bias[5]
    normed_three = (normalized(after_cross)[0] * gain[2] + shift[2]).astype(BF)
    inner = product(normed_three, full_inner) + inner_bias
    activated = gelu(inner).astype(BF)
    if swift:
        activated, far_x, far_y = tied(activated, far_x, far_y)
        mine, other = grid.spread_core(mlp_out, outer_x, outer_y, far_x, far_y)

    top_wide = top.astype(F32)
    grad_w_outer = weight_grad(activated, top)
    if swift:
        grad_w_outer, top, other = tied(grad_w_outer, top, other)
        (full_outer,) = assemble(grid.group, mine, other, (mlp_out.shape[1],))
    part_outer = scattered(grad_w_outer)
    grad_bias_six = jnp.sum(top_wide, axis=0)
    grad_inner = product_back(top, full_outer) * gelu_slope(inner)
    grad_inner_low = grad_inner.astype(BF)
    grad_w_inner = weight_grad(normed_three, grad_inner_low)
    grad_w_inner, grad_inner_low = tied(grad_w_inner, grad_inner_low)
    part_inner = scattered(grad_w_inner)
    grad_inner_bias = jnp.sum(grad_inner, axis=0)
    grad_normed_three = product_back(grad_inner_low, full_inner)
    from_three, gain_three, shift_three = norm_back(grad_normed_three, after_cross, gain[2])
    grad_after_cross = top_wide + from_three
    grad_cross_low = grad_after_cross.astype(BF)
    grad_bias_five = jnp.sum(grad_after_cross, axis=0)
    grad_w_cross_out = weight_grad(cross_mix, grad_cross_low)
    grad_cross_mix = product_back(grad_cross_low, full_cross_out).astype(BF)

    grad_cross_queries, grad_pair = attend_back(
        cross_sources, cross_mix, grad_cross_mix, cross_log, None, padded, frames, width
    )
    if swift:
        part_outer, grad_cross_queries, grad_pair = tied(
            part_outer, grad_cross_queries, grad_pair
        )
        outer_sum, outer_in = grid.hop_one(part_outer)
    grad_frames = product_back(grad_pair, full_cross_kv).astype(BF)
    grad_frames, grad_pair = tied(grad_frames, grad_pair)
    grad_encoded = grid.hand_back(grad_frames)
    grad_w_cross_kv = weight_grad(frame_rows, grad_pair)
    if swift:
        grad_w_cross_kv, grad_cross_queries, outer_in = tied(
            grad_w_cross_kv, grad_cross_queries, outer_in
        )
        outer_sum, outer_in = grid.hop_two(outer_sum, outer_in)
    grad_bias_four = jnp.sum(grad_pair[:, width:].astype(F32), axis=0)
    grad_w_cross_q = weight_grad(normed_two, grad_cross_queries)
    grad_bias_three = jnp.sum(grad_cross_queries.astype(F32), axis=0)
    grad_normed_two = product_back(grad_cross_queries, full_cross_q)
    from_two, gain_two, shift_two = norm_back(grad_normed_two, after_self, gain[1])
    grad_after_self = grad_after_cross + from_two
    grad_self_low = grad_after_self.astype(BF)
    grad_w_self_out = weight_grad(self_mix, grad_self_low)
    grad_bias_two = jnp.sum(grad_after_self, axis=0)
    grad_self_mix = product_back(grad_self_low, full_self_out).astype(BF)
    grad_w_middle = join(grad_w_cross_out, grad_w_cross_q, grad_w_self_out, grad_w_cross_kv)
    grad_w_middle, grad_self_mix = tied(grad_w_middle, grad_self_mix)
    part_middle = scattered(grad_w_middle)
    (grad_pre,) = attend_back(
        self_sources, self_mix, grad_self_mix, self_log, places, tokens, tokens, width
    )
    if swift:
        grad_pre, part_inner = tied(grad_pre, part_inner)
        inner_sum, inner_in = grid.hop_one(part_inner)
    grad_normed_one = product_back(grad_pre, full_qkv)
    grad_w_qkv = weight_grad(normed_one, grad_pre)
    pre_sums = jnp.sum(grad_pre.astype(F32), axis=0)
    from_one, gain_one, shift_one = norm_back(grad_normed_one, residual_in, gain[0])
    grad_rows = (grad_after_self + from_one).astype(BF)

    sums = jnp.stack(
        [
            gain_one,
            gain_two,
            gain_three,
            shift_one,
            shift_two,
            shift_three,
            pre_sums[:width],
            pre_sums[2 * width :],
            grad_bias_two,
            grad_bias_three,
            grad_bias_four,
            grad_bias_five,
            grad_bias_six,
        ]
    )
    inner_sums = grad_inner_bias.reshape(grid.fsdp, -1, shard)
    packed = jnp.concatenate(
        [sums.reshape(-1, grid.fsdp, shard).swapaxes(0, 1), inner_sums], axis=1
    )
    if swift:
        packed = jnp.pad(packed.astype(BF), ((0, 0), (0, shard_rows - kinds), (0, 0)))
        packed = packed.reshape(-1, shard)
        last_kept, last_core = grid.fold_core(grad_w_qkv, packed)
        last_kept, activated, grad_rows = tied(last_kept, activated, grad_rows)
    hidden_rows = (after_cross + product(activated, full_outer) + bias[6]).astype(BF)
    leaving = jnp.concatenate(
        [
            grad_rows.reshape(grid.seq, rows, width),
            hidden_rows.reshape(grid.seq, rows, width),
        ],
        axis=1,
    ).reshape(-1, width)
    if swift:
        last_core, leaving = tied(last_core, leaving)
        last_own, last_near = grid.fold_chips(last_kept, last_core)
        inner_sum, inner_in = grid.hop_two(inner_sum, inner_in)
    leaving = grid.hand_back(leaving)
    if swift:
        inner_in, outer_in, grad_encoded, leaving, *last_near = tied(
            inner_in, outer_in, grad_encoded, leaving, *last_near
        )
        part_last = plus_all(last_own, last_near)
        last_sum, last_in = grid.hop_one(part_last)
        outer_sum, outer_in = grid.hop_three(outer_sum, outer_in)
        inner_sum, inner_in = grid.hop_three(inner_sum, inner_in)
        last_in, part_middle = tied(last_in, part_middle)
        middle_sum, middle_in = grid.hop_one(part_middle)
        last_sum, last_in = grid.hop_two(last_sum, last_in)
        last_in, middle_in = tied(last_in, middle_in)
        middle_sum, middle_in = grid.hop_two(middle_sum, middle_in)
        last_sum, last_in = grid.hop_three(last_sum, last_in)
        outer_in, inner_in, middle_in = tied(outer_in, inner_in, middle_in)
        middle_sum, middle_in = grid.hop_three(middle_sum, middle_in)
        total_outer = grid.hop_end(outer_sum, outer_in)
        total_inner = grid.hop_end(inner_sum, inner_in)
        total_last = grid.hop_end(last_sum, last_in)
        total_middle = grid.hop_end(middle_sum, middle_in)
        total_qkv = total_last[:, : grad_w_qkv.shape[1]]
        mine = total_last[:kinds, grad_w_qkv.shape[1] :]
    else:
        total_outer = grid.seq_sum(part_outer)
        total_inner = grid.seq_sum(part_inner)
        total_middle = grid.seq_sum(part_middle)
        total_qkv = grid.seq_sum(scattered(grad_w_qkv))
        mine = pick(lax.psum(packed, AXES), grid.group, 0)
    total_cross_out, total_cross_q, total_self_out, total_cross_kv = jnp.split(
        total_middle, (width, 2 * width, 3 * width), axis=1
    )

    grad_encoded = grad_encoded[:, :frames]
    grad_hidden_in, hidden_out = leaving[:, :rows], leaving[:, rows:]
    return (
        hidden_out,
        grad_hidden_in,
        grad_encoded,
        mine[:norms],
        mine[norms : 2 * norms],
        mine[2 * norms : 2 * norms + bias_count],
        total_qkv,
        total_self_out,
        total_cross_q,
        total_cross_kv,
        total_cross_out,
        total_inner,
        mine[2 * norms + bias_count :].reshape(-1),
        total_outer,
    )


def solution(mesh):
    rows = P("fsdp", "seq", None)
    wide = P(None, "fsdp")
    tall = P("fsdp", None)
    in_specs = (rows,) * 3 + (wide,) * 3 + (tall,) * 6 + (P("fsdp"), tall)
    out_specs = (rows,) * 3 + (wide,) * 3 + (tall,) * 6 + (P("fsdp"), tall)
    return jax.shard_map(
        functools.partial(local, dict(mesh.shape)),
        mesh=mesh,
        in_specs=in_specs,
        out_specs=out_specs,
        check_vma=False,
    )
```

```python
import functools

import jax
import jax.numpy as jnp
import numpy as np
from jax import lax
from jax.experimental import pallas as pl
from jax.experimental.pallas import tpu as pltpu
from jax.sharding import PartitionSpec as P

HD = 64
LANES = 128
NORM_EPSILON = 1e-05
LOW = -1e30
F32 = jnp.float32
BF = jnp.bfloat16
AXES = ("fsdp", "seq")


def two_heads(rows):
    lane = lax.broadcasted_iota(jnp.int32, rows.shape, 1)
    zero = jnp.zeros_like(rows)
    return jnp.concatenate(
        [jnp.where(lane < HD, rows, zero), jnp.where(lane >= HD, rows, zero)], axis=0
    )


def one_row(stacked):
    count = stacked.shape[0] // 2
    lane = lax.broadcasted_iota(jnp.int32, (count, stacked.shape[1]), 1)
    return jnp.where(lane < HD, stacked[:count], stacked[count:])


def over_rows(first, second):
    return lax.dot_general(first, second, (((0,), (0,)), ((), ())), preferred_element_type=F32)


def over_lanes(first, second):
    return lax.dot_general(first, second, (((1,), (1,)), ((), ())), preferred_element_type=F32)


def chunk_scores(keys, queries, places, step):
    scores = over_lanes(keys, queries)
    if places is not None:
        key_ref, query_ref = places
        rows = slice(step * keys.shape[0], (step + 1) * keys.shape[0])
        scores = jnp.where(key_ref[rows] <= query_ref[...], scores, LOW)
    return scores


def tail_kept(values, valid, other):
    size = values.shape[0]
    if valid == size:
        return values
    first = valid // 8 * 8
    row = lax.broadcasted_iota(jnp.int32, (size - first, values.shape[1]), 0)
    tail = jnp.where(row < valid - first, values[first:], other)
    return jnp.concatenate([values[:first], tail], axis=0)


def forward_kernel(chunk, valid, causal, *refs):
    q_ref, k_ref, v_ref = refs[:3]
    places = refs[3:5] if causal else None
    o_ref, log_ref, s_ref = refs[-3:]
    queries = two_heads(q_ref[...])
    width = queries.shape[0]
    strips = [slice(low, low + chunk) for low in range(0, k_ref.shape[0], chunk)]
    top = jnp.full((1, width), LOW, F32)
    for step, rows in enumerate(strips):
        scores = tail_kept(chunk_scores(k_ref[rows], queries, places, step), valid, LOW)
        s_ref[rows] = scores
        top = jnp.maximum(top, jnp.max(scores, axis=0, keepdims=True))
    total, mixed = jnp.zeros((1, width), F32), jnp.zeros((LANES, width), F32)
    for rows in strips:
        raised = jnp.exp(s_ref[rows] - top)
        total = total + jnp.sum(raised, axis=0, keepdims=True)
        mixed = mixed + over_rows(v_ref[rows], raised.astype(BF))
    o_ref[...] = one_row(jnp.transpose(mixed / total)).astype(BF)
    log_ref[...] = (top + jnp.log(total))[None]


def pair_back(chunk, valid, places, refs, store_key, store_value):
    q_ref, k_ref, v_ref, o_ref, g_ref, log_ref = refs
    queries = two_heads(q_ref[...])
    grads = two_heads(g_ref[...])
    mixed = o_ref[...].astype(F32)
    product = grads.astype(F32) * jnp.concatenate([mixed, mixed], axis=0)
    row_dot = jnp.sum(jnp.transpose(product), axis=0, keepdims=True)
    log_total = log_ref[0]
    grad_queries = jnp.zeros((LANES, queries.shape[0]), F32)
    for step, low in enumerate(range(0, k_ref.shape[0], chunk)):
        rows = slice(low, low + chunk)
        keys = k_ref[rows]
        scores = chunk_scores(keys, queries, places, step)
        weights = jnp.exp(tail_kept(scores, valid, LOW) - log_total)
        grad_weights = over_lanes(v_ref[rows], grads)
        grad_scores = (weights * (grad_weights - row_dot)).astype(BF)
        store_value(rows, jnp.dot(weights.astype(BF), grads, preferred_element_type=F32))
        store_key(rows, jnp.dot(grad_scores, queries, preferred_element_type=F32))
        grad_queries = grad_queries + over_rows(keys, grad_scores)
    return one_row(jnp.transpose(grad_queries)).astype(BF) * BF(HD**-0.5)


def joint_stores(joint_ref, width, first):
    def lanes(part):
        start = (part + first) * width + pl.program_id(0) * LANES
        return pl.ds(pl.multiple_of(start, LANES), LANES)

    def store_key(rows, part):
        joint_ref[rows, lanes(0)] = part.astype(BF)

    def store_value(rows, part):
        joint_ref[rows, lanes(1)] = part.astype(BF)

    return lanes, store_key, store_value


def cross_back_kernel(chunk, valid, width, *refs):
    gq_ref, joint_ref = refs[-2:]
    _, store_key, store_value = joint_stores(joint_ref, width, 0)
    gq_ref[...] = pair_back(chunk, valid, None, refs[:6], store_key, store_value)


def causal_back_kernel(chunk, width, *refs):
    joint_ref = refs[-1]
    lanes, store_key, store_value = joint_stores(joint_ref, width, 1)
    joint_ref[:, lanes(-1)] = pair_back(
        chunk, chunk, refs[6:8], refs[:6], store_key, store_value
    )


def columns(rows, first=0):
    return pl.BlockSpec((rows, LANES), lambda pair, *phase: (0, pair + first))


def place_specs(keys, tokens):
    return [
        pl.BlockSpec((keys, 1), lambda pair, *phase: (0, 0)),
        pl.BlockSpec((1, 2 * tokens), lambda pair, *phase: (0, 0)),
    ]


def log_spec(tokens, first=0):
    return pl.BlockSpec((1, 1, 2 * tokens), lambda pair, *phase: (pair + first, 0, 0))


def attend(sources, places, chunk, valid, width):
    tokens, count = sources[0][0].shape[0], sources[1][0].shape[0]
    causal = places is not None
    pairs = width // LANES
    specs = [columns(member.shape[0], first) for member, first in sources]
    operands = [member for member, _ in sources]
    if causal:
        specs += place_specs(count, tokens)
        operands += list(places)
    return pl.pallas_call(
        functools.partial(forward_kernel, chunk, valid, causal),
        grid=(pairs,),
        in_specs=specs,
        out_specs=[columns(tokens), log_spec(tokens)],
        out_shape=[
            jax.ShapeDtypeStruct((tokens, width), BF),
            jax.ShapeDtypeStruct((pairs, 1, 2 * tokens), F32),
        ],
        scratch_shapes=[pltpu.VMEM((count, 2 * tokens), F32)],
        compiler_params=pltpu.CompilerParams(vmem_limit_bytes=32 << 20),
        cost_estimate=pl.CostEstimate(
            flops=16 * tokens * count * width,
            transcendentals=tokens * count * width // HD,
            bytes_accessed=4 * (tokens + count) * width,
        ),
        name="attend_causal" if causal else "attend_cross",
    )(*operands)


def attend_back(sources, mixed, grads, logs, places, chunk, valid, width):
    tokens, count = sources[0][0].shape[0], sources[1][0].shape[0]
    causal = places is not None
    pairs = width // LANES
    specs = [columns(member.shape[0], first) for member, first in sources]
    specs += [columns(tokens), columns(tokens), log_spec(tokens)]
    operands = [member for member, _ in sources] + [mixed, grads, logs]
    parts = 3 if causal else 2
    out_specs = [pl.BlockSpec((count, parts * width), lambda pair: (0, 0))]
    out_shape = [jax.ShapeDtypeStruct((count, parts * width), BF)]
    if causal:
        specs += place_specs(count, tokens)
        operands += list(places)
        kernel = functools.partial(causal_back_kernel, chunk, width)
    else:
        kernel = functools.partial(cross_back_kernel, chunk, valid, width)
        out_specs = [columns(tokens)] + out_specs
        out_shape = [jax.ShapeDtypeStruct((tokens, width), BF)] + out_shape
    return pl.pallas_call(
        kernel,
        grid=(pairs,),
        in_specs=specs,
        out_specs=out_specs,
        out_shape=out_shape,
        compiler_params=pltpu.CompilerParams(vmem_limit_bytes=40 << 20),
        cost_estimate=pl.CostEstimate(
            flops=40 * tokens * count * width,
            transcendentals=tokens * count * width // HD,
            bytes_accessed=8 * (tokens + count) * width,
        ),
        name="attend_causal_back" if causal else "attend_cross_back",
    )(*operands)


def product(first, second):
    return jnp.dot(first, second, preferred_element_type=F32)


def product_back(incoming, weight):
    return lax.dot_general(
        incoming, weight, (((1,), (1,)), ((), ())), preferred_element_type=F32
    )


def weight_grad(operand, incoming):
    return lax.dot_general(
        operand, incoming, (((0,), (0,)), ((), ())), preferred_element_type=F32
    ).astype(BF)


def normalized(values):
    average = jnp.mean(values, axis=-1, keepdims=True)
    centred = values - average
    variance = jnp.mean(centred * centred, axis=-1, keepdims=True)
    inverse = lax.rsqrt(variance + NORM_EPSILON)
    return centred * inverse, inverse


def norm_back(incoming, values, gain_row):
    rows, inverse = normalized(values)
    scaled = incoming * gain_row
    average = jnp.mean(scaled, axis=-1, keepdims=True)
    aligned = jnp.mean(scaled * rows, axis=-1, keepdims=True)
    gain_grad = jnp.sum(incoming * rows, axis=0)
    shift_grad = jnp.sum(incoming, axis=0)
    return (scaled - average - rows * aligned) * inverse, gain_grad, shift_grad


def gelu(values):
    return values * (1.0 + lax.erf(values * (0.5**0.5))) * 0.5


def gelu_slope(values):
    return (1.0 + lax.erf(values * (0.5**0.5))) * 0.5 + values * jnp.exp(
        -0.5 * values * values
    ) * (0.5 / jnp.pi) ** 0.5


class Grid:
    def __init__(self, fsdp, seq, clips):
        self.fsdp, self.seq, self.clips = fsdp, seq, clips
        self.here = lax.axis_index("seq")
        self.group = lax.axis_index("fsdp")
        self.first = self.first_of(self.group)

    def first_of(self, group):
        return (group % 2) * (self.seq - self.clips)

    def works(self, group, place):
        return 0 <= place - self.first_of(group) < self.clips

    def turn(self, values, step, to_workers):
        pairs = []
        for group in range(self.fsdp):
            for place in range(self.seq):
                target = (place + step) % self.seq
                worker = target if to_workers else place
                if self.works(group, worker):
                    pairs.append((group * self.seq + place, group * self.seq + target))
        return lax.ppermute(values, AXES, pairs)

    def clip_at(self, place):
        return jnp.clip(place - self.first, 0, self.clips - 1)

    def collect(self, values, steps):
        pieces = {}
        for step in steps:
            target = (self.here + step) % self.seq
            sent = lax.dynamic_index_in_dim(values, self.clip_at(target), 0, keepdims=False)
            if step == 0:
                active = (self.here >= self.first) & (self.here < self.first + self.clips)
                pieces[step] = jnp.where(active, sent, jnp.zeros_like(sent))
            else:
                pieces[step] = self.turn(sent, step, True)
        return pieces

    def hand_back(self, rows):
        parts = rows.reshape(self.seq, -1, rows.shape[1])
        moved = lax.all_to_all(parts, "seq", split_axis=0, concat_axis=0, tiled=True)
        return lax.dynamic_slice_in_dim(moved, self.first, self.clips, 0)

    def chain(self, values, links):
        pairs = [
            (group * self.seq + a, group * self.seq + b)
            for group in range(self.fsdp)
            for a, b in links
        ]
        return lax.ppermute(values, AXES, pairs)

    def flip(self, values, bits):
        return lax.ppermute(values, "fsdp", [(f, f ^ bits) for f in range(self.fsdp)])

    def spread_far(self, shard, by_x, by_y):
        half = shard.shape[0] // 2
        return self.flip(by_y[:half], 2), self.flip(by_x[half:], 4)

    def spread_core(self, shard, by_x, by_y, far_x, far_y):
        mine = jnp.stack([shard, by_x, by_y, jnp.concatenate([far_x, far_y], axis=0)])
        return mine, self.flip(mine, 1)

    def fold_core(self, *members):
        core = self.group % 2
        parts = [m.reshape(4, 2, m.shape[0] // 8, m.shape[1]) for m in members]
        sent = jnp.concatenate([pick(p, 1 - core, 1) for p in parts], axis=2)
        kept = jnp.concatenate([pick(p, core, 1) for p in parts], axis=2)
        return kept, self.flip(sent, 1)

    def fold_chips(self, kept, arrived):
        sums = plus(kept, arrived)
        chip = self.group // 2
        moved = [self.flip(pick(sums, chip ^ bits, 0), 2 * bits) for bits in (1, 2, 3)]
        return pick(sums, chip, 0), moved

    def hop_one(self, values):
        return values, self.chain(values, ((0, 1), (3, 2)))

    def hop_two(self, values, arrived):
        half = plus(values, arrived)
        return half, self.chain(half, ((1, 2), (2, 1)))

    def hop_three(self, half, arrived):
        whole = plus(half, arrived)
        return whole, self.chain(whole, ((1, 0), (2, 3)))

    def hop_end(self, whole, back):
        return jnp.where((self.here == 0) | (self.here == 3), back, whole).astype(F32)

    def seq_sum(self, values):
        if self.seq != 4:
            return lax.psum(values, "seq").astype(F32)
        return self.hop_end(*self.hop_three(*self.hop_two(*self.hop_one(values))))


def pick(values, index, axis):
    return lax.dynamic_index_in_dim(values, index, axis, keepdims=False)


def plus(first, second):
    return (first.astype(F32) + second.astype(F32)).astype(first.dtype)


def plus_all(first, others):
    total = first.astype(F32)
    for other in others:
        total = total + other.astype(F32)
    return total.astype(first.dtype)


def tied(*members):
    return lax.optimization_barrier(members)


def join_kernel(*refs):
    start = 0
    for member in refs[:-1]:
        refs[-1][:, start : start + member.shape[1]] = member[...]
        start += member.shape[1]


def join(*members):
    rows, step = members[0].shape[0], 128
    widths = [member.shape[1] for member in members]

    def strip(width):
        return pl.BlockSpec((step, width), lambda i: (i, 0))

    return pl.pallas_call(
        join_kernel,
        grid=(rows // step,),
        in_specs=[strip(width) for width in widths],
        out_specs=strip(sum(widths)),
        out_shape=jax.ShapeDtypeStruct((rows, sum(widths)), BF),
        compiler_params=pltpu.CompilerParams(vmem_limit_bytes=16 << 20),
        cost_estimate=pl.CostEstimate(
            flops=0, transcendentals=0, bytes_accessed=4 * rows * sum(widths)
        ),
        name="join",
    )(*members)


def place_kernel(parts, here_ref, *refs):
    count = len(refs) - len(parts)
    pieces, outs = refs[:count], refs[count:]

    def store(piece):
        for out, (low, high, padded) in zip(outs, parts):
            out[: high - low] = piece[low:high]
            if padded > high - low:
                out[high - low :] = jnp.zeros((padded - high + low, out.shape[1]), out.dtype)

    for step, piece in enumerate(pieces):
        pl.when(pl.program_id(0) == step)(functools.partial(store, piece))


def place(here, pieces, parts):
    count = len(pieces)
    rows, width = pieces[0].shape
    return pl.pallas_call(
        functools.partial(place_kernel, parts),
        grid_spec=pltpu.PrefetchScalarGridSpec(
            num_scalar_prefetch=1,
            grid=(count,),
            in_specs=[pl.BlockSpec((rows, width), lambda step, here: (0, 0))] * count,
            out_specs=[
                pl.BlockSpec((padded, width), lambda step, here: ((here[0] - step) % count, 0))
                for _, _, padded in parts
            ],
        ),
        out_shape=[
            jax.ShapeDtypeStruct((count * padded, width), BF) for _, _, padded in parts
        ],
        compiler_params=pltpu.CompilerParams(vmem_limit_bytes=24 << 20),
        cost_estimate=pl.CostEstimate(
            flops=0, transcendentals=0, bytes_accessed=4 * count * rows * width
        ),
        name="place",
    )(here.reshape(1), *pieces)


def assemble_kernel(widths, rows, group_ref, mine_ref, other_ref, *outs):
    flipped = group_ref[0] % 2

    def store(first_ref, second_ref):
        start = 0
        for out, width in zip(outs, widths):
            out[:rows] = first_ref[0, :, start : start + width]
            out[rows:] = second_ref[0, :, start : start + width]
            start += width

    pl.when(flipped == 0)(lambda: store(mine_ref, other_ref))
    pl.when(flipped == 1)(lambda: store(other_ref, mine_ref))


def assemble(group, mine, other, widths):
    rows, total = mine.shape[1], mine.shape[2]
    source = pl.BlockSpec((1, rows, total), lambda chip, group: (chip, 0, 0))
    return pl.pallas_call(
        functools.partial(assemble_kernel, widths, rows),
        grid_spec=pltpu.PrefetchScalarGridSpec(
            num_scalar_prefetch=1,
            grid=(4,),
            in_specs=[source, source],
            out_specs=[
                pl.BlockSpec((2 * rows, width), lambda chip, group: ((group[0] // 2) ^ chip, 0))
                for width in widths
            ],
        ),
        out_shape=[jax.ShapeDtypeStruct((8 * rows, width), BF) for width in widths],
        compiler_params=pltpu.CompilerParams(vmem_limit_bytes=16 << 20),
        cost_estimate=pl.CostEstimate(
            flops=0, transcendentals=0, bytes_accessed=32 * rows * total
        ),
        name="assemble",
    )(group.reshape(1), mine, other)


def local(
    mesh_shape,
    hidden_in,
    encoded,
    out_grad,
    norm_gain,
    norm_shift,
    biases,
    self_qkv,
    self_out,
    cross_q,
    cross_kv,
    cross_out,
    mlp_in,
    mlp_in_bias,
    mlp_out,
):
    clips, rows, width = hidden_in.shape
    frames = encoded.shape[1]
    padded = (frames + 15) // 16 * 16
    grid = Grid(mesh_shape["fsdp"], mesh_shape["seq"], clips)
    shard = norm_gain.shape[1]
    norms = norm_gain.shape[0]
    bias_count = biases.shape[0]
    scaling = HD ** (-0.5)
    swift = grid.fsdp == 8 and grid.seq == 4 and self_qkv.shape[0] >= 32

    def gathered(*members):
        widths = [member.shape[1] for member in members]
        joined = jnp.concatenate(members, axis=1)
        joined = lax.all_gather(joined, "fsdp", axis=0, tiled=True)
        return jnp.split(joined, np.cumsum(widths)[:-1].tolist(), axis=1)

    def scattered(member):
        return lax.psum_scatter(member, "fsdp", scatter_dimension=0, tiled=True)

    tokens_in = jnp.concatenate([hidden_in, encoded], axis=1)
    pieces = grid.collect(tokens_in, (0, 1, 3) if swift else range(grid.seq))
    small = jnp.concatenate([norm_gain, norm_shift, biases, mlp_in_bias.reshape(-1, shard)], axis=0)
    kinds = small.shape[0]
    shard_rows = self_qkv.shape[0]
    if swift:
        small = jnp.pad(small, ((0, shard_rows - kinds), (0, 0)))
        first_shard = jnp.concatenate([self_qkv, small], axis=1)
        first_widths = (self_qkv.shape[1], shard)
        first_x, first_y = grid.flip(first_shard, 2), grid.flip(first_shard, 4)
    full_self_out, full_cross_q, full_cross_kv = gathered(self_out, cross_q, cross_kv)
    full_cross_out, full_inner = gathered(cross_out, mlp_in)
    if swift:
        first_x, first_y, pieces[1], pieces[3], tokens_in = tied(
            first_x, first_y, pieces[1], pieces[3], tokens_in
        )
        pieces.update(grid.collect(tokens_in, (2,)))
        far_x, far_y = grid.spread_far(first_shard, first_x, first_y)
        far_x, far_y, pieces[2] = tied(far_x, far_y, pieces[2])
        mine, other = grid.spread_core(first_shard, first_x, first_y, far_x, far_y)
        other, mlp_out = tied(other, mlp_out)
        outer_x, outer_y = grid.flip(mlp_out, 2), grid.flip(mlp_out, 4)
        full_qkv, small = assemble(grid.group, mine, other, first_widths)
        small = small.reshape(grid.fsdp, shard_rows, shard)[:, :kinds]
    else:
        (full_qkv,) = gathered(self_qkv)
        small = lax.all_gather(small, "fsdp", axis=0)
        (full_outer,) = gathered(mlp_out)
    vectors = small[:, : 2 * norms + bias_count].swapaxes(0, 1).reshape(-1, width).astype(F32)
    gain, shift, bias = vectors[:norms], vectors[norms : 2 * norms], vectors[2 * norms :]
    inner_bias = small[:, 2 * norms + bias_count :].reshape(1, -1).astype(F32)
    none = jnp.zeros((width,), F32)

    token_rows, frame_rows = place(
        grid.here,
        [pieces[step] for step in range(grid.seq)],
        ((0, rows, rows), (rows, rows + frames, padded)),
    )
    residual_in = token_rows.astype(F32)
    normed_one = (normalized(residual_in)[0] * gain[0] + shift[0]).astype(BF)
    tokens = grid.seq * rows
    line = jnp.arange(tokens)
    places = (line[:, None], jnp.concatenate([line, line])[None, :])
    blocks = width // LANES

    qkv_bias = jnp.concatenate([bias[0], none, bias[1]])
    qkv_scale = jnp.concatenate([none + scaling, none + 1.0, none + 1.0])
    qkv = ((product(normed_one, full_qkv) + qkv_bias) * qkv_scale).astype(BF)
    self_sources = ((qkv, 0), (qkv, blocks), (qkv, 2 * blocks))
    self_mix, self_log = attend(self_sources, places, tokens, tokens, width)
    after_self = residual_in + product(self_mix, full_self_out) + bias[2]
    normed_two = (normalized(after_self)[0] * gain[1] + shift[1]).astype(BF)
    cross_queries = ((product(normed_two, full_cross_q) + bias[3]) * scaling).astype(BF)
    out_grad, cross_queries = tied(out_grad, cross_queries)
    top_pieces = list(grid.collect(out_grad, range(grid.seq)).values())
    kv_bias = jnp.concatenate([none, bias[4]])
    cross_pair = (product(frame_rows, full_cross_kv) + kv_bias).astype(BF)
    cross_sources = ((cross_queries, 0), (cross_pair, 0), (cross_pair, blocks))
    cross_mix, cross_log = attend(cross_sources, None, padded, frames, width)
    if swift:
        cross_mix, outer_x, outer_y, *top_pieces = tied(cross_mix, outer_x, outer_y, *top_pieces)
        far_x, far_y = grid.spread_far(mlp_out, outer_x, outer_y)
    (top,) = place(grid.here, top_pieces, ((0, rows, rows),))
    after_cross = after_self + product(cross_mix, full_cross_out) + bias[5]
    normed_three = (normalized(after_cross)[0] * gain[2] + shift[2]).astype(BF)
    inner = product(normed_three, full_inner) + inner_bias
    activated = gelu(inner).astype(BF)
    if swift:
        activated, far_x, far_y = tied(activated, far_x, far_y)
        mine, other = grid.spread_core(mlp_out, outer_x, outer_y, far_x, far_y)

    top_wide = top.astype(F32)
    grad_w_outer = weight_grad(activated, top)
    if swift:
        grad_w_outer, top, other = tied(grad_w_outer, top, other)
        (full_outer,) = assemble(grid.group, mine, other, (mlp_out.shape[1],))
    part_outer = scattered(grad_w_outer)
    grad_bias_six = jnp.sum(top_wide, axis=0)
    grad_inner = product_back(top, full_outer) * gelu_slope(inner)
    grad_inner_low = grad_inner.astype(BF)
    grad_w_inner = weight_grad(normed_three, grad_inner_low)
    grad_w_inner, grad_inner_low = tied(grad_w_inner, grad_inner_low)
    part_inner = scattered(grad_w_inner)
    grad_inner_bias = jnp.sum(grad_inner, axis=0)
    grad_normed_three = product_back(grad_inner_low, full_inner)
    from_three, gain_three, shift_three = norm_back(grad_normed_three, after_cross, gain[2])
    grad_after_cross = top_wide + from_three
    grad_cross_low = grad_after_cross.astype(BF)
    grad_bias_five = jnp.sum(grad_after_cross, axis=0)
    grad_w_cross_out = weight_grad(cross_mix, grad_cross_low)
    grad_cross_mix = product_back(grad_cross_low, full_cross_out).astype(BF)

    grad_cross_queries, grad_pair = attend_back(
        cross_sources, cross_mix, grad_cross_mix, cross_log, None, padded, frames, width
    )
    if swift:
        part_outer, grad_cross_queries, grad_pair = tied(
            part_outer, grad_cross_queries, grad_pair
        )
        outer_sum, outer_in = grid.hop_one(part_outer)
    grad_frames = product_back(grad_pair, full_cross_kv).astype(BF)
    grad_frames, grad_pair = tied(grad_frames, grad_pair)
    grad_encoded = grid.hand_back(grad_frames)
    grad_w_cross_kv = weight_grad(frame_rows, grad_pair)
    if swift:
        grad_w_cross_kv, grad_cross_queries, outer_in = tied(
            grad_w_cross_kv, grad_cross_queries, outer_in
        )
        outer_sum, outer_in = grid.hop_two(outer_sum, outer_in)
    grad_bias_four = jnp.sum(grad_pair[:, width:].astype(F32), axis=0)
    grad_w_cross_q = weight_grad(normed_two, grad_cross_queries)
    grad_bias_three = jnp.sum(grad_cross_queries.astype(F32), axis=0)
    grad_normed_two = product_back(grad_cross_queries, full_cross_q)
    from_two, gain_two, shift_two = norm_back(grad_normed_two, after_self, gain[1])
    grad_after_self = grad_after_cross + from_two
    grad_self_low = grad_after_self.astype(BF)
    grad_w_self_out = weight_grad(self_mix, grad_self_low)
    grad_bias_two = jnp.sum(grad_after_self, axis=0)
    grad_self_mix = product_back(grad_self_low, full_self_out).astype(BF)
    grad_w_middle = join(grad_w_cross_out, grad_w_cross_q, grad_w_self_out, grad_w_cross_kv)
    grad_w_middle, grad_self_mix = tied(grad_w_middle, grad_self_mix)
    part_middle = scattered(grad_w_middle)
    (grad_pre,) = attend_back(
        self_sources, self_mix, grad_self_mix, self_log, places, tokens, tokens, width
    )
    if swift:
        grad_pre, part_inner = tied(grad_pre, part_inner)
        inner_sum, inner_in = grid.hop_one(part_inner)
    grad_normed_one = product_back(grad_pre, full_qkv)
    grad_w_qkv = weight_grad(normed_one, grad_pre)
    pre_sums = jnp.sum(grad_pre.astype(F32), axis=0)
    from_one, gain_one, shift_one = norm_back(grad_normed_one, residual_in, gain[0])
    grad_rows = (grad_after_self + from_one).astype(BF)

    sums = jnp.stack(
        [
            gain_one,
            gain_two,
            gain_three,
            shift_one,
            shift_two,
            shift_three,
            pre_sums[:width],
            pre_sums[2 * width :],
            grad_bias_two,
            grad_bias_three,
            grad_bias_four,
            grad_bias_five,
            grad_bias_six,
        ]
    )
    inner_sums = grad_inner_bias.reshape(grid.fsdp, -1, shard)
    packed = jnp.concatenate(
        [sums.reshape(-1, grid.fsdp, shard).swapaxes(0, 1), inner_sums], axis=1
    )
    if swift:
        packed = jnp.pad(packed.astype(BF), ((0, 0), (0, shard_rows - kinds), (0, 0)))
        packed = packed.reshape(-1, shard)
        last_kept, last_core = grid.fold_core(grad_w_qkv, packed)
        last_kept, activated, grad_rows = tied(last_kept, activated, grad_rows)
    hidden_rows = (after_cross + product(activated, full_outer) + bias[6]).astype(BF)
    leaving = jnp.concatenate(
        [
            grad_rows.reshape(grid.seq, rows, width),
            hidden_rows.reshape(grid.seq, rows, width),
        ],
        axis=1,
    ).reshape(-1, width)
    if swift:
        last_core, leaving = tied(last_core, leaving)
        last_own, last_near = grid.fold_chips(last_kept, last_core)
    leaving = grid.hand_back(leaving)
    if swift:
        inner_in, outer_in, grad_encoded, leaving, *last_near = tied(
            inner_in, outer_in, grad_encoded, leaving, *last_near
        )
        part_last = plus_all(last_own, last_near)
        last_sum, last_in = grid.hop_one(part_last)
        outer_sum, outer_in = grid.hop_three(outer_sum, outer_in)
        inner_sum, inner_in = grid.hop_two(inner_sum, inner_in)
        last_in, inner_in, part_middle = tied(last_in, inner_in, part_middle)
        middle_sum, middle_in = grid.hop_one(part_middle)
        last_sum, last_in = grid.hop_two(last_sum, last_in)
        inner_sum, inner_in = grid.hop_three(inner_sum, inner_in)
        last_in, middle_in = tied(last_in, middle_in)
        middle_sum, middle_in = grid.hop_two(middle_sum, middle_in)
        last_sum, last_in = grid.hop_three(last_sum, last_in)
        outer_in, inner_in, middle_in = tied(outer_in, inner_in, middle_in)
        middle_sum, middle_in = grid.hop_three(middle_sum, middle_in)
        total_outer = grid.hop_end(outer_sum, outer_in)
        total_inner = grid.hop_end(inner_sum, inner_in)
        total_last = grid.hop_end(last_sum, last_in)
        total_middle = grid.hop_end(middle_sum, middle_in)
        total_qkv = total_last[:, : grad_w_qkv.shape[1]]
        mine = total_last[:kinds, grad_w_qkv.shape[1] :]
    else:
        total_outer = grid.seq_sum(part_outer)
        total_inner = grid.seq_sum(part_inner)
        total_middle = grid.seq_sum(part_middle)
        total_qkv = grid.seq_sum(scattered(grad_w_qkv))
        mine = pick(lax.psum(packed, AXES), grid.group, 0)
    total_cross_out, total_cross_q, total_self_out, total_cross_kv = jnp.split(
        total_middle, (width, 2 * width, 3 * width), axis=1
    )

    grad_encoded = grad_encoded[:, :frames]
    grad_hidden_in, hidden_out = leaving[:, :rows], leaving[:, rows:]
    return (
        hidden_out,
        grad_hidden_in,
        grad_encoded,
        mine[:norms],
        mine[norms : 2 * norms],
        mine[2 * norms : 2 * norms + bias_count],
        total_qkv,
        total_self_out,
        total_cross_q,
        total_cross_kv,
        total_cross_out,
        total_inner,
        mine[2 * norms + bias_count :].reshape(-1),
        total_outer,
    )


def solution(mesh):
    rows = P("fsdp", "seq", None)
    wide = P(None, "fsdp")
    tall = P("fsdp", None)
    in_specs = (rows,) * 3 + (wide,) * 3 + (tall,) * 6 + (P("fsdp"), tall)
    out_specs = (rows,) * 3 + (wide,) * 3 + (tall,) * 6 + (P("fsdp"), tall)
    return jax.shard_map(
        functools.partial(local, dict(mesh.shape)),
        mesh=mesh,
        in_specs=in_specs,
        out_specs=out_specs,
        check_vma=False,
    )
```

```python
import functools

import jax
import jax.numpy as jnp
import numpy as np
from jax import lax
from jax.experimental import pallas as pl
from jax.experimental.pallas import tpu as pltpu
from jax.sharding import PartitionSpec as P

HD = 64
LANES = 128
NORM_EPSILON = 1e-05
LOW = -1e30
F32 = jnp.float32
BF = jnp.bfloat16
AXES = ("fsdp", "seq")


def two_heads(rows):
    lane = lax.broadcasted_iota(jnp.int32, rows.shape, 1)
    zero = jnp.zeros_like(rows)
    return jnp.concatenate(
        [jnp.where(lane < HD, rows, zero), jnp.where(lane >= HD, rows, zero)], axis=0
    )


def one_row(stacked):
    count = stacked.shape[0] // 2
    lane = lax.broadcasted_iota(jnp.int32, (count, stacked.shape[1]), 1)
    return jnp.where(lane < HD, stacked[:count], stacked[count:])


def over_rows(first, second):
    return lax.dot_general(first, second, (((0,), (0,)), ((), ())), preferred_element_type=F32)


def over_lanes(first, second):
    return lax.dot_general(first, second, (((1,), (1,)), ((), ())), preferred_element_type=F32)


def chunk_scores(keys, queries, places, step):
    scores = over_lanes(keys, queries)
    if places is not None:
        key_ref, query_ref = places
        rows = slice(step * keys.shape[0], (step + 1) * keys.shape[0])
        scores = jnp.where(key_ref[rows] <= query_ref[...], scores, LOW)
    return scores


def tail_kept(values, valid, other):
    size = values.shape[0]
    if valid == size:
        return values
    first = valid // 8 * 8
    row = lax.broadcasted_iota(jnp.int32, (size - first, values.shape[1]), 0)
    tail = jnp.where(row < valid - first, values[first:], other)
    return jnp.concatenate([values[:first], tail], axis=0)


def forward_kernel(chunk, valid, causal, *refs):
    q_ref, k_ref, v_ref = refs[:3]
    places = refs[3:5] if causal else None
    o_ref, log_ref, s_ref = refs[-3:]
    queries = two_heads(q_ref[...])
    width = queries.shape[0]
    strips = [slice(low, low + chunk) for low in range(0, k_ref.shape[0], chunk)]
    top = jnp.full((1, width), LOW, F32)
    for step, rows in enumerate(strips):
        scores = tail_kept(chunk_scores(k_ref[rows], queries, places, step), valid, LOW)
        s_ref[rows] = scores
        top = jnp.maximum(top, jnp.max(scores, axis=0, keepdims=True))
    total, mixed = jnp.zeros((1, width), F32), jnp.zeros((LANES, width), F32)
    for rows in strips:
        raised = jnp.exp(s_ref[rows] - top)
        total = total + jnp.sum(raised, axis=0, keepdims=True)
        mixed = mixed + over_rows(v_ref[rows], raised.astype(BF))
    o_ref[...] = one_row(jnp.transpose(mixed / total)).astype(BF)
    log_ref[...] = (top + jnp.log(total))[None]


def pair_back(chunk, valid, places, refs, store_key, store_value):
    q_ref, k_ref, v_ref, o_ref, g_ref, log_ref = refs
    queries = two_heads(q_ref[...])
    grads = two_heads(g_ref[...])
    mixed = o_ref[...].astype(F32)
    product = grads.astype(F32) * jnp.concatenate([mixed, mixed], axis=0)
    row_dot = jnp.sum(jnp.transpose(product), axis=0, keepdims=True)
    log_total = log_ref[0]
    grad_queries = jnp.zeros((LANES, queries.shape[0]), F32)
    for step, low in enumerate(range(0, k_ref.shape[0], chunk)):
        rows = slice(low, low + chunk)
        keys = k_ref[rows]
        scores = chunk_scores(keys, queries, places, step)
        weights = jnp.exp(tail_kept(scores, valid, LOW) - log_total)
        grad_weights = over_lanes(v_ref[rows], grads)
        grad_scores = (weights * (grad_weights - row_dot)).astype(BF)
        store_value(rows, jnp.dot(weights.astype(BF), grads, preferred_element_type=F32))
        store_key(rows, jnp.dot(grad_scores, queries, preferred_element_type=F32))
        grad_queries = grad_queries + over_rows(keys, grad_scores)
    return one_row(jnp.transpose(grad_queries)).astype(BF) * BF(HD**-0.5)


def joint_stores(joint_ref, width, first):
    def lanes(part):
        start = (part + first) * width + pl.program_id(0) * LANES
        return pl.ds(pl.multiple_of(start, LANES), LANES)

    def store_key(rows, part):
        joint_ref[rows, lanes(0)] = part.astype(BF)

    def store_value(rows, part):
        joint_ref[rows, lanes(1)] = part.astype(BF)

    return lanes, store_key, store_value


def cross_back_kernel(chunk, valid, width, *refs):
    gq_ref, joint_ref = refs[-2:]
    _, store_key, store_value = joint_stores(joint_ref, width, 0)
    gq_ref[...] = pair_back(chunk, valid, None, refs[:6], store_key, store_value)


def causal_back_kernel(chunk, width, *refs):
    joint_ref = refs[-1]
    lanes, store_key, store_value = joint_stores(joint_ref, width, 1)
    joint_ref[:, lanes(-1)] = pair_back(
        chunk, chunk, refs[6:8], refs[:6], store_key, store_value
    )


def columns(rows, first=0):
    return pl.BlockSpec((rows, LANES), lambda pair, *phase: (0, pair + first))


def place_specs(keys, tokens):
    return [
        pl.BlockSpec((keys, 1), lambda pair, *phase: (0, 0)),
        pl.BlockSpec((1, 2 * tokens), lambda pair, *phase: (0, 0)),
    ]


def log_spec(tokens, first=0):
    return pl.BlockSpec((1, 1, 2 * tokens), lambda pair, *phase: (pair + first, 0, 0))


def attend(sources, places, chunk, valid, width):
    tokens, count = sources[0][0].shape[0], sources[1][0].shape[0]
    causal = places is not None
    pairs = width // LANES
    specs = [columns(member.shape[0], first) for member, first in sources]
    operands = [member for member, _ in sources]
    if causal:
        specs += place_specs(count, tokens)
        operands += list(places)
    return pl.pallas_call(
        functools.partial(forward_kernel, chunk, valid, causal),
        grid=(pairs,),
        in_specs=specs,
        out_specs=[columns(tokens), log_spec(tokens)],
        out_shape=[
            jax.ShapeDtypeStruct((tokens, width), BF),
            jax.ShapeDtypeStruct((pairs, 1, 2 * tokens), F32),
        ],
        scratch_shapes=[pltpu.VMEM((count, 2 * tokens), F32)],
        compiler_params=pltpu.CompilerParams(vmem_limit_bytes=32 << 20),
        cost_estimate=pl.CostEstimate(
            flops=16 * tokens * count * width,
            transcendentals=tokens * count * width // HD,
            bytes_accessed=4 * (tokens + count) * width,
        ),
        name="attend_causal" if causal else "attend_cross",
    )(*operands)


def attend_back(sources, mixed, grads, logs, places, chunk, valid, width):
    tokens, count = sources[0][0].shape[0], sources[1][0].shape[0]
    causal = places is not None
    pairs = width // LANES
    specs = [columns(member.shape[0], first) for member, first in sources]
    specs += [columns(tokens), columns(tokens), log_spec(tokens)]
    operands = [member for member, _ in sources] + [mixed, grads, logs]
    parts = 3 if causal else 2
    out_specs = [pl.BlockSpec((count, parts * width), lambda pair: (0, 0))]
    out_shape = [jax.ShapeDtypeStruct((count, parts * width), BF)]
    if causal:
        specs += place_specs(count, tokens)
        operands += list(places)
        kernel = functools.partial(causal_back_kernel, chunk, width)
    else:
        kernel = functools.partial(cross_back_kernel, chunk, valid, width)
        out_specs = [columns(tokens)] + out_specs
        out_shape = [jax.ShapeDtypeStruct((tokens, width), BF)] + out_shape
    return pl.pallas_call(
        kernel,
        grid=(pairs,),
        in_specs=specs,
        out_specs=out_specs,
        out_shape=out_shape,
        compiler_params=pltpu.CompilerParams(vmem_limit_bytes=40 << 20),
        cost_estimate=pl.CostEstimate(
            flops=40 * tokens * count * width,
            transcendentals=tokens * count * width // HD,
            bytes_accessed=8 * (tokens + count) * width,
        ),
        name="attend_causal_back" if causal else "attend_cross_back",
    )(*operands)


def product(first, second):
    return jnp.dot(first, second, preferred_element_type=F32)


def product_back(incoming, weight):
    return lax.dot_general(
        incoming, weight, (((1,), (1,)), ((), ())), preferred_element_type=F32
    )


def weight_grad(operand, incoming):
    return lax.dot_general(
        operand, incoming, (((0,), (0,)), ((), ())), preferred_element_type=F32
    ).astype(BF)


def normalized(values):
    average = jnp.mean(values, axis=-1, keepdims=True)
    centred = values - average
    variance = jnp.mean(centred * centred, axis=-1, keepdims=True)
    inverse = lax.rsqrt(variance + NORM_EPSILON)
    return centred * inverse, inverse


def norm_back(incoming, values, gain_row):
    rows, inverse = normalized(values)
    scaled = incoming * gain_row
    average = jnp.mean(scaled, axis=-1, keepdims=True)
    aligned = jnp.mean(scaled * rows, axis=-1, keepdims=True)
    gain_grad = jnp.sum(incoming * rows, axis=0)
    shift_grad = jnp.sum(incoming, axis=0)
    return (scaled - average - rows * aligned) * inverse, gain_grad, shift_grad


def gelu(values):
    return values * (1.0 + lax.erf(values * (0.5**0.5))) * 0.5


def gelu_slope(values):
    return (1.0 + lax.erf(values * (0.5**0.5))) * 0.5 + values * jnp.exp(
        -0.5 * values * values
    ) * (0.5 / jnp.pi) ** 0.5


class Grid:
    def __init__(self, fsdp, seq, clips):
        self.fsdp, self.seq, self.clips = fsdp, seq, clips
        self.here = lax.axis_index("seq")
        self.group = lax.axis_index("fsdp")
        self.first = self.first_of(self.group)

    def first_of(self, group):
        return (group % 2) * (self.seq - self.clips)

    def works(self, group, place):
        return 0 <= place - self.first_of(group) < self.clips

    def turn(self, values, step, to_workers):
        pairs = []
        for group in range(self.fsdp):
            for place in range(self.seq):
                target = (place + step) % self.seq
                worker = target if to_workers else place
                if self.works(group, worker):
                    pairs.append((group * self.seq + place, group * self.seq + target))
        return lax.ppermute(values, AXES, pairs)

    def clip_at(self, place):
        return jnp.clip(place - self.first, 0, self.clips - 1)

    def collect(self, values, steps):
        pieces = {}
        for step in steps:
            target = (self.here + step) % self.seq
            sent = lax.dynamic_index_in_dim(values, self.clip_at(target), 0, keepdims=False)
            if step == 0:
                active = (self.here >= self.first) & (self.here < self.first + self.clips)
                pieces[step] = jnp.where(active, sent, jnp.zeros_like(sent))
            else:
                pieces[step] = self.turn(sent, step, True)
        return pieces

    def hand_back(self, rows):
        parts = rows.reshape(self.seq, -1, rows.shape[1])
        moved = lax.all_to_all(parts, "seq", split_axis=0, concat_axis=0, tiled=True)
        return lax.dynamic_slice_in_dim(moved, self.first, self.clips, 0)

    def chain(self, values, links):
        pairs = [
            (group * self.seq + a, group * self.seq + b)
            for group in range(self.fsdp)
            for a, b in links
        ]
        return lax.ppermute(values, AXES, pairs)

    def flip(self, values, bits):
        return lax.ppermute(values, "fsdp", [(f, f ^ bits) for f in range(self.fsdp)])

    def spread_far(self, shard, by_x, by_y):
        half = shard.shape[0] // 2
        return self.flip(by_y[:half], 2), self.flip(by_x[half:], 4)

    def spread_core(self, shard, by_x, by_y, far_x, far_y):
        mine = jnp.stack([shard, by_x, by_y, jnp.concatenate([far_x, far_y], axis=0)])
        return mine, self.flip(mine, 1)

    def fold_core(self, *members):
        core = self.group % 2
        parts = [m.reshape(4, 2, m.shape[0] // 8, m.shape[1]) for m in members]
        sent = jnp.concatenate([pick(p, 1 - core, 1) for p in parts], axis=2)
        kept = jnp.concatenate([pick(p, core, 1) for p in parts], axis=2)
        return kept, self.flip(sent, 1)

    def fold_chips(self, kept, arrived):
        sums = plus(kept, arrived)
        chip = self.group // 2
        moved = [self.flip(pick(sums, chip ^ bits, 0), 2 * bits) for bits in (1, 2, 3)]
        return pick(sums, chip, 0), moved

    def hop_one(self, values):
        return values, self.chain(values, ((0, 1), (3, 2)))

    def hop_two(self, values, arrived):
        half = plus(values, arrived)
        return half, self.chain(half, ((1, 2), (2, 1)))

    def hop_three(self, half, arrived):
        whole = plus(half, arrived)
        return whole, self.chain(whole, ((1, 0), (2, 3)))

    def hop_end(self, whole, back):
        return jnp.where((self.here == 0) | (self.here == 3), back, whole).astype(F32)

    def seq_sum(self, values):
        if self.seq != 4:
            return lax.psum(values, "seq").astype(F32)
        return self.hop_end(*self.hop_three(*self.hop_two(*self.hop_one(values))))


def pick(values, index, axis):
    return lax.dynamic_index_in_dim(values, index, axis, keepdims=False)


def plus(first, second):
    return (first.astype(F32) + second.astype(F32)).astype(first.dtype)


def plus_all(first, others):
    total = first.astype(F32)
    for other in others:
        total = total + other.astype(F32)
    return total.astype(first.dtype)


def tied(*members):
    return lax.optimization_barrier(members)


def join_kernel(*refs):
    start = 0
    for member in refs[:-1]:
        refs[-1][:, start : start + member.shape[1]] = member[...]
        start += member.shape[1]


def join(*members):
    rows, step = members[0].shape[0], 128
    widths = [member.shape[1] for member in members]

    def strip(width):
        return pl.BlockSpec((step, width), lambda i: (i, 0))

    return pl.pallas_call(
        join_kernel,
        grid=(rows // step,),
        in_specs=[strip(width) for width in widths],
        out_specs=strip(sum(widths)),
        out_shape=jax.ShapeDtypeStruct((rows, sum(widths)), BF),
        compiler_params=pltpu.CompilerParams(vmem_limit_bytes=16 << 20),
        cost_estimate=pl.CostEstimate(
            flops=0, transcendentals=0, bytes_accessed=4 * rows * sum(widths)
        ),
        name="join",
    )(*members)


def place_kernel(parts, here_ref, *refs):
    count = len(refs) - len(parts)
    pieces, outs = refs[:count], refs[count:]

    def store(piece):
        for out, (low, high, padded) in zip(outs, parts):
            out[: high - low] = piece[low:high]
            if padded > high - low:
                out[high - low :] = jnp.zeros((padded - high + low, out.shape[1]), out.dtype)

    for step, piece in enumerate(pieces):
        pl.when(pl.program_id(0) == step)(functools.partial(store, piece))


def place(here, pieces, parts):
    count = len(pieces)
    rows, width = pieces[0].shape
    return pl.pallas_call(
        functools.partial(place_kernel, parts),
        grid_spec=pltpu.PrefetchScalarGridSpec(
            num_scalar_prefetch=1,
            grid=(count,),
            in_specs=[pl.BlockSpec((rows, width), lambda step, here: (0, 0))] * count,
            out_specs=[
                pl.BlockSpec((padded, width), lambda step, here: ((here[0] - step) % count, 0))
                for _, _, padded in parts
            ],
        ),
        out_shape=[
            jax.ShapeDtypeStruct((count * padded, width), BF) for _, _, padded in parts
        ],
        compiler_params=pltpu.CompilerParams(vmem_limit_bytes=24 << 20),
        cost_estimate=pl.CostEstimate(
            flops=0, transcendentals=0, bytes_accessed=4 * count * rows * width
        ),
        name="place",
    )(here.reshape(1), *pieces)


def assemble_kernel(widths, rows, group_ref, mine_ref, other_ref, *outs):
    flipped = group_ref[0] % 2

    def store(first_ref, second_ref):
        start = 0
        for out, width in zip(outs, widths):
            out[:rows] = first_ref[0, :, start : start + width]
            out[rows:] = second_ref[0, :, start : start + width]
            start += width

    pl.when(flipped == 0)(lambda: store(mine_ref, other_ref))
    pl.when(flipped == 1)(lambda: store(other_ref, mine_ref))


def assemble(group, mine, other, widths):
    rows, total = mine.shape[1], mine.shape[2]
    source = pl.BlockSpec((1, rows, total), lambda chip, group: (chip, 0, 0))
    return pl.pallas_call(
        functools.partial(assemble_kernel, widths, rows),
        grid_spec=pltpu.PrefetchScalarGridSpec(
            num_scalar_prefetch=1,
            grid=(4,),
            in_specs=[source, source],
            out_specs=[
                pl.BlockSpec((2 * rows, width), lambda chip, group: ((group[0] // 2) ^ chip, 0))
                for width in widths
            ],
        ),
        out_shape=[jax.ShapeDtypeStruct((8 * rows, width), BF) for width in widths],
        compiler_params=pltpu.CompilerParams(vmem_limit_bytes=16 << 20),
        cost_estimate=pl.CostEstimate(
            flops=0, transcendentals=0, bytes_accessed=32 * rows * total
        ),
        name="assemble",
    )(group.reshape(1), mine, other)


def local(
    mesh_shape,
    hidden_in,
    encoded,
    out_grad,
    norm_gain,
    norm_shift,
    biases,
    self_qkv,
    self_out,
    cross_q,
    cross_kv,
    cross_out,
    mlp_in,
    mlp_in_bias,
    mlp_out,
):
    clips, rows, width = hidden_in.shape
    frames = encoded.shape[1]
    padded = (frames + 15) // 16 * 16
    grid = Grid(mesh_shape["fsdp"], mesh_shape["seq"], clips)
    shard = norm_gain.shape[1]
    norms = norm_gain.shape[0]
    bias_count = biases.shape[0]
    scaling = HD ** (-0.5)
    swift = grid.fsdp == 8 and grid.seq == 4 and self_qkv.shape[0] >= 32

    def gathered(*members):
        widths = [member.shape[1] for member in members]
        joined = jnp.concatenate(members, axis=1)
        joined = lax.all_gather(joined, "fsdp", axis=0, tiled=True)
        return jnp.split(joined, np.cumsum(widths)[:-1].tolist(), axis=1)

    def scattered(member):
        return lax.psum_scatter(member, "fsdp", scatter_dimension=0, tiled=True)

    tokens_in = jnp.concatenate([hidden_in, encoded], axis=1)
    pieces = grid.collect(tokens_in, (0, 1, 3) if swift else range(grid.seq))
    small = jnp.concatenate([norm_gain, norm_shift, biases, mlp_in_bias.reshape(-1, shard)], axis=0)
    kinds = small.shape[0]
    shard_rows = self_qkv.shape[0]
    if swift:
        small = jnp.pad(small, ((0, shard_rows - kinds), (0, 0)))
        first_shard = jnp.concatenate([self_qkv, small], axis=1)
        first_widths = (self_qkv.shape[1], shard)
        first_x, first_y = grid.flip(first_shard, 2), grid.flip(first_shard, 4)
    full_self_out, full_cross_q, full_cross_kv, full_cross_out = gathered(
        self_out, cross_q, cross_kv, cross_out
    )
    (full_inner,) = gathered(mlp_in)
    if swift:
        first_x, first_y, pieces[1], pieces[3], tokens_in = tied(
            first_x, first_y, pieces[1], pieces[3], tokens_in
        )
        pieces.update(grid.collect(tokens_in, (2,)))
        far_x, far_y = grid.spread_far(first_shard, first_x, first_y)
        far_x, far_y, pieces[2] = tied(far_x, far_y, pieces[2])
        mine, other = grid.spread_core(first_shard, first_x, first_y, far_x, far_y)
        other, mlp_out = tied(other, mlp_out)
        outer_x, outer_y = grid.flip(mlp_out, 2), grid.flip(mlp_out, 4)
        full_qkv, small = assemble(grid.group, mine, other, first_widths)
        small = small.reshape(grid.fsdp, shard_rows, shard)[:, :kinds]
    else:
        (full_qkv,) = gathered(self_qkv)
        small = lax.all_gather(small, "fsdp", axis=0)
        (full_outer,) = gathered(mlp_out)
    vectors = small[:, : 2 * norms + bias_count].swapaxes(0, 1).reshape(-1, width).astype(F32)
    gain, shift, bias = vectors[:norms], vectors[norms : 2 * norms], vectors[2 * norms :]
    inner_bias = small[:, 2 * norms + bias_count :].reshape(1, -1).astype(F32)
    none = jnp.zeros((width,), F32)

    token_rows, frame_rows = place(
        grid.here,
        [pieces[step] for step in range(grid.seq)],
        ((0, rows, rows), (rows, rows + frames, padded)),
    )
    residual_in = token_rows.astype(F32)
    normed_one = (normalized(residual_in)[0] * gain[0] + shift[0]).astype(BF)
    tokens = grid.seq * rows
    line = jnp.arange(tokens)
    places = (line[:, None], jnp.concatenate([line, line])[None, :])
    blocks = width // LANES

    qkv_bias = jnp.concatenate([bias[0], none, bias[1]])
    qkv_scale = jnp.concatenate([none + scaling, none + 1.0, none + 1.0])
    qkv = ((product(normed_one, full_qkv) + qkv_bias) * qkv_scale).astype(BF)
    self_sources = ((qkv, 0), (qkv, blocks), (qkv, 2 * blocks))
    self_mix, self_log = attend(self_sources, places, tokens, tokens, width)
    after_self = residual_in + product(self_mix, full_self_out) + bias[2]
    normed_two = (normalized(after_self)[0] * gain[1] + shift[1]).astype(BF)
    cross_queries = ((product(normed_two, full_cross_q) + bias[3]) * scaling).astype(BF)
    out_grad, cross_queries = tied(out_grad, cross_queries)
    top_pieces = list(grid.collect(out_grad, range(grid.seq)).values())
    kv_bias = jnp.concatenate([none, bias[4]])
    cross_pair = (product(frame_rows, full_cross_kv) + kv_bias).astype(BF)
    cross_sources = ((cross_queries, 0), (cross_pair, 0), (cross_pair, blocks))
    cross_mix, cross_log = attend(cross_sources, None, padded, frames, width)
    if swift:
        cross_mix, outer_x, outer_y, *top_pieces = tied(cross_mix, outer_x, outer_y, *top_pieces)
        far_x, far_y = grid.spread_far(mlp_out, outer_x, outer_y)
    (top,) = place(grid.here, top_pieces, ((0, rows, rows),))
    after_cross = after_self + product(cross_mix, full_cross_out) + bias[5]
    normed_three = (normalized(after_cross)[0] * gain[2] + shift[2]).astype(BF)
    inner = product(normed_three, full_inner) + inner_bias
    activated = gelu(inner).astype(BF)
    if swift:
        activated, far_x, far_y = tied(activated, far_x, far_y)
        mine, other = grid.spread_core(mlp_out, outer_x, outer_y, far_x, far_y)

    top_wide = top.astype(F32)
    grad_w_outer = weight_grad(activated, top)
    if swift:
        grad_w_outer, top, other = tied(grad_w_outer, top, other)
        (full_outer,) = assemble(grid.group, mine, other, (mlp_out.shape[1],))
    part_outer = scattered(grad_w_outer)
    grad_bias_six = jnp.sum(top_wide, axis=0)
    grad_inner = product_back(top, full_outer) * gelu_slope(inner)
    grad_inner_low = grad_inner.astype(BF)
    grad_w_inner = weight_grad(normed_three, grad_inner_low)
    grad_w_inner, grad_inner_low = tied(grad_w_inner, grad_inner_low)
    part_inner = scattered(grad_w_inner)
    grad_inner_bias = jnp.sum(grad_inner, axis=0)
    grad_normed_three = product_back(grad_inner_low, full_inner)
    from_three, gain_three, shift_three = norm_back(grad_normed_three, after_cross, gain[2])
    grad_after_cross = top_wide + from_three
    grad_cross_low = grad_after_cross.astype(BF)
    grad_bias_five = jnp.sum(grad_after_cross, axis=0)
    grad_w_cross_out = weight_grad(cross_mix, grad_cross_low)
    grad_cross_mix = product_back(grad_cross_low, full_cross_out).astype(BF)

    grad_cross_queries, grad_pair = attend_back(
        cross_sources, cross_mix, grad_cross_mix, cross_log, None, padded, frames, width
    )
    if swift:
        part_outer, grad_cross_queries, grad_pair = tied(
            part_outer, grad_cross_queries, grad_pair
        )
        outer_sum, outer_in = grid.hop_one(part_outer)
    grad_frames = product_back(grad_pair, full_cross_kv).astype(BF)
    grad_frames, grad_pair = tied(grad_frames, grad_pair)
    grad_encoded = grid.hand_back(grad_frames)
    grad_w_cross_kv = weight_grad(frame_rows, grad_pair)
    if swift:
        grad_w_cross_kv, grad_cross_queries, outer_in = tied(
            grad_w_cross_kv, grad_cross_queries, outer_in
        )
        outer_sum, outer_in = grid.hop_two(outer_sum, outer_in)
    grad_bias_four = jnp.sum(grad_pair[:, width:].astype(F32), axis=0)
    grad_w_cross_q = weight_grad(normed_two, grad_cross_queries)
    grad_bias_three = jnp.sum(grad_cross_queries.astype(F32), axis=0)
    grad_normed_two = product_back(grad_cross_queries, full_cross_q)
    from_two, gain_two, shift_two = norm_back(grad_normed_two, after_self, gain[1])
    grad_after_self = grad_after_cross + from_two
    grad_self_low = grad_after_self.astype(BF)
    grad_w_self_out = weight_grad(self_mix, grad_self_low)
    grad_bias_two = jnp.sum(grad_after_self, axis=0)
    grad_self_mix = product_back(grad_self_low, full_self_out).astype(BF)
    grad_w_middle = join(grad_w_cross_out, grad_w_cross_q, grad_w_self_out, grad_w_cross_kv)
    grad_w_middle, grad_self_mix = tied(grad_w_middle, grad_self_mix)
    part_middle = scattered(grad_w_middle)
    (grad_pre,) = attend_back(
        self_sources, self_mix, grad_self_mix, self_log, places, tokens, tokens, width
    )
    if swift:
        grad_pre, part_inner = tied(grad_pre, part_inner)
        inner_sum, inner_in = grid.hop_one(part_inner)
    grad_normed_one = product_back(grad_pre, full_qkv)
    grad_w_qkv = weight_grad(normed_one, grad_pre)
    pre_sums = jnp.sum(grad_pre.astype(F32), axis=0)
    from_one, gain_one, shift_one = norm_back(grad_normed_one, residual_in, gain[0])
    grad_rows = (grad_after_self + from_one).astype(BF)

    sums = jnp.stack(
        [
            gain_one,
            gain_two,
            gain_three,
            shift_one,
            shift_two,
            shift_three,
            pre_sums[:width],
            pre_sums[2 * width :],
            grad_bias_two,
            grad_bias_three,
            grad_bias_four,
            grad_bias_five,
            grad_bias_six,
        ]
    )
    inner_sums = grad_inner_bias.reshape(grid.fsdp, -1, shard)
    packed = jnp.concatenate(
        [sums.reshape(-1, grid.fsdp, shard).swapaxes(0, 1), inner_sums], axis=1
    )
    if swift:
        packed = jnp.pad(packed.astype(BF), ((0, 0), (0, shard_rows - kinds), (0, 0)))
        packed = packed.reshape(-1, shard)
        last_kept, last_core = grid.fold_core(grad_w_qkv, packed)
        last_kept, activated, grad_rows = tied(last_kept, activated, grad_rows)
    hidden_rows = (after_cross + product(activated, full_outer) + bias[6]).astype(BF)
    leaving = jnp.concatenate(
        [
            grad_rows.reshape(grid.seq, rows, width),
            hidden_rows.reshape(grid.seq, rows, width),
        ],
        axis=1,
    ).reshape(-1, width)
    if swift:
        last_core, leaving = tied(last_core, leaving)
        last_own, last_near = grid.fold_chips(last_kept, last_core)
    leaving = grid.hand_back(leaving)
    if swift:
        inner_in, outer_in, grad_encoded, leaving, *last_near = tied(
            inner_in, outer_in, grad_encoded, leaving, *last_near
        )
        part_last = plus_all(last_own, last_near)
        last_sum, last_in = grid.hop_one(part_last)
        outer_sum, outer_in = grid.hop_three(outer_sum, outer_in)
        inner_sum, inner_in = grid.hop_two(inner_sum, inner_in)
        last_in, inner_in, part_middle = tied(last_in, inner_in, part_middle)
        middle_sum, middle_in = grid.hop_one(part_middle)
        last_sum, last_in = grid.hop_two(last_sum, last_in)
        inner_sum, inner_in = grid.hop_three(inner_sum, inner_in)
        last_in, middle_in = tied(last_in, middle_in)
        middle_sum, middle_in = grid.hop_two(middle_sum, middle_in)
        last_sum, last_in = grid.hop_three(last_sum, last_in)
        outer_in, inner_in, middle_in = tied(outer_in, inner_in, middle_in)
        middle_sum, middle_in = grid.hop_three(middle_sum, middle_in)
        total_outer = grid.hop_end(outer_sum, outer_in)
        total_inner = grid.hop_end(inner_sum, inner_in)
        total_last = grid.hop_end(last_sum, last_in)
        total_middle = grid.hop_end(middle_sum, middle_in)
        total_qkv = total_last[:, : grad_w_qkv.shape[1]]
        mine = total_last[:kinds, grad_w_qkv.shape[1] :]
    else:
        total_outer = grid.seq_sum(part_outer)
        total_inner = grid.seq_sum(part_inner)
        total_middle = grid.seq_sum(part_middle)
        total_qkv = grid.seq_sum(scattered(grad_w_qkv))
        mine = pick(lax.psum(packed, AXES), grid.group, 0)
    total_cross_out, total_cross_q, total_self_out, total_cross_kv = jnp.split(
        total_middle, (width, 2 * width, 3 * width), axis=1
    )

    grad_encoded = grad_encoded[:, :frames]
    grad_hidden_in, hidden_out = leaving[:, :rows], leaving[:, rows:]
    return (
        hidden_out,
        grad_hidden_in,
        grad_encoded,
        mine[:norms],
        mine[norms : 2 * norms],
        mine[2 * norms : 2 * norms + bias_count],
        total_qkv,
        total_self_out,
        total_cross_q,
        total_cross_kv,
        total_cross_out,
        total_inner,
        mine[2 * norms + bias_count :].reshape(-1),
        total_outer,
    )


def solution(mesh):
    rows = P("fsdp", "seq", None)
    wide = P(None, "fsdp")
    tall = P("fsdp", None)
    in_specs = (rows,) * 3 + (wide,) * 3 + (tall,) * 6 + (P("fsdp"), tall)
    out_specs = (rows,) * 3 + (wide,) * 3 + (tall,) * 6 + (P("fsdp"), tall)
    return jax.shard_map(
        functools.partial(local, dict(mesh.shape)),
        mesh=mesh,
        in_specs=in_specs,
        out_specs=out_specs,
        check_vma=False,
    )
```
